32 devices in a mesh: groups: 2 (over y), scan: 4 (over z), angle: 2 (over x), tile: 2 (over core).
Axes of the slice: x: 2, y: 2, z: 4, core: 2. Of those that a mesh axis runs over, the one named last changes fastest.
Arguments:
- transmission: float32 [8, 2, 256, 256], P(('groups', 'angle', 'tile'), None, 'scan'), parts along dimension 0, may hold values from -4 to 4
- scaled_dual: float32 [8, 2, 256, 256], P(('groups', 'angle', 'tile'), None, 'scan'), parts along dimension 0, may hold values from -4 to 4
- projected: float32 [8, 2, 256, 256], P(('groups', 'angle', 'tile'), None, 'scan'), parts along dimension 0, may hold values from -4 to 4
- volume: float32 [4, 8, 256, 256], P('groups', ('angle', 'tile'), 'scan'), parts along dimension 0, may hold values from -0.4 to 0.4
- intensities: bfloat16 [8, 16, 128, 128], P(('groups', 'angle', 'tile'), 'scan'), parts along dimension 0, may hold values from 0 to 2
- probe_wave: float32 [4, 128, 128], P('groups'), parts along dimension 0, may hold values from -4 to 4
- slot_first_rows: int32 [8, 16], P(('groups', 'angle', 'tile'), 'scan'), parts along dimension 0, may hold values from 0 to 128
- slot_first_columns: int32 [8, 16], P(('groups', 'angle', 'tile'), 'scan'), parts along dimension 0, may hold values from 0 to 64
- patch_counts: int32 [8, 4], P(('groups', 'angle', 'tile'), 'scan'), parts along dimension 0, may hold values from 1 to 4, as said below
- shift_table: int32 [4, 8], P(None, ('angle', 'tile')), may hold values from -63 to 63, as said below
- tap_weight: float32 [4, 8], P(None, ('angle', 'tile')), may hold values from 0 to 1
Outputs:
- new_transmission: float32 [8, 2, 256, 256], P(('groups', 'angle', 'tile'), None, 'scan'), parts along dimension 0
- new_dual: float32 [8, 2, 256, 256], P(('groups', 'angle', 'tile'), None, 'scan'), parts along dimension 0
- new_volume: float32 [4, 8, 256, 256], P('groups', ('angle', 'tile'), 'scan'), parts along dimension 0
- new_projected: float32 [8, 2, 256, 256], P(('groups', 'angle', 'tile'), None, 'scan'), parts along dimension 0
The draws below stay inside these ranges and needn't reach their ends.
There are 2 independent parts, one for each index of `groups`. The reference program is written for one: setup_inputs(seed, part) draws one part's arguments, and reference() takes and returns one part's arrays. A program takes and returns all parts, laid end to end along the dimension named above; an argument that names none is the same for every part. Nothing has to cross between parts.
Inputs may be any that keep to these rules, and one draw needn't show every extreme that they name: Only the first patch_counts[a, r] slots of region r are live; for each angle some region has all 4 slots live. `shift_table`: for every angle the shift is s = (slope * (2 y - 7)) // 7 for an integer slope of that angle from 1 to 63; some angle has slope 64 - 1.
All inputs are finite; a program needn't handle non-finite values.
Results may differ from the reference program's by a relative error of at most 0.0003.
Values sent between devices are 32-bit elements; how exact they have to be, the bound alone decides.
No kernel may reach another device: no remote copies, remote signals or barrier semaphores. Data moves between devices by JAX's collectives and lax.ppermute only.
A program may use at most 64 MiB of HBM per device.

```python
import jax
import jax.numpy as jnp
from jax import lax

PATCH_LENGTH = 128
REGION_COLUMNS = 64
AXIAL_ROWS = 256
CAP = 4
NDET = 256
ANGLE_COUNT = 4
NY = 8
SLOT_COUNT = 16
N_SCAN = 4


def draw_patch_counts(key, part):
    baseline = jax.random.randint(jax.random.fold_in(key, 11), (ANGLE_COUNT, N_SCAN), 1, CAP + 1)
    full_region = jax.random.randint(jax.random.fold_in(key, 12), (ANGLE_COUNT,), 0, N_SCAN)
    region_ids = jnp.arange(N_SCAN, dtype=jnp.int32)
    return jnp.where(region_ids[None, :] == full_region[:, None], CAP, baseline).astype(jnp.int32)


def draw_shift_table(key, part):
    slopes = jax.random.randint(jax.random.fold_in(key, 21), (ANGLE_COUNT,), 1, REGION_COLUMNS)
    chosen = jax.random.randint(jax.random.fold_in(key, 22), (), 0, ANGLE_COUNT)
    slopes = jnp.where(jnp.arange(ANGLE_COUNT, dtype=jnp.int32) == chosen, REGION_COLUMNS - 1, slopes)
    row_ids = jnp.arange(NY, dtype=jnp.int32)
    return (slopes[:, None] * (2 * row_ids[None, :] + 1 - NY) // (NY - 1)).astype(jnp.int32)


def touch_ends(array, stream_key, least, high):
    longest = array.shape.index(max(array.shape))
    spots = []
    for shift in (0, 1):
        where = [jax.random.randint(jax.random.fold_in(stream_key, axis), (), 0, length) for axis, length in enumerate(array.shape)]
        where[longest] = (where[longest] + shift) % array.shape[longest]
        spots.append(tuple(where))
    return array.at[spots[0]].set(least).at[spots[1]].set(high)


def levels(stream_key, dims, shards, least, high):
    gain, own = 1.0, jax.random.fold_in(stream_key, 6)
    for dim, shards_of in shards:
        steps = jnp.exp(jax.random.uniform(jax.random.fold_in(own, dim), (shards_of,), jnp.float32, least / len(shards), high / len(shards)))
        gain = gain * jnp.repeat(steps, dims[dim] // shards_of).reshape([-1 if axis == dim else 1 for axis in range(len(dims))])
    return gain


def bell_draw(stream_key, extent, deviation, reach, pieces=(), kind=jnp.bfloat16):
    drawn = jax.random.normal(stream_key, extent, jnp.float32) * deviation
    if len(pieces) > 0:
        drawn = levels(stream_key, extent, pieces, -0.22, 0.18) * drawn
    return jnp.clip(drawn, min=-reach, max=reach).astype(kind)


def setup_inputs(seed: int = 0, part: int = 0) -> dict:
    keys = jax.random.split(jax.random.key(seed), 12)
    part_splits = jax.random.split(jax.random.fold_in(keys[11], part), 12)
    return {
        "transmission": bell_draw(part_splits[0], (ANGLE_COUNT, 2, NDET, AXIAL_ROWS), 0.5, 4.0, ((0, 4), (2, 4)), jnp.float32),
        "scaled_dual": bell_draw(part_splits[1], (ANGLE_COUNT, 2, NDET, AXIAL_ROWS), 0.25, 4.0, ((0, 4), (2, 4)), jnp.float32),
        "projected": bell_draw(part_splits[2], (ANGLE_COUNT, 2, NDET, AXIAL_ROWS), 0.5, 4.0, ((0, 4), (2, 4)), jnp.float32),
        "volume": bell_draw(part_splits[3], (2, NY, NDET, AXIAL_ROWS), 0.05, 0.4, ((1, 4), (2, 4)), jnp.float32),
        "intensities": jnp.clip(2.0 * jax.random.uniform(part_splits[4], (ANGLE_COUNT, SLOT_COUNT, PATCH_LENGTH, PATCH_LENGTH), jnp.float32) ** levels(part_splits[4], (ANGLE_COUNT, SLOT_COUNT, PATCH_LENGTH, PATCH_LENGTH), ((0, 4), (1, 4)), -0.2, 0.2), 0.0, 2.0).astype(jnp.bfloat16),
        "probe_wave": bell_draw(part_splits[5], (2, PATCH_LENGTH, PATCH_LENGTH), 0.7, 4.0, (), jnp.float32),
        "slot_first_rows": touch_ends(jax.random.randint(part_splits[6], (ANGLE_COUNT, SLOT_COUNT), 0, AXIAL_ROWS - PATCH_LENGTH + 1), jax.random.fold_in(part_splits[6], 1), 0, AXIAL_ROWS - PATCH_LENGTH).astype(jnp.int32),
        "slot_first_columns": touch_ends(jax.random.randint(part_splits[7], (ANGLE_COUNT, SLOT_COUNT), 0, REGION_COLUMNS + 1), jax.random.fold_in(part_splits[7], 1), 0, REGION_COLUMNS).astype(jnp.int32),
        "patch_counts": draw_patch_counts(jax.random.fold_in(jax.random.fold_in(keys[11], part), 71), part),
        "shift_table": draw_shift_table(jax.random.fold_in(keys[11], 71), part),
        "tap_weight": jnp.clip(1.0 * jax.random.uniform(keys[10], (ANGLE_COUNT, NY), jnp.float32) ** levels(keys[10], (ANGLE_COUNT, NY), ((1, 4),), -0.2, 0.2), 0.0, 1.0),
    }


penalty = 4.0
amplitude_step = 0.25
tv_weight = 1.0
smoothing = 0.05
step_size = 0.008

def tv_core(padded):
    baseline = padded[:, :-1, :-1, :-1]
    along_y = padded[:, 1:, :-1, :-1] - baseline
    along_x = padded[:, :-1, 1:, :-1] - baseline
    along_z = padded[:, :-1, :-1, 1:] - baseline
    inverse = 1.0 / jnp.sqrt(along_y * along_y + along_x * along_x + along_z * along_z + smoothing * smoothing)
    norm_y = along_y * inverse
    norm_x = along_x * inverse
    norm_z = along_z * inverse
    divergence = norm_y[:, 1:, 1:, 1:] - norm_y[:, :-1, 1:, 1:] + (norm_x[:, 1:, 1:, 1:] - norm_x[:, 1:, :-1, 1:]) + (norm_z[:, 1:, 1:, 1:] - norm_z[:, 1:, 1:, :-1])
    return -divergence

def patch_sums(angle_plane, rows_one, columns_one, intensity_one, counts_one, probe_wave):
    widened = jnp.pad(angle_plane, ((0, 0), (REGION_COLUMNS, REGION_COLUMNS), (0, 0)))
    slot_ids = jnp.arange(N_SCAN * CAP, dtype=jnp.int32)
    owners = slot_ids // CAP
    starts = (owners * REGION_COLUMNS + columns_one).astype(jnp.int32)
    row_starts = rows_one.astype(jnp.int32)
    active = (slot_ids % CAP < counts_one[owners]).astype(angle_plane.dtype)
    anchor = jnp.zeros((), jnp.int32)

    def window(col_start, row_start):
        return lax.dynamic_slice(widened, (anchor, col_start, row_start), (2, PATCH_LENGTH, PATCH_LENGTH))
    windows = jax.vmap(window)(starts, row_starts)
    exit_wave = lax.complex(probe_wave[0], probe_wave[1]) * lax.complex(windows[:, 0], windows[:, 1])
    far_field = jnp.fft.fft2(exit_wave, norm='ortho')
    magnitude = jnp.real(far_field) ** 2 + jnp.imag(far_field) ** 2
    corrected = far_field * (1.0 - amplitude_step * (magnitude - intensity_one.astype(angle_plane.dtype)))
    near_field = jnp.fft.ifft2(corrected, norm='ortho')
    update = lax.complex(probe_wave[0], -probe_wave[1]) * near_field
    density = probe_wave[0] * probe_wave[0] + probe_wave[1] * probe_wave[1]
    contrib = jnp.stack([jnp.real(update), jnp.imag(update), jnp.broadcast_to(density, jnp.real(update).shape)], axis=1)
    contrib = contrib * active[:, None, None, None]

    def add_patch(running, element):
        block_terms, col_start, row_start = element
        corner = (anchor, col_start, row_start)
        current = lax.dynamic_slice(running, corner, (3, PATCH_LENGTH, PATCH_LENGTH))
        return (lax.dynamic_update_slice(running, current + block_terms, corner), None)
    totals, _ = lax.scan(add_patch, jnp.zeros((3, NDET + 2 * REGION_COLUMNS, AXIAL_ROWS), angle_plane.dtype), (contrib, starts, row_starts))
    return totals[:, REGION_COLUMNS:REGION_COLUMNS + NDET]

def forward_project(volume, shift_table, tap_weight):
    widened = jnp.pad(volume, ((0, 0), (0, 0), (REGION_COLUMNS, REGION_COLUMNS), (0, 0)))
    rows_first = jnp.moveaxis(widened, 1, 0)
    anchor = jnp.zeros((), jnp.int32)

    def per_angle(element):
        offsets, fractions = element

        def add_row(running, entry):
            row_plane, offset, fraction = entry
            section = lax.dynamic_slice(row_plane, (anchor, (REGION_COLUMNS + offset).astype(jnp.int32), anchor), (2, NDET + 1, AXIAL_ROWS))
            return (running + (1.0 - fraction) * section[:, :-1] + fraction * section[:, 1:], None)
        result, _ = lax.scan(add_row, jnp.zeros((2, NDET, AXIAL_ROWS), volume.dtype), (rows_first, offsets, fractions))
        return result
    return lax.map(per_angle, (shift_table, tap_weight))

def back_project(residual, shift_table, tap_weight):
    widened = jnp.pad(residual, ((0, 0), (0, 0), (REGION_COLUMNS, REGION_COLUMNS), (0, 0)))
    anchor = jnp.zeros((), jnp.int32)

    def per_row(element):
        offsets, fractions = element

        def add_angle(running, entry):
            angle_plane, offset, fraction = entry
            section = lax.dynamic_slice(angle_plane, (anchor, (REGION_COLUMNS - offset - 1).astype(jnp.int32), anchor), (2, NDET + 1, AXIAL_ROWS))
            return (running + (1.0 - fraction) * section[:, 1:] + fraction * section[:, :-1], None)
        result, _ = lax.scan(add_angle, jnp.zeros((2, NDET, AXIAL_ROWS), residual.dtype), (widened, offsets, fractions))
        return result
    row_terms = lax.map(per_row, (shift_table.T, tap_weight.T))
    return jnp.moveaxis(row_terms, 0, 1)

def reference(transmission, scaled_dual, projected, volume, intensities, probe_wave, slot_first_rows, slot_first_columns, patch_counts, shift_table, tap_weight):

    def per_angle(element):
        plane_one, rows_one, columns_one, intensity_one, counts_one = element
        return patch_sums(plane_one, rows_one, columns_one, intensity_one, counts_one, probe_wave)
    totals = lax.map(per_angle, (transmission, slot_first_rows, slot_first_columns, intensities, patch_counts))
    new_transmission = (totals[:, 0:2] + penalty * (projected - scaled_dual)) / (totals[:, 2:3] + penalty)
    residual = projected - new_transmission - scaled_dual
    padded = jnp.pad(volume, ((0, 0), (1, 1), (1, 1), (1, 1)))
    descent = back_project(residual, shift_table, tap_weight) + tv_weight * tv_core(padded)
    new_volume = volume - step_size * descent
    new_projected = forward_project(new_volume, shift_table, tap_weight)
    new_dual = scaled_dual + new_transmission - new_projected
    return (new_transmission, new_dual, new_volume, new_projected)
```

```python
import math

import jax
import jax.numpy as jnp
import numpy as np
from jax import lax
from jax.experimental import pallas as pl
from jax.experimental.pallas import tpu as pltpu
from jax.sharding import PartitionSpec as P

penalty = 4.0
amplitude_step = 0.25
tv_weight = 1.0
smoothing = 0.05
step_size = 0.008

VMEM = pl.BlockSpec(memory_space=pltpu.VMEM)
SMEM = pl.BlockSpec(memory_space=pltpu.SMEM)
LANES = 128


def split(values):
    high = values.astype(jnp.bfloat16)
    return (high, (values - high.astype(jnp.float32)).astype(jnp.bfloat16))


def product(left, right):
    total = jnp.dot(left[0], right[0], preferred_element_type=jnp.float32)
    total += jnp.dot(left[0], right[1], preferred_element_type=jnp.float32)
    return total + jnp.dot(left[1], right[0], preferred_element_type=jnp.float32)


def dft_tables(length):
    grid_ids = np.arange(length)
    radians = (grid_ids[:, None] * grid_ids[None, :] % length) * (2.0 * math.pi / length)
    cosine = np.cos(radians) / math.sqrt(length)
    sine = np.sin(radians) / math.sqrt(length)
    forward = np.block([[cosine, sine], [-sine, cosine]])
    tables = []
    for table in (forward, forward.T):
        high = table.astype(jnp.bfloat16)
        tables += [high, (table - high.astype(np.float64)).astype(jnp.bfloat16)]
    return tables


def tile_is_first():
    return lax.axis_index("tile") == 0


def scan_is_even():
    return lax.rem(lax.axis_index("scan"), 2) == 0


def outer_rows(ya_ref, yb_ref, channel):
    last = ya_ref.shape[1] - 1
    first = tile_is_first()
    below = jnp.where(first, yb_ref[channel, last], ya_ref[channel, last])
    above = jnp.where(first, ya_ref[channel, 0], yb_ref[channel, 0])
    return (below, above)


def patch_kernel(
    rows_ref,
    columns_ref,
    count_ref,
    plane_ref,
    plane_a_ref,
    plane_b_ref,
    intensity_ref,
    probe_ref,
    forward_high_ref,
    forward_low_ref,
    inverse_high_ref,
    inverse_low_ref,
    volume_ref,
    ya_ref,
    yb_ref,
    own_ref,
    rim_a_ref,
    rim_b_ref,
    wide,
    totals,
):
    width = plane_ref.shape[2]
    side = probe_ref.shape[1]
    slots = intensity_ref.shape[1]
    even = scan_is_even()
    at_a = pl.multiple_of(jnp.where(even, 2 * width, 0), width)
    at_b = pl.multiple_of(jnp.where(even, 0, 2 * width), width)
    wide[:, width : 2 * width] = plane_ref[0]
    wide[:, pl.ds(at_a, width)] = plane_a_ref[0]
    wide[:, pl.ds(at_b, width)] = plane_b_ref[0]
    lanes = lax.broadcasted_iota(jnp.int32, (side, side), 1)
    sublanes = lax.broadcasted_iota(jnp.int32, (side, side), 0)
    forward = (forward_high_ref[...], forward_low_ref[...])
    inverse = (inverse_high_ref[...], inverse_low_ref[...])
    probes, waves, masks = [], [], []
    for slot in range(slots):
        column = columns_ref[0, slot]
        row = rows_ref[0, slot]
        turn = lax.rem(row, side)
        probe = [pltpu.roll(pltpu.roll(probe_ref[part], column, 0), turn, 1) for part in range(2)]
        near_lanes = lanes >= row
        near_columns = sublanes >= column
        window = []
        for part in range(2):
            near = jnp.where(near_lanes, wide[part, :side, :side], wide[part, :side, side:])
            wrapped = jnp.where(
                near_lanes[:width], wide[part, side:, :side], wide[part, side:, side:]
            )
            wrapped = jnp.concatenate([wrapped, near[width:]], axis=0)
            window.append(jnp.where(near_columns, near, wrapped))
        wave_real = probe[0] * window[0] - probe[1] * window[1]
        wave_imaginary = probe[0] * window[1] + probe[1] * window[0]
        probes.append(probe)
        waves.append(jnp.concatenate([wave_real, wave_imaginary], axis=1))
        live = jnp.full((side, side), slot < count_ref[0, 0])
        masks.append((near_lanes, near_columns, live))
    half = product(split(jnp.concatenate(waves, axis=0)), inverse)
    half = jnp.concatenate(
        [
            jnp.concatenate(
                [half[slot * side : (slot + 1) * side, part * side : (part + 1) * side] for slot in range(slots)],
                axis=1,
            )
            for part in range(2)
        ],
        axis=0,
    )
    far = product(forward, split(half))
    far_real, far_imaginary = far[:side], far[side:]
    intensity = jnp.concatenate(
        [intensity_ref[0, slot].astype(jnp.float32) for slot in range(slots)], axis=1
    )
    factor = 1.0 - amplitude_step * (
        far_real * far_real + far_imaginary * far_imaginary - intensity
    )
    corrected = jnp.concatenate([far_real * factor, far_imaginary * factor], axis=0)
    half = product(inverse, split(corrected))
    half = jnp.concatenate(
        [
            jnp.concatenate(
                [half[part * side : (part + 1) * side, slot * side : (slot + 1) * side] for part in range(2)],
                axis=1,
            )
            for slot in range(slots)
        ],
        axis=0,
    )
    near = product(split(half), forward)
    totals[...] = jnp.zeros_like(totals)
    for slot in range(slots):
        probe = probes[slot]
        near_real = near[slot * side : (slot + 1) * side, :side]
        near_imaginary = near[slot * side : (slot + 1) * side, side:]
        terms = (
            probe[0] * near_real + probe[1] * near_imaginary,
            probe[0] * near_imaginary - probe[1] * near_real,
            probe[0] * probe[0] + probe[1] * probe[1],
        )
        near_lanes, near_columns, live = masks[slot]
        inner = live & near_columns
        outer = (live & jnp.logical_not(near_columns))[:width]
        for part, term in enumerate(terms):
            for start, lane_mask in ((0, near_lanes), (side, jnp.logical_not(near_lanes))):
                at = slice(start, start + side)
                totals[part, :side, at] += jnp.where(inner & lane_mask, term, 0.0)
                totals[part, side:, at] += jnp.where(outer & lane_mask[:width], term[:width], 0.0)
    own_ref[...] = totals[:, width : 2 * width]
    below_above = [outer_rows(ya_ref, yb_ref, channel) for channel in range(2)]
    parts = totals.shape[0]
    count = volume_ref.shape[1]
    for rim_ref, at, low in ((rim_a_ref, at_a, jnp.logical_not(even)), (rim_b_ref, at_b, even)):
        for part in range(parts):
            rim_ref[part * width : (part + 1) * width] = totals[part, pl.ds(at, width)]
        edge_rows = []
        for channel in range(2):
            planes = [below_above[channel][0]]
            planes += [volume_ref[channel, row] for row in range(count)]
            planes.append(below_above[channel][1])
            for plane in planes:
                edge_rows.append(jnp.where(low, plane[:1], plane[width - 1 :]))
        rim_ref[parts * width :] = jnp.concatenate(edge_rows, axis=0)


def fold_kernel(own_ref, rim_a_ref, rim_b_ref, projected_ref, dual_ref, object_ref, residual_ref):
    width = own_ref.shape[1]
    sums = [
        own_ref[part]
        + rim_a_ref[part * width : (part + 1) * width]
        + rim_b_ref[part * width : (part + 1) * width]
        for part in range(3)
    ]
    for part in range(2):
        target = projected_ref[0, part]
        dual = dual_ref[0, part]
        updated = (sums[part] + penalty * (target - dual)) / (sums[2] + penalty)
        object_ref[0, part] = updated
        residual_ref[part] = target - updated - dual


def variation_kernel(volume_ref, ya_ref, yb_ref, rim_a_ref, rim_b_ref, base_ref, padded, norms):
    width = volume_ref.shape[2]
    length = volume_ref.shape[3]
    count = volume_ref.shape[1]
    margin = 8
    edges_at = rim_a_ref.shape[0] - 2 * (count + 2)
    even = scan_is_even()
    lanes = lax.broadcasted_iota(jnp.int32, (width, length), 1)
    first_lane = lanes == 0
    last_lane = lanes == length - 1
    for channel in range(2):
        below, above = outer_rows(ya_ref, yb_ref, channel)
        planes = [below] + [volume_ref[channel, row] for row in range(count)] + [above]
        for row, plane in enumerate(planes):
            at = edges_at + channel * (count + 2) + row
            edge_a = rim_a_ref[at : at + 1]
            edge_b = rim_b_ref[at : at + 1]
            padded[row, margin : margin + width] = plane
            padded[row, margin - 1 : margin] = jnp.where(even, edge_b, edge_a)
            padded[row, margin + width : margin + width + 1] = jnp.where(even, edge_a, edge_b)
        previous_y = None
        for row in range(count + 1):
            here = padded[row, margin : margin + width]
            along_y = padded[row + 1, margin : margin + width] - here
            along_x = padded[row, margin + 1 : margin + width + 1] - here
            along_z = jnp.where(last_lane, 0.0, pltpu.roll(here, length - 1, 1)) - here
            inverse = lax.rsqrt(
                along_y * along_y + along_x * along_x + along_z * along_z + smoothing * smoothing
            )
            norm_y = along_y * inverse
            if row > 0:
                norm_x = along_x * inverse
                norm_z = along_z * inverse
                corner = padded[row, margin - 1 : margin]
                corner_y = padded[row + 1, margin - 1 : margin] - corner
                corner_x = here[:1] - corner
                corner_z = (
                    jnp.where(last_lane[:1], 0.0, pltpu.roll(corner, length - 1, 1)) - corner
                )
                corner_norm = corner_x * lax.rsqrt(
                    corner_y * corner_y
                    + corner_x * corner_x
                    + corner_z * corner_z
                    + smoothing * smoothing
                )
                norms[margin : margin + width] = norm_x
                norms[margin - 1 : margin] = corner_norm
                behind_x = norms[margin - 1 : margin + width - 1]
                ahead = here * lax.rsqrt(here * here + smoothing * smoothing)
                behind_z = jnp.where(first_lane, ahead, pltpu.roll(norm_z, 1, 1))
                divergence = (
                    norm_y - previous_y + (norm_x - behind_x) + (norm_z - behind_z)
                )
                base_ref[channel, row - 1] = here + (step_size * tv_weight) * divergence
            previous_y = norm_y


def project_kernel(
    shift_ref,
    weight_ref,
    here_ref,
    side_ref,
    other_ref,
    base_ref,
    beside_ref,
    volume_ref,
    keep_ref,
    send_ref,
    wide,
    updated,
):
    width = base_ref.shape[2]
    count = base_ref.shape[1]
    angles = here_ref.shape[0]
    tiles = lax.axis_size("tile")
    columns = angles // tiles
    me, tile, scan = lax.axis_index("angle"), lax.axis_index("tile"), lax.axis_index("scan")
    upper = me >= columns // 2
    right = lax.rem(scan + tile, 2) == 0
    side_at = pl.multiple_of(jnp.where(right, 2 * width, 0), width)
    other_at = pl.multiple_of(jnp.where(right, 0, 2 * width), width)

    def angle_of(turn, flip):
        return lax.rem(me + turn, columns) * tiles + (tile if flip == 0 else 1 - tile)

    chunks = [slice(at, at + LANES) for at in range(0, base_ref.shape[3], LANES)]
    for turn in range(columns):
        for flip in range(tiles):
            block = turn * tiles + flip
            for chunk, at in enumerate(chunks):
                near, far = angle_of(turn, flip), angle_of(turn, 1 - flip)
                wide[near, :, chunk, width : 2 * width] = here_ref[block, :, :, at]
                wide[near, :, chunk, pl.ds(side_at, width)] = side_ref[block, :, :, at]
                wide[far, :, chunk, pl.ds(other_at, width)] = other_ref[block, :, :, at]
    exists = jnp.where(upper, scan < lax.axis_size("scan") - 1, scan > 0).astype(jnp.float32)
    own_at = pl.multiple_of(jnp.where(upper, 0, width), width)
    beside_at = pl.multiple_of(jnp.where(upper, width, 0), width)
    for row in range(count):
        for channel in range(2):
            for chunk, at in enumerate(chunks):
                total = jnp.zeros((2 * width, LANES), jnp.float32)
                for angle in range(angles):
                    start = jnp.where(upper, width, 0) - shift_ref[angle, row]
                    fraction = weight_ref[angle, row]
                    total += (1.0 - fraction) * wide[angle, channel, chunk, pl.ds(start, 2 * width)]
                    total += fraction * wide[angle, channel, chunk, pl.ds(start - 1, 2 * width)]
                updated[row, channel, chunk] = total
                part = updated.at[row, channel, chunk]
                own = base_ref[channel, row, :, at] - step_size * part[pl.ds(own_at, width)]
                beside = beside_ref[channel, row, :, at] - step_size * part[pl.ds(beside_at, width)]
                volume_ref[channel, row, :, at] = own
                part[pl.ds(own_at, width)] = own
                part[pl.ds(beside_at, width)] = beside * exists
    for turn in range(columns):
        for flip, out_ref in ((0, keep_ref), (1, send_ref)):
            angle = angle_of(turn, flip)
            for channel in range(2):
                for chunk, at in enumerate(chunks):
                    total = jnp.zeros((width, LANES), jnp.float32)
                    for row in range(count):
                        start = jnp.where(upper, 0, width) + shift_ref[angle, row]
                        fraction = weight_ref[angle, row]
                        total += (1.0 - fraction) * updated[row, channel, chunk, pl.ds(start, width)]
                        total += fraction * updated[row, channel, chunk, pl.ds(start + 1, width)]
                    out_ref[turn, channel, :, at] = total


def call(kernel, shapes, in_specs, scratch, flops, name):
    moved = 4 * sum(math.prod(shape) for shape in shapes)
    return pl.pallas_call(
        kernel,
        name=name,
        out_shape=[jax.ShapeDtypeStruct(shape, jnp.float32) for shape in shapes],
        in_specs=in_specs,
        out_specs=[VMEM] * len(shapes),
        scratch_shapes=[pltpu.VMEM(shape, jnp.float32) for shape in scratch],
        cost_estimate=pl.CostEstimate(flops=flops, bytes_accessed=2 * moved, transcendentals=0),
    )


def body(
    transmission,
    scaled_dual,
    projected,
    volume,
    intensities,
    probe_wave,
    slot_first_rows,
    slot_first_columns,
    patch_counts,
    shift_table,
    tap_weight,
):
    width, length = transmission.shape[2:]
    count = volume.shape[1]
    scans, columns, tiles = (lax.axis_size(axis) for axis in ("scan", "angle", "tile"))
    rounds = [[(i, i + 1) for i in range(first, scans - 1, 2)] for first in (0, 1)]
    both = [pairs + [(target, source) for source, target in pairs] for pairs in rounds]
    swap = [(0, 1), (1, 0)]

    def exchange(block, number):
        return lax.ppermute(block, "scan", both[number])

    def across(block):
        return lax.ppermute(block, "tile", swap)

    plane_a = exchange(transmission, 0)
    plane_b = exchange(transmission, 1)
    rows_a = across(volume)
    bridge = [(i * tiles + 1, (i + 1) * tiles) for i in range(columns - 1)]
    bridge += [(target, source) for source, target in bridge]
    rows_b = lax.ppermute(volume, ("angle", "tile"), bridge)
    tables = [jnp.asarray(table) for table in dft_tables(probe_wave.shape[1])]
    rim_rows = 3 * width + 2 * (count + 2)
    own, rim_a, rim_b = call(
        patch_kernel,
        [(3, width, length), (rim_rows, length), (rim_rows, length)],
        [SMEM] * 3 + [VMEM] * 12,
        [(2, 3 * width, length), (3, 3 * width, length)],
        10**9,
        "patches",
    )(
        slot_first_rows,
        slot_first_columns,
        patch_counts,
        transmission,
        plane_a,
        plane_b,
        intensities,
        probe_wave,
        *tables,
        volume,
        rows_a,
        rows_b,
    )
    rim_a = exchange(rim_a, 0)
    rim_b = exchange(rim_b, 1)
    new_transmission, residual = call(
        fold_kernel,
        [transmission.shape, transmission.shape[1:]],
        [VMEM] * 5,
        [],
        10**6,
        "fold",
    )(own, rim_a, rim_b, projected, scaled_dual)
    by_column = [residual]
    for turn in range(1, columns):
        route = [(i, (i - turn) % columns) for i in range(columns)]
        by_column.append(lax.ppermute(residual, "angle", route))
    (base,) = call(
        variation_kernel,
        [volume.shape],
        [VMEM] * 5,
        [(count + 2, width + 16, length), (width + 16, length)],
        10**7,
        "variation",
    )(volume, rows_a, rows_b, rim_a, rim_b)
    lower = range(columns // 2)
    route = []
    for scan in range(scans):
        for column in range(columns):
            target = scan + 1 if column in lower else scan - 1
            if 0 <= target < scans:
                route.append((scan * columns + column, target * columns + column))
    beside = lax.ppermute(base, ("scan", "angle"), route)
    here = jnp.stack([block for pair in ((b, across(b)) for b in by_column) for block in pair])
    route = [(s * tiles + t, d * tiles + t) for t in range(tiles) for s, d in both[t]]
    side = lax.ppermute(here, ("scan", "tile"), route)
    other = across(side)
    new_volume, keep, send = call(
        project_kernel,
        [volume.shape, (columns, 2, width, length), (columns, 2, width, length)],
        [SMEM] * 2 + [VMEM] * 5,
        [
            (columns * tiles, 2, length // LANES, 3 * width, LANES),
            (count, 2, length // LANES, 2 * width, LANES),
        ],
        10**8,
        "project",
    )(shift_table, tap_weight, here, side, other, base, beside)
    sums = keep + across(send)
    new_projected = sums[0]
    for turn in range(1, columns):
        route = [(i, (i + turn) % columns) for i in range(columns)]
        new_projected = new_projected + lax.ppermute(sums[turn], "angle", route)
    new_projected = new_projected[None]
    new_dual = scaled_dual + new_transmission - new_projected
    return (new_transmission, new_dual, new_volume, new_projected)


def solution(mesh):
    plane = P(("groups", "angle", "tile"), None, "scan", None)
    cells = P("groups", ("angle", "tile"), "scan", None)
    slots = P(("groups", "angle", "tile"), "scan")
    return jax.shard_map(
        body,
        mesh=mesh,
        in_specs=(
            plane,
            plane,
            plane,
            cells,
            P(("groups", "angle", "tile"), "scan", None, None),
            P("groups", None, None),
            slots,
            slots,
            slots,
            P(None, ("angle", "tile")),
            P(None, ("angle", "tile")),
        ),
        out_specs=(plane, plane, cells, plane),
        check_vma=False,
    )
```

```python
import math

import jax
import jax.numpy as jnp
import numpy as np
from jax import lax
from jax.experimental import pallas as pl
from jax.experimental.pallas import tpu as pltpu
from jax.sharding import PartitionSpec as P


penalty = 4.0
amplitude_step = 0.25
tv_weight = 1.0
smoothing = 0.05
step_size = 0.008

VMEM = pl.BlockSpec(memory_space=pltpu.VMEM)
SMEM = pl.BlockSpec(memory_space=pltpu.SMEM)
HBM = pl.BlockSpec(memory_space=pltpu.MemorySpace.HBM)
LANES = 128
SPARE_BYTES = 8 << 20


def split(values):
    high = values.astype(jnp.bfloat16)
    return (high, (values - high.astype(jnp.float32)).astype(jnp.bfloat16))


def product(left, right):
    total = jnp.dot(left[0], right[0], preferred_element_type=jnp.float32)
    total += jnp.dot(left[0], right[1], preferred_element_type=jnp.float32)
    return total + jnp.dot(left[1], right[0], preferred_element_type=jnp.float32)


def dft_tables(length):
    grid_ids = np.arange(length)
    radians = (grid_ids[:, None] * grid_ids[None, :] % length) * (2.0 * math.pi / length)
    cosine = np.cos(radians) / math.sqrt(length)
    sine = np.sin(radians) / math.sqrt(length)
    forward = np.block([[cosine, sine], [-sine, cosine]])
    tables = []
    for table in (forward, forward.T):
        high = table.astype(jnp.bfloat16)
        tables += [high, (table - high.astype(np.float64)).astype(jnp.bfloat16)]
    return tables


def tile_is_first():
    return lax.axis_index("tile") == 0


def scan_is_even():
    return lax.rem(lax.axis_index("scan"), 2) == 0


def outer_rows(ya_ref, yb_ref, channel):
    last = ya_ref.shape[1] - 1
    first = tile_is_first()
    below = jnp.where(first, yb_ref[channel, last], ya_ref[channel, last])
    above = jnp.where(first, ya_ref[channel, 0], yb_ref[channel, 0])
    return (below, above)


def slot_masks(rows_ref, columns_ref, count_ref, slot, side):
    lanes = lax.broadcasted_iota(jnp.int32, (side, side), 1)
    sublanes = lax.broadcasted_iota(jnp.int32, (side, side), 0)
    near_lanes = lanes >= rows_ref[0, slot]
    near_columns = sublanes >= columns_ref[0, slot]
    return (near_lanes, near_columns, jnp.full((side, side), slot < count_ref[0, 0]))


def place(totals, part, term, masks, width):
    side = term.shape[0]
    near_lanes, near_columns, live = masks
    inner = live & near_columns
    outer = (live & jnp.logical_not(near_columns))[:width]
    for start, lane_mask in ((0, near_lanes), (side, jnp.logical_not(near_lanes))):
        at = slice(start, start + side)
        totals[part, :side, at] += jnp.where(inner & lane_mask, term, 0.0)
        totals[part, side:, at] += jnp.where(outer & lane_mask[:width], term[:width], 0.0)


def prepare_kernel(rows_ref, columns_ref, count_ref, probe_ref, *refs):
    half = (len(refs) - 3) // 2
    sources, (probes_ref, density_ref), targets, done = refs[:half], refs[half : half + 2], refs[half + 2 : -1], refs[-1]
    copies = [
        pltpu.make_async_copy(source, target, done.at[number])
        for number, (source, target) in enumerate(zip(sources, targets))
    ]
    for copy in copies:
        copy.start()
    side = probe_ref.shape[1]
    slots = probes_ref.shape[0]
    width = density_ref.shape[1] - side
    density_ref[...] = jnp.zeros_like(density_ref)
    for slot in range(slots):
        turn = lax.rem(rows_ref[0, slot], side)
        probe = [
            pltpu.roll(pltpu.roll(probe_ref[part], columns_ref[0, slot], 0), turn, 1)
            for part in range(2)
        ]
        for part in range(2):
            probes_ref[slot, part] = probe[part]
        masks = slot_masks(rows_ref, columns_ref, count_ref, slot, side)
        place(density_ref, 0, probe[0] * probe[0] + probe[1] * probe[1], masks, width)
    for copy in copies:
        copy.wait()


def patch_kernel(
    rows_ref,
    columns_ref,
    count_ref,
    probes_ref,
    density_ref,
    plane_ref,
    intensity_ref,
    volume_ref,
    forward_high_ref,
    forward_low_ref,
    inverse_high_ref,
    inverse_low_ref,
    plane_a_ref,
    plane_b_ref,
    ya_ref,
    yb_ref,
    own_ref,
    rim_a_ref,
    rim_b_ref,
    wide,
    totals,
):
    width = plane_ref.shape[2]
    slots, _, side, _ = probes_ref.shape
    even = scan_is_even()
    at_a = pl.multiple_of(jnp.where(even, 2 * width, 0), width)
    at_b = pl.multiple_of(jnp.where(even, 0, 2 * width), width)
    wide[:, width : 2 * width] = plane_ref[0]
    wide[:, pl.ds(at_a, width)] = plane_a_ref[0]
    wide[:, pl.ds(at_b, width)] = plane_b_ref[0]
    forward = (forward_high_ref[...], forward_low_ref[...])
    inverse = (inverse_high_ref[...], inverse_low_ref[...])
    waves, masks = [], []
    for slot in range(slots):
        probe = probes_ref[slot]
        masks.append(slot_masks(rows_ref, columns_ref, count_ref, slot, side))
        near_lanes, near_columns, _ = masks[slot]
        window = []
        for part in range(2):
            near = jnp.where(near_lanes, wide[part, :side, :side], wide[part, :side, side:])
            wrapped = jnp.where(
                near_lanes[:width], wide[part, side:, :side], wide[part, side:, side:]
            )
            wrapped = jnp.concatenate([wrapped, near[width:]], axis=0)
            window.append(jnp.where(near_columns, near, wrapped))
        wave_real = probe[0] * window[0] - probe[1] * window[1]
        wave_imaginary = probe[0] * window[1] + probe[1] * window[0]
        waves.append(jnp.concatenate([wave_real, wave_imaginary], axis=1))
    half = product(split(jnp.concatenate(waves, axis=0)), inverse)
    half = jnp.concatenate(
        [
            jnp.concatenate(
                [half[slot * side : (slot + 1) * side, part * side : (part + 1) * side] for slot in range(slots)],
                axis=1,
            )
            for part in range(2)
        ],
        axis=0,
    )
    far = product(forward, split(half))
    far_real, far_imaginary = far[:side], far[side:]
    intensity = jnp.concatenate(
        [intensity_ref[0, slot].astype(jnp.float32) for slot in range(slots)], axis=1
    )
    factor = 1.0 - amplitude_step * (
        far_real * far_real + far_imaginary * far_imaginary - intensity
    )
    corrected = jnp.concatenate([far_real * factor, far_imaginary * factor], axis=0)
    half = product(inverse, split(corrected))
    half = jnp.concatenate(
        [
            jnp.concatenate(
                [half[part * side : (part + 1) * side, slot * side : (slot + 1) * side] for part in range(2)],
                axis=1,
            )
            for slot in range(slots)
        ],
        axis=0,
    )
    near = product(split(half), forward)
    totals[:2] = jnp.zeros_like(totals[:2])
    totals[2:] = density_ref[...]
    for slot in range(slots):
        probe = probes_ref[slot]
        near_real = near[slot * side : (slot + 1) * side, :side]
        near_imaginary = near[slot * side : (slot + 1) * side, side:]
        place(totals, 0, probe[0] * near_real + probe[1] * near_imaginary, masks[slot], width)
        place(totals, 1, probe[0] * near_imaginary - probe[1] * near_real, masks[slot], width)
    own_ref[...] = totals[:, width : 2 * width]
    below_above = [outer_rows(ya_ref, yb_ref, channel) for channel in range(2)]
    parts = totals.shape[0]
    count = volume_ref.shape[1]
    for rim_ref, at, low in ((rim_a_ref, at_a, jnp.logical_not(even)), (rim_b_ref, at_b, even)):
        for part in range(parts):
            rim_ref[part * width : (part + 1) * width] = totals[part, pl.ds(at, width)]
        edge_rows = []
        for channel in range(2):
            planes = [below_above[channel][0]]
            planes += [volume_ref[channel, row] for row in range(count)]
            planes.append(below_above[channel][1])
            for plane in planes:
                edge_rows.append(jnp.where(low, plane[:1], plane[width - 1 :]))
        rim_ref[parts * width :] = jnp.concatenate(edge_rows, axis=0)


def fold_kernel(own_ref, rim_a_ref, rim_b_ref, projected_ref, dual_ref, object_ref, residual_ref):
    width = own_ref.shape[1]
    sums = [
        own_ref[part]
        + rim_a_ref[part * width : (part + 1) * width]
        + rim_b_ref[part * width : (part + 1) * width]
        for part in range(3)
    ]
    for part in range(2):
        target = projected_ref[0, part]
        dual = dual_ref[0, part]
        updated = (sums[part] + penalty * (target - dual)) / (sums[2] + penalty)
        object_ref[0, part] = updated
        residual_ref[part] = target - updated - dual


def variation_kernel(volume_ref, ya_ref, yb_ref, rim_a_ref, rim_b_ref, base_ref, padded, norms):
    width = volume_ref.shape[2]
    length = volume_ref.shape[3]
    count = volume_ref.shape[1]
    margin = 8
    edges_at = rim_a_ref.shape[0] - 2 * (count + 2)
    even = scan_is_even()
    lanes = lax.broadcasted_iota(jnp.int32, (width, length), 1)
    first_lane = lanes == 0
    last_lane = lanes == length - 1
    for channel in range(2):
        below, above = outer_rows(ya_ref, yb_ref, channel)
        planes = [below] + [volume_ref[channel, row] for row in range(count)] + [above]
        for row, plane in enumerate(planes):
            at = edges_at + channel * (count + 2) + row
            edge_a = rim_a_ref[at : at + 1]
            edge_b = rim_b_ref[at : at + 1]
            padded[row, margin : margin + width] = plane
            padded[row, margin - 1 : margin] = jnp.where(even, edge_b, edge_a)
            padded[row, margin + width : margin + width + 1] = jnp.where(even, edge_a, edge_b)
        previous_y = None
        for row in range(count + 1):
            here = padded[row, margin : margin + width]
            along_y = padded[row + 1, margin : margin + width] - here
            along_x = padded[row, margin + 1 : margin + width + 1] - here
            along_z = jnp.where(last_lane, 0.0, pltpu.roll(here, length - 1, 1)) - here
            inverse = lax.rsqrt(
                along_y * along_y + along_x * along_x + along_z * along_z + smoothing * smoothing
            )
            norm_y = along_y * inverse
            if row > 0:
                norm_x = along_x * inverse
                norm_z = along_z * inverse
                corner = padded[row, margin - 1 : margin]
                corner_y = padded[row + 1, margin - 1 : margin] - corner
                corner_x = here[:1] - corner
                corner_z = (
                    jnp.where(last_lane[:1], 0.0, pltpu.roll(corner, length - 1, 1)) - corner
                )
                corner_norm = corner_x * lax.rsqrt(
                    corner_y * corner_y
                    + corner_x * corner_x
                    + corner_z * corner_z
                    + smoothing * smoothing
                )
                norms[margin : margin + width] = norm_x
                norms[margin - 1 : margin] = corner_norm
                behind_x = norms[margin - 1 : margin + width - 1]
                ahead = here * lax.rsqrt(here * here + smoothing * smoothing)
                behind_z = jnp.where(first_lane, ahead, pltpu.roll(norm_z, 1, 1))
                divergence = (
                    norm_y - previous_y + (norm_x - behind_x) + (norm_z - behind_z)
                )
                base_ref[channel, row - 1] = here + (step_size * tv_weight) * divergence
            previous_y = norm_y


def project_kernel(
    shift_ref,
    weight_ref,
    here_ref,
    side_a_ref,
    side_b_ref,
    here_too_ref,
    side_a_too_ref,
    side_b_too_ref,
    base_ref,
    beside_ref,
    volume_ref,
    keep_ref,
    send_ref,
    wide,
    updated,
):
    width = base_ref.shape[2]
    count = base_ref.shape[1]
    columns = here_ref.shape[0]
    tiles = lax.axis_size("tile")
    angles = columns * tiles
    me, tile, scan = lax.axis_index("angle"), lax.axis_index("tile"), lax.axis_index("scan")
    upper = me >= columns // 2
    even = scan_is_even()
    at_a = pl.multiple_of(jnp.where(even, 2 * width, 0), width)
    at_b = pl.multiple_of(jnp.where(even, 0, 2 * width), width)

    def angle_of(turn, flip):
        return lax.rem(me + turn, columns) * tiles + (tile if flip == 0 else 1 - tile)

    chunks = [slice(at, at + LANES) for at in range(0, base_ref.shape[3], LANES)]
    blocks = ((here_ref, side_a_ref, side_b_ref), (here_too_ref, side_a_too_ref, side_b_too_ref))
    for turn in range(columns):
        for flip in range(tiles):
            angle = angle_of(turn, flip)
            for chunk, at in enumerate(chunks):
                for ref, start in zip(blocks[flip], (width, at_a, at_b)):
                    wide[angle, :, chunk, pl.ds(start, width)] = ref[turn, :, :, at]
    exists = jnp.where(upper, scan < lax.axis_size("scan") - 1, scan > 0).astype(jnp.float32)
    own_at = pl.multiple_of(jnp.where(upper, 0, width), width)
    beside_at = pl.multiple_of(jnp.where(upper, width, 0), width)
    for row in range(count):
        for channel in range(2):
            for chunk, at in enumerate(chunks):
                total = jnp.zeros((2 * width, LANES), jnp.float32)
                for angle in range(angles):
                    start = jnp.where(upper, width, 0) - shift_ref[row, angle]
                    fraction = weight_ref[row, angle]
                    total += (1.0 - fraction) * wide[angle, channel, chunk, pl.ds(start, 2 * width)]
                    total += fraction * wide[angle, channel, chunk, pl.ds(start - 1, 2 * width)]
                updated[row, channel, chunk] = total
                part = updated.at[row, channel, chunk]
                own = base_ref[channel, row, :, at] - step_size * part[pl.ds(own_at, width)]
                beside = beside_ref[channel, row, :, at] - step_size * part[pl.ds(beside_at, width)]
                volume_ref[channel, row, :, at] = own
                part[pl.ds(own_at, width)] = own
                part[pl.ds(beside_at, width)] = beside * exists
    for turn in range(columns):
        for flip, out_ref in ((0, keep_ref), (1, send_ref)):
            angle = angle_of(turn, flip)
            for channel in range(2):
                for chunk, at in enumerate(chunks):
                    total = jnp.zeros((width, LANES), jnp.float32)
                    for row in range(count):
                        start = jnp.where(upper, 0, width) + shift_ref[row, angle]
                        fraction = weight_ref[row, angle]
                        total += (1.0 - fraction) * updated[row, channel, chunk, pl.ds(start, width)]
                        total += fraction * updated[row, channel, chunk, pl.ds(start + 1, width)]
                    out_ref[turn, channel, :, at] = total


def call(kernel, shapes, operands, scratch, flops, scalars=0, staged=()):
    held = sum(operand.nbytes for operand in operands[scalars:] + staged)
    held += 4 * sum(math.prod(shape) for shape in shapes)
    own = 4 * sum(math.prod(shape) for shape in scratch)
    outputs = [jax.ShapeDtypeStruct(shape, jnp.float32) for shape in shapes]
    outputs += [jax.ShapeDtypeStruct(array.shape, array.dtype) for array in staged]
    scratch_shapes = [pltpu.VMEM(shape, jnp.float32) for shape in scratch]
    if staged:
        scratch_shapes.append(pltpu.SemaphoreType.DMA((len(staged),)))
    in_specs = [SMEM] * scalars + [VMEM] * (len(operands) - scalars) + [HBM] * len(staged)
    return pl.pallas_call(
        kernel,
        out_shape=outputs,
        in_specs=in_specs,
        out_specs=[VMEM] * len(outputs),
        scratch_shapes=scratch_shapes,
        compiler_params=pltpu.CompilerParams(vmem_limit_bytes=held + own + SPARE_BYTES),
        cost_estimate=pl.CostEstimate(flops=flops, bytes_accessed=held, transcendentals=0),
    )(*operands, *(pltpu.with_memory_space_constraint(array, pltpu.HBM) for array in staged))


def body(
    transmission,
    scaled_dual,
    projected,
    volume,
    intensities,
    probe_wave,
    slot_first_rows,
    slot_first_columns,
    patch_counts,
    shift_table,
    tap_weight,
):
    width, length = transmission.shape[2:]
    count = volume.shape[1]
    scans, columns, tiles = (lax.axis_size(axis) for axis in ("scan", "angle", "tile"))
    rounds = [[(i, i + 1) for i in range(first, scans - 1, 2)] for first in (0, 1)]
    both = [pairs + [(target, source) for source, target in pairs] for pairs in rounds]
    swap = [(0, 1), (1, 0)]

    def exchange(block, number):
        return lax.ppermute(block, "scan", both[number])

    def across(block):
        return lax.ppermute(block, "tile", swap)

    plane_a = exchange(transmission, 0)
    plane_b = exchange(transmission, 1)
    bridge = [(i * tiles + 1, (i + 1) * tiles) for i in range(columns - 1)]
    bridge += [(target, source) for source, target in bridge]
    rows_b = lax.ppermute(volume, ("angle", "tile"), bridge)
    rows_a = across(volume)
    tables = [jnp.asarray(table) for table in dft_tables(probe_wave.shape[1])]
    rim_rows = 3 * width + 2 * (count + 2)
    scalars = (slot_first_rows, slot_first_columns, patch_counts)
    slots = slot_first_rows.shape[1]
    side = probe_wave.shape[1]
    prepared = call(
        prepare_kernel,
        [(slots, 2, side, side), (1, 3 * width, length)],
        (*scalars, probe_wave),
        [],
        10**7,
        3,
        (transmission, intensities, volume, *tables),
    )
    volume_here = prepared[4]
    own, rim_a, rim_b = call(
        patch_kernel,
        [(3, width, length), (rim_rows, length), (rim_rows, length)],
        (*scalars, *prepared, plane_a, plane_b, rows_a, rows_b),
        [(2, 3 * width, length), (3, 3 * width, length)],
        10**9,
        3,
    )
    rim_a = exchange(rim_a, 0)
    rim_b = exchange(rim_b, 1)
    new_transmission, residual = call(
        fold_kernel,
        [transmission.shape, transmission.shape[1:]],
        (own, rim_a, rim_b, projected, scaled_dual),
        [],
        10**6,
    )
    by_column = [residual]
    for turn in range(1, columns):
        route = [(i, (i - turn) % columns) for i in range(columns)]
        by_column.append(lax.ppermute(residual, "angle", route))
    (base,) = call(
        variation_kernel,
        [volume.shape],
        (volume_here, rows_a, rows_b, rim_a, rim_b),
        [(count + 2, width + 16, length), (width + 16, length)],
        10**7,
    )
    lower = range(columns // 2)
    route = []
    for scan in range(scans):
        for column in range(columns):
            target = scan + 1 if column in lower else scan - 1
            if 0 <= target < scans:
                route.append((scan * columns + column, target * columns + column))
    beside = lax.ppermute(base, ("scan", "angle"), route)
    here = jnp.stack(by_column)
    side_a = exchange(here, 0)
    side_b = exchange(here, 1)
    shared = [across(block) for block in (here, side_a, side_b)]
    new_volume, keep, send = call(
        project_kernel,
        [volume.shape, (columns, 2, width, length), (columns, 2, width, length)],
        (shift_table.T, tap_weight.T, here, side_a, side_b, *shared, base, beside),
        [
            (columns * tiles, 2, length // LANES, 3 * width, LANES),
            (count, 2, length // LANES, 2 * width, LANES),
        ],
        10**8,
        2,
    )
    received = across(send)
    new_projected = keep[0] + received[0]
    for turn in range(1, columns):
        route = [(i, (i + turn) % columns) for i in range(columns)]
        part = lax.ppermute(keep[turn] + received[turn], "angle", route)
        new_projected = new_projected + part
    new_projected = new_projected[None]
    new_dual = scaled_dual + new_transmission - new_projected
    return (new_transmission, new_dual, new_volume, new_projected)


def solution(mesh):
    plane = P(("groups", "angle", "tile"), None, "scan", None)
    cells = P("groups", ("angle", "tile"), "scan", None)
    slots = P(("groups", "angle", "tile"), "scan")
    return jax.shard_map(
        body,
        mesh=mesh,
        in_specs=(
            plane,
            plane,
            plane,
            cells,
            P(("groups", "angle", "tile"), "scan", None, None),
            P("groups", None, None),
            slots,
            slots,
            slots,
            P(None, ("angle", "tile")),
            P(None, ("angle", "tile")),
        ),
        out_specs=(plane, plane, cells, plane),
        check_vma=False,
    )
```

```python
import math

import jax
import jax.numpy as jnp
import numpy as np
from jax import lax
from jax.experimental import pallas as pl
from jax.experimental.pallas import tpu as pltpu
from jax.sharding import PartitionSpec as P


penalty = 4.0
amplitude_step = 0.25
tv_weight = 1.0
smoothing = 0.05
step_size = 0.008

VMEM = pl.BlockSpec(memory_space=pltpu.VMEM)
SMEM = pl.BlockSpec(memory_space=pltpu.SMEM)
HBM = pl.BlockSpec(memory_space=pltpu.MemorySpace.HBM)
LANES = 128
SUBLANES = 8
SPARE_BYTES = 8 << 20


def split(values):
    high = values.astype(jnp.bfloat16)
    return (high, (values - high.astype(jnp.float32)).astype(jnp.bfloat16))


def product(left, right):
    total = jnp.dot(left[0], right[0], preferred_element_type=jnp.float32)
    total += jnp.dot(left[0], right[1], preferred_element_type=jnp.float32)
    return total + jnp.dot(left[1], right[0], preferred_element_type=jnp.float32)


def dft_tables(length):
    grid_ids = np.arange(length)
    radians = (grid_ids[:, None] * grid_ids[None, :] % length) * (2.0 * math.pi / length)
    cosine = np.cos(radians) / math.sqrt(length)
    sine = np.sin(radians) / math.sqrt(length)
    forward = np.block([[cosine, sine], [-sine, cosine]])
    tables = []
    for table in (forward, forward.T):
        high = table.astype(jnp.bfloat16)
        tables += [high, (table - high.astype(np.float64)).astype(jnp.bfloat16)]
    return tables


def tile_is_first():
    return lax.axis_index("tile") == 0


def scan_is_even():
    return lax.rem(lax.axis_index("scan"), 2) == 0


def outer_rows(ya_ref, yb_ref, channel):
    last = ya_ref.shape[1] - 1
    first = tile_is_first()
    below = jnp.where(first, yb_ref[channel, last], ya_ref[channel, last])
    above = jnp.where(first, ya_ref[channel, 0], yb_ref[channel, 0])
    return (below, above)


def slot_masks(rows_ref, columns_ref, count_ref, slot, side):
    lanes = lax.broadcasted_iota(jnp.int32, (side, side), 1)
    sublanes = lax.broadcasted_iota(jnp.int32, (side, side), 0)
    near_lanes = lanes >= rows_ref[0, slot]
    near_columns = sublanes >= columns_ref[0, slot]
    return (near_lanes, near_columns, jnp.full((side, side), slot < count_ref[0, 0]))


def place(totals, part, term, masks, width):
    side = term.shape[0]
    near_lanes, near_columns, live = masks
    inner = live & near_columns
    outer = (live & jnp.logical_not(near_columns))[:width]
    for start, lane_mask in ((0, near_lanes), (side, jnp.logical_not(near_lanes))):
        at = slice(start, start + side)
        totals[part, :side, at] += jnp.where(inner & lane_mask, term, 0.0)
        totals[part, side:, at] += jnp.where(outer & lane_mask[:width], term[:width], 0.0)


def prepare_kernel(
    rows_ref, columns_ref, count_ref, shift_ref, weight_ref, probe_ref, *refs
):
    half = (len(refs) - 4) // 2
    sources, targets, done = refs[:half], refs[half + 3 : -1], refs[-1]
    probes_ref, density_ref, tables_ref = refs[half : half + 3]
    copies = [
        pltpu.make_async_copy(source, target, done.at[number])
        for number, (source, target) in enumerate(zip(sources, targets))
    ]
    for copy in copies:
        copy.start()
    side = probe_ref.shape[1]
    slots = probes_ref.shape[0]
    width = density_ref.shape[1] - side
    density_ref[...] = jnp.zeros_like(density_ref)
    for slot in range(slots):
        turn = lax.rem(rows_ref[0, slot], side)
        probe = [
            pltpu.roll(pltpu.roll(probe_ref[part], columns_ref[0, slot], 0), turn, 1)
            for part in range(2)
        ]
        for part in range(2):
            probes_ref[slot, part] = probe[part]
        masks = slot_masks(rows_ref, columns_ref, count_ref, slot, side)
        place(density_ref, 0, probe[0] * probe[0] + probe[1] * probe[1], masks, width)
    places = lax.broadcasted_iota(jnp.int32, tables_ref.shape[1:], 0)
    for angle in range(tables_ref.shape[0]):
        table = jnp.zeros(tables_ref.shape[1:], jnp.float32)
        for row in range(shift_ref.shape[0]):
            table = jnp.where(places == 2 * row, shift_ref[row, angle].astype(jnp.float32), table)
            table = jnp.where(places == 2 * row + 1, weight_ref[row, angle], table)
        tables_ref[angle] = table
    for copy in copies:
        copy.wait()


def patch_kernel(
    rows_ref,
    columns_ref,
    count_ref,
    probes_ref,
    density_ref,
    plane_ref,
    intensity_ref,
    volume_ref,
    forward_high_ref,
    forward_low_ref,
    inverse_high_ref,
    inverse_low_ref,
    plane_a_ref,
    plane_b_ref,
    ya_ref,
    yb_ref,
    own_ref,
    rim_a_ref,
    rim_b_ref,
    wide,
    totals,
):
    width = plane_ref.shape[2]
    slots, _, side, _ = probes_ref.shape
    even = scan_is_even()
    at_a = pl.multiple_of(jnp.where(even, 2 * width, 0), width)
    at_b = pl.multiple_of(jnp.where(even, 0, 2 * width), width)
    wide[:, width : 2 * width] = plane_ref[0]
    wide[:, pl.ds(at_a, width)] = plane_a_ref[0]
    wide[:, pl.ds(at_b, width)] = plane_b_ref[0]
    forward = (forward_high_ref[...], forward_low_ref[...])
    inverse = (inverse_high_ref[...], inverse_low_ref[...])
    waves, masks = [], []
    for slot in range(slots):
        probe = probes_ref[slot]
        masks.append(slot_masks(rows_ref, columns_ref, count_ref, slot, side))
        near_lanes, near_columns, _ = masks[slot]
        window = []
        for part in range(2):
            near = jnp.where(near_lanes, wide[part, :side, :side], wide[part, :side, side:])
            wrapped = jnp.where(
                near_lanes[:width], wide[part, side:, :side], wide[part, side:, side:]
            )
            wrapped = jnp.concatenate([wrapped, near[width:]], axis=0)
            window.append(jnp.where(near_columns, near, wrapped))
        wave_real = probe[0] * window[0] - probe[1] * window[1]
        wave_imaginary = probe[0] * window[1] + probe[1] * window[0]
        waves.append(jnp.concatenate([wave_real, wave_imaginary], axis=1))
    half = product(split(jnp.concatenate(waves, axis=0)), inverse)
    half = jnp.concatenate(
        [
            jnp.concatenate(
                [half[slot * side : (slot + 1) * side, part * side : (part + 1) * side] for slot in range(slots)],
                axis=1,
            )
            for part in range(2)
        ],
        axis=0,
    )
    far = product(forward, split(half))
    far_real, far_imaginary = far[:side], far[side:]
    intensity = jnp.concatenate(
        [intensity_ref[0, slot].astype(jnp.float32) for slot in range(slots)], axis=1
    )
    factor = 1.0 - amplitude_step * (
        far_real * far_real + far_imaginary * far_imaginary - intensity
    )
    corrected = jnp.concatenate([far_real * factor, far_imaginary * factor], axis=0)
    half = product(inverse, split(corrected))
    half = jnp.concatenate(
        [
            jnp.concatenate(
                [half[part * side : (part + 1) * side, slot * side : (slot + 1) * side] for part in range(2)],
                axis=1,
            )
            for slot in range(slots)
        ],
        axis=0,
    )
    near = product(split(half), forward)
    totals[:2] = jnp.zeros_like(totals[:2])
    totals[2:] = density_ref[...]
    for slot in range(slots):
        probe = probes_ref[slot]
        near_real = near[slot * side : (slot + 1) * side, :side]
        near_imaginary = near[slot * side : (slot + 1) * side, side:]
        place(totals, 0, probe[0] * near_real + probe[1] * near_imaginary, masks[slot], width)
        place(totals, 1, probe[0] * near_imaginary - probe[1] * near_real, masks[slot], width)
    own_ref[...] = totals[:, width : 2 * width]
    below_above = [outer_rows(ya_ref, yb_ref, channel) for channel in range(2)]
    parts = totals.shape[0]
    count = volume_ref.shape[1]
    for rim_ref, at, low in ((rim_a_ref, at_a, jnp.logical_not(even)), (rim_b_ref, at_b, even)):
        for part in range(parts):
            rim_ref[part * width : (part + 1) * width] = totals[part, pl.ds(at, width)]
        edge_rows = []
        for channel in range(2):
            planes = [below_above[channel][0]]
            planes += [volume_ref[channel, row] for row in range(count)]
            planes.append(below_above[channel][1])
            for plane in planes:
                edge_rows.append(jnp.where(low, plane[:1], plane[width - 1 :]))
        rim_ref[parts * width :] = jnp.concatenate(edge_rows, axis=0)


def fold_kernel(own_ref, rim_a_ref, rim_b_ref, projected_ref, dual_ref, object_ref, residual_ref):
    width = own_ref.shape[1]
    sums = [
        own_ref[part]
        + rim_a_ref[part * width : (part + 1) * width]
        + rim_b_ref[part * width : (part + 1) * width]
        for part in range(3)
    ]
    for part in range(2):
        target = projected_ref[0, part]
        dual = dual_ref[0, part]
        updated = (sums[part] + penalty * (target - dual)) / (sums[2] + penalty)
        object_ref[0, part] = updated
        residual_ref[part * width : (part + 1) * width] = target - updated - dual


def variation_kernel(volume_ref, ya_ref, yb_ref, rim_a_ref, rim_b_ref, base_ref, padded, norms):
    width = volume_ref.shape[2]
    length = volume_ref.shape[3]
    count = volume_ref.shape[1]
    margin = 8
    edges_at = rim_a_ref.shape[0] - 2 * (count + 2)
    even = scan_is_even()
    lanes = lax.broadcasted_iota(jnp.int32, (width, length), 1)
    first_lane = lanes == 0
    last_lane = lanes == length - 1
    for channel in range(2):
        below, above = outer_rows(ya_ref, yb_ref, channel)
        planes = [below] + [volume_ref[channel, row] for row in range(count)] + [above]
        for row, plane in enumerate(planes):
            at = edges_at + channel * (count + 2) + row
            edge_a = rim_a_ref[at : at + 1]
            edge_b = rim_b_ref[at : at + 1]
            padded[row, margin : margin + width] = plane
            padded[row, margin - 1 : margin] = jnp.where(even, edge_b, edge_a)
            padded[row, margin + width : margin + width + 1] = jnp.where(even, edge_a, edge_b)
        previous_y = None
        for row in range(count + 1):
            here = padded[row, margin : margin + width]
            along_y = padded[row + 1, margin : margin + width] - here
            along_x = padded[row, margin + 1 : margin + width + 1] - here
            along_z = jnp.where(last_lane, 0.0, pltpu.roll(here, length - 1, 1)) - here
            inverse = lax.rsqrt(
                along_y * along_y + along_x * along_x + along_z * along_z + smoothing * smoothing
            )
            norm_y = along_y * inverse
            if row > 0:
                norm_x = along_x * inverse
                norm_z = along_z * inverse
                corner = padded[row, margin - 1 : margin]
                corner_y = padded[row + 1, margin - 1 : margin] - corner
                corner_x = here[:1] - corner
                corner_z = (
                    jnp.where(last_lane[:1], 0.0, pltpu.roll(corner, length - 1, 1)) - corner
                )
                corner_norm = corner_x * lax.rsqrt(
                    corner_y * corner_y
                    + corner_x * corner_x
                    + corner_z * corner_z
                    + smoothing * smoothing
                )
                norms[margin : margin + width] = norm_x
                norms[margin - 1 : margin] = corner_norm
                behind_x = norms[margin - 1 : margin + width - 1]
                ahead = here * lax.rsqrt(here * here + smoothing * smoothing)
                behind_z = jnp.where(first_lane, ahead, pltpu.roll(norm_z, 1, 1))
                divergence = (
                    norm_y - previous_y + (norm_x - behind_x) + (norm_z - behind_z)
                )
                base_ref[channel, row - 1] = here + (step_size * tv_weight) * divergence
            previous_y = norm_y


def spread_kernel(shift_ref, weight_ref, base_ref, beside_ref, keep_ref, send_ref, padded):
    width = base_ref.shape[2]
    count = base_ref.shape[1]
    columns, tiles = keep_ref.shape[0], lax.axis_size("tile")
    me, tile, scan = lax.axis_index("angle"), lax.axis_index("tile"), lax.axis_index("scan")
    upper = me >= columns // 2
    chunks = [slice(at, at + LANES) for at in range(0, base_ref.shape[3], LANES)]
    exists = jnp.where(upper, scan < lax.axis_size("scan") - 1, scan > 0).astype(jnp.float32)
    own_at = pl.multiple_of(jnp.where(upper, 0, width), width)
    beside_at = pl.multiple_of(jnp.where(upper, width, 0), width)
    for row in range(count):
        for channel in range(2):
            for chunk, at in enumerate(chunks):
                padded[row, channel, chunk, pl.ds(own_at, width)] = base_ref[channel, row, :, at]
                padded[row, channel, chunk, pl.ds(beside_at, width)] = (
                    beside_ref[channel, row, :, at] * exists
                )
    for turn in range(columns):
        for flip, out_ref in ((0, keep_ref), (1, send_ref)):
            angle = lax.rem(me + turn, columns) * tiles + (tile if flip == 0 else 1 - tile)
            for channel in range(2):
                for chunk, at in enumerate(chunks):
                    total = jnp.zeros((width, LANES), jnp.float32)
                    for row in range(count):
                        start = jnp.where(upper, 0, width) + shift_ref[row, angle]
                        fraction = weight_ref[row, angle]
                        total += (1.0 - fraction) * padded[row, channel, chunk, pl.ds(start, width)]
                        total += fraction * padded[row, channel, chunk, pl.ds(start + 1, width)]
                    out_ref[turn, channel, :, at] = total


def operator_kernel(*refs):
    rays, (high_ref, low_ref) = refs[:-2], refs[-2:]
    tiles = lax.axis_size("tile")
    columns = len(rays) // tiles
    rows_out, reach = high_ref.shape[1:]
    width = reach // 3
    count = rows_out // (2 * width) - 1
    me, tile, scan = lax.axis_index("angle"), lax.axis_index("tile"), lax.axis_index("scan")

    def taps(shape, first, table, row, step):
        lanes = lax.broadcasted_iota(jnp.int32, shape, 1)
        sublanes = lax.broadcasted_iota(jnp.int32, shape, 0)
        offset = (lanes - sublanes).astype(jnp.float32) - first
        shift = step * table[2 * row : 2 * row + 1, : shape[1]]
        fraction = table[2 * row + 1 : 2 * row + 2, : shape[1]]
        return jnp.where(offset == shift, 1.0 - fraction, 0.0) + jnp.where(
            offset == shift + step, fraction, 0.0
        )

    def angle_of(turn, flip):
        return lax.rem(me + turn, columns) * tiles + (tile if flip == 0 else 1 - tile)

    cells = lax.broadcasted_iota(jnp.int32, (width, 2 * width), 1)
    forward = []
    backward = [[] for _ in range(columns)]
    for turn in range(columns):
        upper = lax.rem(me + turn, columns) >= columns // 2
        base_at = jnp.where(upper, 0, width)
        first_cell = jnp.where(upper, 0, jnp.where(scan > 0, 0, width))
        end_cell = jnp.where(upper & (scan == lax.axis_size("scan") - 1), width, 2 * width)
        inside = (cells >= first_cell) & (cells < end_cell)
        for flip in range(tiles):
            for row in range(count):
                parts = []
                for own in range(tiles):
                    table = rays[turn * tiles + flip][angle_of(0, own)]
                    part = taps((width, 2 * width), base_at.astype(jnp.float32), table, row, 1.0)
                    parts.append(jnp.where(inside, part, 0.0))
                forward.append(jnp.concatenate(parts, axis=0))
                for source in range(columns):
                    table = rays[turn * tiles + flip][angle_of(source, 0)]
                    first = (width - base_at).astype(jnp.float32)
                    backward[source].append(taps((2 * width, reach), first, table, row, -1.0))
    left = split(jnp.concatenate(forward, axis=1))
    for source in range(columns):
        both = product(left, split(jnp.concatenate(backward[source], axis=0)))
        blocks = [both]
        for flip in range(tiles):
            for row in range(count):
                table = rays[flip][angle_of(source, 0)]
                blocks.append(taps((width, reach), float(width), table, row, -1.0))
        high_ref[source], low_ref[source] = split(jnp.concatenate(blocks, axis=0))


def apply_kernel(here_ref, side_a_ref, side_b_ref, high_ref, low_ref, keep_ref, own_ref, send_ref, wide):
    width = keep_ref.shape[1]
    columns = here_ref.shape[0]
    count = own_ref.shape[1]
    even = scan_is_even()
    at_a = pl.multiple_of(jnp.where(even, 2 * width, 0), width)
    at_b = pl.multiple_of(jnp.where(even, 0, 2 * width), width)
    for source in range(columns):
        for channel in range(2):
            at = slice(channel * width, (channel + 1) * width)
            wide[source, channel, width : 2 * width] = here_ref[source, at]
            wide[source, channel, pl.ds(at_a, width)] = side_a_ref[source, at]
            wide[source, channel, pl.ds(at_b, width)] = side_b_ref[source, at]
    for channel in range(2):
        total = 0.0
        for source in range(columns):
            total += product((high_ref[source], low_ref[source]), split(wide[source, channel]))
        keep_ref[channel] = total[:width]
        send_ref[channel * width : (channel + 1) * width] = total[width : 2 * width]
        for row in range(count):
            at = (2 + row) * width
            own_ref[channel, row] = total[at : at + width]
            target = (2 + channel * count + row) * width
            send_ref[target : target + width] = total[at + count * width : at + (count + 1) * width]


def finish_kernel(
    keep_ref, own_ref, received_ref, base_ref, spread_ref, object_ref, dual_ref, dual_out_ref, volume_ref, projected_ref
):
    width = keep_ref.shape[1]
    count = own_ref.shape[1]
    for channel in range(2):
        received = received_ref[channel * width : (channel + 1) * width]
        projection = spread_ref[channel] - step_size * (keep_ref[channel] + received)
        projected_ref[0, channel] = projection
        dual_out_ref[0, channel] = dual_ref[0, channel] + object_ref[0, channel] - projection
        for row in range(count):
            at = (2 + channel * count + row) * width
            descent = own_ref[channel, row] + received_ref[at : at + width]
            volume_ref[channel, row] = base_ref[channel, row] - step_size * descent


def call(kernel, shapes, operands, scratch, flops, scalars=0, staged=(), kind=jnp.float32):
    held = sum(operand.nbytes for operand in operands[scalars:] + staged)
    held += 4 * sum(math.prod(shape) for shape in shapes)
    own = 4 * sum(math.prod(shape) for shape in scratch)
    outputs = [jax.ShapeDtypeStruct(shape, kind) for shape in shapes]
    outputs += [jax.ShapeDtypeStruct(array.shape, array.dtype) for array in staged]
    scratch_shapes = [pltpu.VMEM(shape, jnp.float32) for shape in scratch]
    if staged:
        scratch_shapes.append(pltpu.SemaphoreType.DMA((len(staged),)))
    in_specs = [SMEM] * scalars + [VMEM] * (len(operands) - scalars) + [HBM] * len(staged)
    return pl.pallas_call(
        kernel,
        out_shape=outputs,
        in_specs=in_specs,
        out_specs=[VMEM] * len(outputs),
        scratch_shapes=scratch_shapes,
        compiler_params=pltpu.CompilerParams(vmem_limit_bytes=held + own + SPARE_BYTES),
        cost_estimate=pl.CostEstimate(flops=flops, bytes_accessed=held, transcendentals=0),
    )(*operands, *(pltpu.with_memory_space_constraint(array, pltpu.HBM) for array in staged))


def body(
    transmission,
    scaled_dual,
    projected,
    volume,
    intensities,
    probe_wave,
    slot_first_rows,
    slot_first_columns,
    patch_counts,
    shift_table,
    tap_weight,
):
    width, length = transmission.shape[2:]
    count = volume.shape[1]
    scans, columns, tiles = (lax.axis_size(axis) for axis in ("scan", "angle", "tile"))
    rounds = [[(i, i + 1) for i in range(first, scans - 1, 2)] for first in (0, 1)]
    both = [pairs + [(target, source) for source, target in pairs] for pairs in rounds]
    swap = [(0, 1), (1, 0)]

    def exchange(block, number):
        return lax.ppermute(block, "scan", both[number])

    def across(block):
        return lax.ppermute(block, "tile", swap)

    plane_a = exchange(transmission, 0)
    plane_b = exchange(transmission, 1)
    bridge = [(i * tiles + 1, (i + 1) * tiles) for i in range(columns - 1)]
    bridge += [(target, source) for source, target in bridge]
    rows_b = lax.ppermute(volume, ("angle", "tile"), bridge)
    rows_a = across(volume)
    tables = [jnp.asarray(table) for table in dft_tables(probe_wave.shape[1])]
    rim_rows = 3 * width + 2 * (count + 2)
    scalars = (slot_first_rows, slot_first_columns, patch_counts)
    slots = slot_first_rows.shape[1]
    side = probe_wave.shape[1]
    probes, density, rays, *held = call(
        prepare_kernel,
        [(slots, 2, side, side), (1, 3 * width, length), (columns * tiles, SUBLANES, length)],
        (*scalars, shift_table.T, tap_weight.T, probe_wave),
        [],
        10**7,
        5,
        (transmission, intensities, volume, *tables),
    )
    volume_here = held[2]
    turns = [[(i, (i - turn) % columns) for i in range(columns)] for turn in range(columns)]
    by_row = [rays]
    for turn in range(1, columns):
        by_row.append(lax.ppermute(rays, "angle", turns[turn]))
    by_row = [block for table in by_row for block in (table, across(table))]
    own, rim_a, rim_b = call(
        patch_kernel,
        [(3, width, length), (rim_rows, length), (rim_rows, length)],
        (*scalars, probes, density, *held, plane_a, plane_b, rows_a, rows_b),
        [(2, 3 * width, length), (3, 3 * width, length)],
        10**9,
        3,
    )
    rim_a = exchange(rim_a, 0)
    rim_b = exchange(rim_b, 1)
    high, low = call(
        operator_kernel,
        [(columns, (2 + 2 * count) * width, 3 * width)] * 2,
        tuple(by_row),
        [],
        10**8,
        kind=jnp.bfloat16,
    )
    new_transmission, residual = call(
        fold_kernel,
        [transmission.shape, (2 * width, length)],
        (own, rim_a, rim_b, projected, scaled_dual),
        [],
        10**6,
    )
    by_column = [residual]
    for turn in range(1, columns):
        by_column.append(lax.ppermute(residual, "angle", turns[turn]))
    (base,) = call(
        variation_kernel,
        [volume.shape],
        (volume_here, rows_a, rows_b, rim_a, rim_b),
        [(count + 2, width + 16, length), (width + 16, length)],
        10**7,
    )
    lower = range(columns // 2)
    route = []
    for scan in range(scans):
        for column in range(columns):
            target = scan + 1 if column in lower else scan - 1
            if 0 <= target < scans:
                route.append((scan * columns + column, target * columns + column))
    beside = lax.ppermute(base, ("scan", "angle"), route)
    here = jnp.stack(by_column)
    side_a = exchange(here, 0)
    side_b = exchange(here, 1)
    block = (columns, 2, width, length)
    keep, send = call(
        spread_kernel,
        [block, block],
        (shift_table.T, tap_weight.T, base, beside),
        [(count, 2, length // LANES, 2 * width, LANES)],
        10**7,
        2,
    )
    received = across(send)
    spread = keep[0] + received[0]
    for turn in range(1, columns):
        route = [(i, (i + turn) % columns) for i in range(columns)]
        spread = spread + lax.ppermute(keep[turn] + received[turn], "angle", route)
    keep, own, send = call(
        apply_kernel,
        [(2, width, length), volume.shape, ((2 + 2 * count) * width, length)],
        (here, side_a, side_b, high, low),
        [(columns, 2, 3 * width, length)],
        10**9,
    )
    received = across(send)
    new_dual, new_volume, new_projected = call(
        finish_kernel,
        [transmission.shape, volume.shape, transmission.shape],
        (keep, own, received, base, spread, new_transmission, scaled_dual),
        [],
        10**6,
    )
    return (new_transmission, new_dual, new_volume, new_projected)


def solution(mesh):
    plane = P(("groups", "angle", "tile"), None, "scan", None)
    cells = P("groups", ("angle", "tile"), "scan", None)
    slots = P(("groups", "angle", "tile"), "scan")
    return jax.shard_map(
        body,
        mesh=mesh,
        in_specs=(
            plane,
            plane,
            plane,
            cells,
            P(("groups", "angle", "tile"), "scan", None, None),
            P("groups", None, None),
            slots,
            slots,
            slots,
            P(None, ("angle", "tile")),
            P(None, ("angle", "tile")),
        ),
        out_specs=(plane, plane, cells, plane),
        check_vma=False,
    )
```

```python
import math

import jax
import jax.numpy as jnp
import numpy as np
from jax import lax
from jax.experimental import pallas as pl
from jax.experimental.pallas import tpu as pltpu
from jax.sharding import PartitionSpec as P


penalty = 4.0
amplitude_step = 0.25
tv_weight = 1.0
smoothing = 0.05
step_size = 0.008

VMEM = pl.BlockSpec(memory_space=pltpu.VMEM)
SMEM = pl.BlockSpec(memory_space=pltpu.SMEM)
HBM = pl.BlockSpec(memory_space=pltpu.MemorySpace.HBM)
LANES = 128
SUBLANES = 8
SPARE_BYTES = 8 << 20


def split(values):
    high = values.astype(jnp.bfloat16)
    return (high, (values - high.astype(jnp.float32)).astype(jnp.bfloat16))


def product(left, right):
    total = jnp.dot(left[0], right[0], preferred_element_type=jnp.float32)
    total += jnp.dot(left[0], right[1], preferred_element_type=jnp.float32)
    return total + jnp.dot(left[1], right[0], preferred_element_type=jnp.float32)


def dft_tables(length):
    grid_ids = np.arange(length)
    radians = (grid_ids[:, None] * grid_ids[None, :] % length) * (2.0 * math.pi / length)
    cosine = np.cos(radians) / math.sqrt(length)
    sine = np.sin(radians) / math.sqrt(length)
    forward = np.block([[cosine, sine], [-sine, cosine]])
    tables = []
    for table in (forward, forward.T):
        high = table.astype(jnp.bfloat16)
        tables += [high, (table - high.astype(np.float64)).astype(jnp.bfloat16)]
    return tables


def tile_is_first():
    return lax.axis_index("tile") == 0


def scan_is_even():
    return lax.rem(lax.axis_index("scan"), 2) == 0


def pack_kernel(plane_ref, volume_ref, packed_ref, slabs, done):
    width = plane_ref.shape[2]
    count = volume_ref.shape[1]
    copies = [
        (plane_ref.at[0, channel], packed_ref.at[channel * width : (channel + 1) * width])
        for channel in range(2)
    ]
    for channel in range(2):
        for row in range(count):
            for side, at in enumerate((0, width - SUBLANES)):
                source = volume_ref.at[channel, row, at : at + SUBLANES]
                copies.append((source, slabs.at[(channel * count + row) * 2 + side]))
    copies = [
        pltpu.make_async_copy(source, target, done.at[number])
        for number, (source, target) in enumerate(copies)
    ]
    for copy in copies:
        copy.start()
    for copy in copies[2:]:
        copy.wait()
    for edge in range(slabs.shape[0]):
        take = 0 if edge % 2 == 0 else SUBLANES - 1
        packed_ref[2 * width + edge : 2 * width + edge + 1] = slabs[edge, take : take + 1]
    for copy in copies[:2]:
        copy.wait()


def edges_of(plane_a_ref, plane_b_ref, number, width):
    even = scan_is_even()
    at = 2 * width + 2 * number
    first_a, last_a = plane_a_ref[at : at + 1], plane_a_ref[at + 1 : at + 2]
    first_b, last_b = plane_b_ref[at : at + 1], plane_b_ref[at + 1 : at + 2]
    return (jnp.where(even, last_b, last_a), jnp.where(even, first_a, first_b))


def slot_masks(rows_ref, columns_ref, count_ref, slot, side):
    lanes = lax.broadcasted_iota(jnp.int32, (side, side), 1)
    sublanes = lax.broadcasted_iota(jnp.int32, (side, side), 0)
    near_lanes = lanes >= rows_ref[0, slot]
    near_columns = sublanes >= columns_ref[0, slot]
    return (near_lanes, near_columns, jnp.full((side, side), slot < count_ref[0, 0]))


def place(totals, part, term, masks, width):
    side = term.shape[0]
    near_lanes, near_columns, live = masks
    inner = live & near_columns
    outer = (live & jnp.logical_not(near_columns))[:width]
    for start, lane_mask in ((0, near_lanes), (side, jnp.logical_not(near_lanes))):
        at = slice(start, start + side)
        totals[part, :side, at] += jnp.where(inner & lane_mask, term, 0.0)
        totals[part, side:, at] += jnp.where(outer & lane_mask[:width], term[:width], 0.0)


def prepare_kernel(
    rows_ref, columns_ref, count_ref, shift_ref, weight_ref, *refs
):
    half = (len(refs) - 4) // 2
    sources, targets, done = refs[:half], refs[half + 3 : -1], refs[-1]
    probes_ref, density_ref, tables_ref = refs[half : half + 3]
    copies = [
        pltpu.make_async_copy(source, target, done.at[number])
        for number, (source, target) in enumerate(zip(sources, targets))
    ]
    for copy in copies:
        copy.start()
    probe_ref = targets[0]
    side = probe_ref.shape[1]
    slots = probes_ref.shape[0]
    width = density_ref.shape[1] - side
    density_ref[...] = jnp.zeros_like(density_ref)
    copies[0].wait()
    for slot in range(slots):
        turn = lax.rem(rows_ref[0, slot], side)
        probe = [
            pltpu.roll(pltpu.roll(probe_ref[part], columns_ref[0, slot], 0), turn, 1)
            for part in range(2)
        ]
        for part in range(2):
            probes_ref[slot, part] = probe[part]
        masks = slot_masks(rows_ref, columns_ref, count_ref, slot, side)
        place(density_ref, 0, probe[0] * probe[0] + probe[1] * probe[1], masks, width)
    places = lax.broadcasted_iota(jnp.int32, tables_ref.shape[1:], 0)
    for angle in range(tables_ref.shape[0]):
        table = jnp.zeros(tables_ref.shape[1:], jnp.float32)
        for row in range(shift_ref.shape[0]):
            table = jnp.where(places == 2 * row, shift_ref[row, angle].astype(jnp.float32), table)
            table = jnp.where(places == 2 * row + 1, weight_ref[row, angle], table)
        tables_ref[angle] = table
    for copy in copies[1:]:
        copy.wait()


def patch_kernel(
    rows_ref,
    columns_ref,
    count_ref,
    probes_ref,
    density_ref,
    plane_ref,
    intensity_ref,
    volume_ref,
    forward_high_ref,
    forward_low_ref,
    inverse_high_ref,
    inverse_low_ref,
    plane_a_ref,
    plane_b_ref,
    own_ref,
    rim_a_ref,
    rim_b_ref,
    row_a_ref,
    row_b_ref,
    wide,
    totals,
):
    width = volume_ref.shape[2]
    slots, _, side, _ = probes_ref.shape
    even = scan_is_even()
    at_a = pl.multiple_of(jnp.where(even, 2 * width, 0), width)
    at_b = pl.multiple_of(jnp.where(even, 0, 2 * width), width)
    for part in range(2):
        at = slice(part * width, (part + 1) * width)
        wide[part, width : 2 * width] = plane_ref[at]
        wide[part, pl.ds(at_a, width)] = plane_a_ref[at]
        wide[part, pl.ds(at_b, width)] = plane_b_ref[at]
    forward = (forward_high_ref[...], forward_low_ref[...])
    inverse = (inverse_high_ref[...], inverse_low_ref[...])
    waves, masks = [], []
    for slot in range(slots):
        probe = probes_ref[slot]
        masks.append(slot_masks(rows_ref, columns_ref, count_ref, slot, side))
        near_lanes, near_columns, _ = masks[slot]
        window = []
        for part in range(2):
            near = jnp.where(near_lanes, wide[part, :side, :side], wide[part, :side, side:])
            wrapped = jnp.where(
                near_lanes[:width], wide[part, side:, :side], wide[part, side:, side:]
            )
            wrapped = jnp.concatenate([wrapped, near[width:]], axis=0)
            window.append(jnp.where(near_columns, near, wrapped))
        wave_real = probe[0] * window[0] - probe[1] * window[1]
        wave_imaginary = probe[0] * window[1] + probe[1] * window[0]
        waves.append(jnp.concatenate([wave_real, wave_imaginary], axis=1))
    half = product(split(jnp.concatenate(waves, axis=0)), inverse)
    half = jnp.concatenate(
        [
            jnp.concatenate(
                [half[slot * side : (slot + 1) * side, part * side : (part + 1) * side] for slot in range(slots)],
                axis=1,
            )
            for part in range(2)
        ],
        axis=0,
    )
    far = product(forward, split(half))
    far_real, far_imaginary = far[:side], far[side:]
    intensity = jnp.concatenate(
        [intensity_ref[0, slot].astype(jnp.float32) for slot in range(slots)], axis=1
    )
    factor = 1.0 - amplitude_step * (
        far_real * far_real + far_imaginary * far_imaginary - intensity
    )
    corrected = jnp.concatenate([far_real * factor, far_imaginary * factor], axis=0)
    half = product(inverse, split(corrected))
    half = jnp.concatenate(
        [
            jnp.concatenate(
                [half[part * side : (part + 1) * side, slot * side : (slot + 1) * side] for part in range(2)],
                axis=1,
            )
            for slot in range(slots)
        ],
        axis=0,
    )
    near = product(split(half), forward)
    totals[:2] = jnp.zeros_like(totals[:2])
    totals[2:] = density_ref[...]
    for slot in range(slots):
        probe = probes_ref[slot]
        near_real = near[slot * side : (slot + 1) * side, :side]
        near_imaginary = near[slot * side : (slot + 1) * side, side:]
        place(totals, 0, probe[0] * near_real + probe[1] * near_imaginary, masks[slot], width)
        place(totals, 1, probe[0] * near_imaginary - probe[1] * near_real, masks[slot], width)
    own_ref[...] = totals[:, width : 2 * width]
    for rim_ref, at in ((rim_a_ref, at_a), (rim_b_ref, at_b)):
        for part in range(totals.shape[0]):
            rim_ref[part * width : (part + 1) * width] = totals[part, pl.ds(at, width)]
    first_tile = tile_is_first()
    count = volume_ref.shape[1]
    for channel in range(2):
        rows = []
        for row in (0, count - 1):
            before, after = edges_of(plane_a_ref, plane_b_ref, channel * count + row, width)
            rows.append((volume_ref[channel, row], jnp.concatenate([before, after], axis=0)))
        for low, row_ref in ((jnp.logical_not(first_tile), row_a_ref), (first_tile, row_b_ref)):
            row_ref[channel, :width] = jnp.where(low, rows[0][0], rows[1][0])
            row_ref[channel, width : width + 2] = jnp.where(low, rows[0][1], rows[1][1])


def fold_kernel(own_ref, rim_a_ref, rim_b_ref, projected_ref, dual_ref, object_ref, residual_ref):
    width = own_ref.shape[1]
    sums = [
        own_ref[part]
        + rim_a_ref[part * width : (part + 1) * width]
        + rim_b_ref[part * width : (part + 1) * width]
        for part in range(3)
    ]
    for part in range(2):
        target = projected_ref[0, part]
        dual = dual_ref[0, part]
        updated = (sums[part] + penalty * (target - dual)) / (sums[2] + penalty)
        object_ref[0, part] = updated
        residual_ref[part * width : (part + 1) * width] = target - updated - dual


def variation_kernel(
    volume_ref, plane_a_ref, plane_b_ref, row_a_ref, row_b_ref, base_ref, padded, norms
):
    width = volume_ref.shape[2]
    length = volume_ref.shape[3]
    count = volume_ref.shape[1]
    margin = 8
    first_tile = tile_is_first()
    lanes = lax.broadcasted_iota(jnp.int32, (width, length), 1)
    first_lane = lanes == 0
    last_lane = lanes == length - 1
    for channel in range(2):
        for row in range(count):
            before, after = edges_of(plane_a_ref, plane_b_ref, channel * count + row, width)
            padded[row + 1, margin : margin + width] = volume_ref[channel, row]
            padded[row + 1, margin - 1 : margin] = before
            padded[row + 1, margin + width : margin + width + 1] = after
        row_a, row_b = row_a_ref[channel], row_b_ref[channel]
        for row, beside in (
            (0, jnp.where(first_tile, row_b, row_a)),
            (count + 1, jnp.where(first_tile, row_a, row_b)),
        ):
            padded[row, margin : margin + width] = beside[:width]
            padded[row, margin - 1 : margin] = beside[width : width + 1]
            padded[row, margin + width : margin + width + 1] = beside[width + 1 : width + 2]
        previous_y = None
        for row in range(count + 1):
            here = padded[row, margin : margin + width]
            along_y = padded[row + 1, margin : margin + width] - here
            along_x = padded[row, margin + 1 : margin + width + 1] - here
            along_z = jnp.where(last_lane, 0.0, pltpu.roll(here, length - 1, 1)) - here
            inverse = lax.rsqrt(
                along_y * along_y + along_x * along_x + along_z * along_z + smoothing * smoothing
            )
            norm_y = along_y * inverse
            if row > 0:
                norm_x = along_x * inverse
                norm_z = along_z * inverse
                corner = padded[row, margin - 1 : margin]
                corner_y = padded[row + 1, margin - 1 : margin] - corner
                corner_x = here[:1] - corner
                corner_z = (
                    jnp.where(last_lane[:1], 0.0, pltpu.roll(corner, length - 1, 1)) - corner
                )
                corner_norm = corner_x * lax.rsqrt(
                    corner_y * corner_y
                    + corner_x * corner_x
                    + corner_z * corner_z
                    + smoothing * smoothing
                )
                norms[margin : margin + width] = norm_x
                norms[margin - 1 : margin] = corner_norm
                behind_x = norms[margin - 1 : margin + width - 1]
                ahead = here * lax.rsqrt(here * here + smoothing * smoothing)
                behind_z = jnp.where(first_lane, ahead, pltpu.roll(norm_z, 1, 1))
                divergence = (
                    norm_y - previous_y + (norm_x - behind_x) + (norm_z - behind_z)
                )
                base_ref[channel, row - 1] = here + (step_size * tv_weight) * divergence
            previous_y = norm_y


def spread_kernel(shift_ref, weight_ref, base_ref, beside_ref, keep_ref, send_ref, padded):
    width = base_ref.shape[2]
    count = base_ref.shape[1]
    columns, tiles = keep_ref.shape[0], lax.axis_size("tile")
    me, tile, scan = lax.axis_index("angle"), lax.axis_index("tile"), lax.axis_index("scan")
    upper = me >= columns // 2
    chunks = [slice(at, at + LANES) for at in range(0, base_ref.shape[3], LANES)]
    exists = jnp.where(upper, scan < lax.axis_size("scan") - 1, scan > 0).astype(jnp.float32)
    own_at = pl.multiple_of(jnp.where(upper, 0, width), width)
    beside_at = pl.multiple_of(jnp.where(upper, width, 0), width)
    for row in range(count):
        for channel in range(2):
            for chunk, at in enumerate(chunks):
                padded[row, channel, chunk, pl.ds(own_at, width)] = base_ref[channel, row, :, at]
                padded[row, channel, chunk, pl.ds(beside_at, width)] = (
                    beside_ref[channel, row, :, at] * exists
                )
    for turn in range(columns):
        for flip, out_ref in ((0, keep_ref), (1, send_ref)):
            angle = lax.rem(me + turn, columns) * tiles + (tile if flip == 0 else 1 - tile)
            for channel in range(2):
                for chunk, at in enumerate(chunks):
                    total = jnp.zeros((width, LANES), jnp.float32)
                    for row in range(count):
                        start = jnp.where(upper, 0, width) + shift_ref[row, angle]
                        fraction = weight_ref[row, angle]
                        total += (1.0 - fraction) * padded[row, channel, chunk, pl.ds(start, width)]
                        total += fraction * padded[row, channel, chunk, pl.ds(start + 1, width)]
                    out_ref[turn, channel, :, at] = total


def operator_kernel(*refs):
    rays, (high_ref, low_ref) = refs[:-2], refs[-2:]
    tiles = lax.axis_size("tile")
    columns = len(rays) // tiles
    rows_out, reach = high_ref.shape[1:]
    width = reach // 3
    count = rows_out // (2 * width) - 1
    me, tile, scan = lax.axis_index("angle"), lax.axis_index("tile"), lax.axis_index("scan")

    def taps(shape, first, table, row, step):
        lanes = lax.broadcasted_iota(jnp.int32, shape, 1)
        sublanes = lax.broadcasted_iota(jnp.int32, shape, 0)
        offset = (lanes - sublanes).astype(jnp.float32) - first
        shift = step * table[2 * row : 2 * row + 1, : shape[1]]
        fraction = table[2 * row + 1 : 2 * row + 2, : shape[1]]
        return jnp.where(offset == shift, 1.0 - fraction, 0.0) + jnp.where(
            offset == shift + step, fraction, 0.0
        )

    def angle_of(turn, flip):
        return lax.rem(me + turn, columns) * tiles + (tile if flip == 0 else 1 - tile)

    cells = lax.broadcasted_iota(jnp.int32, (width, 2 * width), 1)
    forward = []
    backward = [[] for _ in range(columns)]
    for turn in range(columns):
        upper = lax.rem(me + turn, columns) >= columns // 2
        base_at = jnp.where(upper, 0, width)
        first_cell = jnp.where(upper, 0, jnp.where(scan > 0, 0, width))
        end_cell = jnp.where(upper & (scan == lax.axis_size("scan") - 1), width, 2 * width)
        inside = (cells >= first_cell) & (cells < end_cell)
        for flip in range(tiles):
            for row in range(count):
                parts = []
                for own in range(tiles):
                    table = rays[turn * tiles + flip][angle_of(0, own)]
                    part = taps((width, 2 * width), base_at.astype(jnp.float32), table, row, 1.0)
                    parts.append(jnp.where(inside, part, 0.0))
                forward.append(jnp.concatenate(parts, axis=0))
                for source in range(columns):
                    table = rays[turn * tiles + flip][angle_of(source, 0)]
                    first = (width - base_at).astype(jnp.float32)
                    backward[source].append(taps((2 * width, reach), first, table, row, -1.0))
    left = split(jnp.concatenate(forward, axis=1))
    for source in range(columns):
        both = product(left, split(jnp.concatenate(backward[source], axis=0)))
        blocks = [both]
        for flip in range(tiles):
            for row in range(count):
                table = rays[flip][angle_of(source, 0)]
                blocks.append(taps((width, reach), float(width), table, row, -1.0))
        high_ref[source], low_ref[source] = split(jnp.concatenate(blocks, axis=0))


def apply_kernel(here_ref, side_a_ref, side_b_ref, high_ref, low_ref, keep_ref, own_ref, send_ref, wide):
    width = keep_ref.shape[1]
    columns = here_ref.shape[0]
    count = own_ref.shape[1]
    even = scan_is_even()
    at_a = pl.multiple_of(jnp.where(even, 2 * width, 0), width)
    at_b = pl.multiple_of(jnp.where(even, 0, 2 * width), width)
    for source in range(columns):
        for channel in range(2):
            at = slice(channel * width, (channel + 1) * width)
            wide[source, channel, width : 2 * width] = here_ref[source, at]
            wide[source, channel, pl.ds(at_a, width)] = side_a_ref[source, at]
            wide[source, channel, pl.ds(at_b, width)] = side_b_ref[source, at]
    for channel in range(2):
        total = 0.0
        for source in range(columns):
            total += product((high_ref[source], low_ref[source]), split(wide[source, channel]))
        keep_ref[channel] = total[:width]
        send_ref[channel * width : (channel + 1) * width] = total[width : 2 * width]
        for row in range(count):
            at = (2 + row) * width
            own_ref[channel, row] = total[at : at + width]
            target = (2 + channel * count + row) * width
            send_ref[target : target + width] = total[at + count * width : at + (count + 1) * width]


def finish_kernel(
    keep_ref, own_ref, received_ref, base_ref, spread_ref, object_ref, dual_ref, dual_out_ref, volume_ref, projected_ref
):
    width = keep_ref.shape[1]
    count = own_ref.shape[1]
    for channel in range(2):
        received = received_ref[channel * width : (channel + 1) * width]
        projection = spread_ref[channel] - step_size * (keep_ref[channel] + received)
        projected_ref[0, channel] = projection
        dual_out_ref[0, channel] = dual_ref[0, channel] + object_ref[0, channel] - projection
        for row in range(count):
            at = (2 + channel * count + row) * width
            descent = own_ref[channel, row] + received_ref[at : at + width]
            volume_ref[channel, row] = base_ref[channel, row] - step_size * descent


def call(kernel, shapes, operands, scratch, flops, scalars=0, staged=(), copies=0, kind=jnp.float32):
    held = sum(operand.nbytes for operand in operands[scalars:] + staged)
    held += 4 * sum(math.prod(shape) for shape in shapes)
    own = 4 * sum(math.prod(shape) for shape in scratch)
    outputs = [jax.ShapeDtypeStruct(shape, kind) for shape in shapes]
    scratch_shapes = [pltpu.VMEM(shape, jnp.float32) for shape in scratch]
    if staged and not copies:
        outputs += [jax.ShapeDtypeStruct(array.shape, array.dtype) for array in staged]
        copies = len(staged)
    if copies:
        scratch_shapes.append(pltpu.SemaphoreType.DMA((copies,)))
    in_specs = [SMEM] * scalars + [VMEM] * (len(operands) - scalars) + [HBM] * len(staged)
    return pl.pallas_call(
        kernel,
        out_shape=outputs,
        in_specs=in_specs,
        out_specs=[VMEM] * len(outputs),
        scratch_shapes=scratch_shapes,
        compiler_params=pltpu.CompilerParams(vmem_limit_bytes=held + own + SPARE_BYTES),
        cost_estimate=pl.CostEstimate(flops=flops, bytes_accessed=held, transcendentals=0),
    )(*operands, *(pltpu.with_memory_space_constraint(array, pltpu.HBM) for array in staged))


def body(
    transmission,
    scaled_dual,
    projected,
    volume,
    intensities,
    probe_wave,
    slot_first_rows,
    slot_first_columns,
    patch_counts,
    shift_table,
    tap_weight,
):
    width, length = transmission.shape[2:]
    count = volume.shape[1]
    scans, columns, tiles = (lax.axis_size(axis) for axis in ("scan", "angle", "tile"))
    rounds = [[(i, i + 1) for i in range(first, scans - 1, 2)] for first in (0, 1)]
    both = [pairs + [(target, source) for source, target in pairs] for pairs in rounds]
    swap = [(0, 1), (1, 0)]

    def exchange(block, number):
        return lax.ppermute(block, "scan", both[number])

    def across(block):
        return lax.ppermute(block, "tile", swap)

    edges = 2 * 2 * count
    (plane,) = call(
        pack_kernel,
        [(2 * width + -(-edges // SUBLANES) * SUBLANES, length)],
        (),
        [(edges, SUBLANES, length)],
        10**5,
        staged=(transmission, volume),
        copies=2 + edges,
    )
    plane_a = exchange(plane, 0)
    plane_b = exchange(plane, 1)
    tables = [jnp.asarray(table) for table in dft_tables(probe_wave.shape[1])]
    scalars = (slot_first_rows, slot_first_columns, patch_counts)
    slots = slot_first_rows.shape[1]
    side = probe_wave.shape[1]
    probes, density, rays, _, *held = call(
        prepare_kernel,
        [(slots, 2, side, side), (1, 3 * width, length), (columns * tiles, SUBLANES, length)],
        (*scalars, shift_table.T, tap_weight.T),
        [],
        10**7,
        5,
        (probe_wave, intensities, volume, *tables),
    )
    volume_here = held[1]
    turns = [[(i, (i - turn) % columns) for i in range(columns)] for turn in range(columns)]
    by_row = [rays]
    for turn in range(1, columns):
        by_row.append(lax.ppermute(rays, "angle", turns[turn]))
    by_row = [block for table in by_row for block in (table, across(table))]
    own, rim_a, rim_b, row_a, row_b = call(
        patch_kernel,
        [(3, width, length)]
        + [(3 * width, length)] * 2
        + [(2, width + SUBLANES, length)] * 2,
        (*scalars, probes, density, plane, *held, plane_a, plane_b),
        [(2, 3 * width, length), (3, 3 * width, length)],
        10**9,
        3,
    )
    rim_a = exchange(rim_a, 0)
    rim_b = exchange(rim_b, 1)
    bridge = [(i * tiles + 1, (i + 1) * tiles) for i in range(columns - 1)]
    bridge += [(target, source) for source, target in bridge]
    row_b = lax.ppermute(row_b, ("angle", "tile"), bridge)
    row_a = across(row_a)
    high, low = call(
        operator_kernel,
        [(columns, (2 + 2 * count) * width, 3 * width)] * 2,
        tuple(by_row),
        [],
        10**8,
        kind=jnp.bfloat16,
    )
    new_transmission, residual = call(
        fold_kernel,
        [transmission.shape, (2 * width, length)],
        (own, rim_a, rim_b, projected, scaled_dual),
        [],
        10**6,
    )
    by_column = [residual]
    for turn in range(1, columns):
        by_column.append(lax.ppermute(residual, "angle", turns[turn]))
    (base,) = call(
        variation_kernel,
        [volume.shape],
        (volume_here, plane_a, plane_b, row_a, row_b),
        [(count + 2, width + 16, length), (width + 16, length)],
        10**7,
    )
    lower = range(columns // 2)
    route = []
    for scan in range(scans):
        for column in range(columns):
            target = scan + 1 if column in lower else scan - 1
            if 0 <= target < scans:
                route.append((scan * columns + column, target * columns + column))
    beside = lax.ppermute(base, ("scan", "angle"), route)
    here = jnp.stack(by_column)
    side_a = exchange(here, 0)
    side_b = exchange(here, 1)
    block = (columns, 2, width, length)
    keep, send = call(
        spread_kernel,
        [block, block],
        (shift_table.T, tap_weight.T, base, beside),
        [(count, 2, length // LANES, 2 * width, LANES)],
        10**7,
        2,
    )
    received = across(send)
    spread = keep[0] + received[0]
    for turn in range(1, columns):
        route = [(i, (i + turn) % columns) for i in range(columns)]
        spread = spread + lax.ppermute(keep[turn] + received[turn], "angle", route)
    keep, own, send = call(
        apply_kernel,
        [(2, width, length), volume.shape, ((2 + 2 * count) * width, length)],
        (here, side_a, side_b, high, low),
        [(columns, 2, 3 * width, length)],
        10**9,
    )
    received = across(send)
    new_dual, new_volume, new_projected = call(
        finish_kernel,
        [transmission.shape, volume.shape, transmission.shape],
        (keep, own, received, base, spread, new_transmission, scaled_dual),
        [],
        10**6,
    )
    return (new_transmission, new_dual, new_volume, new_projected)


def solution(mesh):
    plane = P(("groups", "angle", "tile"), None, "scan", None)
    cells = P("groups", ("angle", "tile"), "scan", None)
    slots = P(("groups", "angle", "tile"), "scan")
    return jax.shard_map(
        body,
        mesh=mesh,
        in_specs=(
            plane,
            plane,
            plane,
            cells,
            P(("groups", "angle", "tile"), "scan", None, None),
            P("groups", None, None),
            slots,
            slots,
            slots,
            P(None, ("angle", "tile")),
            P(None, ("angle", "tile")),
        ),
        out_specs=(plane, plane, cells, plane),
        check_vma=False,
    )
```

```python
import math

import jax
import jax.numpy as jnp
import numpy as np
from jax import lax
from jax.experimental import pallas as pl
from jax.experimental.pallas import tpu as pltpu
from jax.sharding import PartitionSpec as P


penalty = 4.0
amplitude_step = 0.25
tv_weight = 1.0
smoothing = 0.05
step_size = 0.008

VMEM = pl.BlockSpec(memory_space=pltpu.VMEM)
SMEM = pl.BlockSpec(memory_space=pltpu.SMEM)
HBM = pl.BlockSpec(memory_space=pltpu.MemorySpace.HBM)
LANES = 128
SUBLANES = 8
SPARE_BYTES = 8 << 20


def split(values):
    high = values.astype(jnp.bfloat16)
    return (high, (values - high.astype(jnp.float32)).astype(jnp.bfloat16))


def product(left, right):
    total = jnp.dot(left[0], right[0], preferred_element_type=jnp.float32)
    total += jnp.dot(left[0], right[1], preferred_element_type=jnp.float32)
    return total + jnp.dot(left[1], right[0], preferred_element_type=jnp.float32)


def dft_tables(length):
    grid_ids = np.arange(length)
    radians = (grid_ids[:, None] * grid_ids[None, :] % length) * (2.0 * math.pi / length)
    cosine = np.cos(radians) / math.sqrt(length)
    sine = np.sin(radians) / math.sqrt(length)
    forward = np.block([[cosine, sine], [-sine, cosine]])
    tables = []
    for table in (forward, forward.T):
        high = table.astype(jnp.bfloat16)
        tables += [high, (table - high.astype(np.float64)).astype(jnp.bfloat16)]
    return tables


def tile_is_first():
    return lax.axis_index("tile") == 0


def scan_is_even():
    return lax.rem(lax.axis_index("scan"), 2) == 0


def pack_kernel(plane_ref, volume_ref, packed_ref, slabs, done):
    width = plane_ref.shape[2]
    count = volume_ref.shape[1]
    copies = [
        (plane_ref.at[0, channel], packed_ref.at[channel * width : (channel + 1) * width])
        for channel in range(2)
    ]
    for channel in range(2):
        for row in range(count):
            for side, at in enumerate((0, width - SUBLANES)):
                source = volume_ref.at[channel, row, at : at + SUBLANES]
                copies.append((source, slabs.at[(channel * count + row) * 2 + side]))
    copies = [
        pltpu.make_async_copy(source, target, done.at[number])
        for number, (source, target) in enumerate(copies)
    ]
    for copy in copies:
        copy.start()
    for copy in copies[2:]:
        copy.wait()
    for edge in range(slabs.shape[0]):
        take = 0 if edge % 2 == 0 else SUBLANES - 1
        packed_ref[2 * width + edge : 2 * width + edge + 1] = slabs[edge, take : take + 1]
    for copy in copies[:2]:
        copy.wait()


def edges_of(plane_a_ref, plane_b_ref, number, width):
    even = scan_is_even()
    at = 2 * width + 2 * number
    first_a, last_a = plane_a_ref[at : at + 1], plane_a_ref[at + 1 : at + 2]
    first_b, last_b = plane_b_ref[at : at + 1], plane_b_ref[at + 1 : at + 2]
    return (jnp.where(even, last_b, last_a), jnp.where(even, first_a, first_b))


def slot_masks(rows_ref, columns_ref, count_ref, slot, side):
    lanes = lax.broadcasted_iota(jnp.int32, (side, side), 1)
    sublanes = lax.broadcasted_iota(jnp.int32, (side, side), 0)
    near_lanes = lanes >= rows_ref[0, slot]
    near_columns = sublanes >= columns_ref[0, slot]
    return (near_lanes, near_columns, jnp.full((side, side), slot < count_ref[0, 0]))


def place(totals, part, term, masks, width):
    side = term.shape[0]
    near_lanes, near_columns, live = masks
    inner = live & near_columns
    outer = (live & jnp.logical_not(near_columns))[:width]
    for start, lane_mask in ((0, near_lanes), (side, jnp.logical_not(near_lanes))):
        at = slice(start, start + side)
        totals[part, :side, at] += jnp.where(inner & lane_mask, term, 0.0)
        totals[part, side:, at] += jnp.where(outer & lane_mask[:width], term[:width], 0.0)


def prepare_kernel(count_ref, *refs):
    held = (len(refs) - 13) // 2
    sources = refs[: held + 4]
    probes_ref, density_ref, slots_ref, rays_ref = refs[held + 4 : held + 8]
    targets, done = refs[held + 8 : -1], refs[-1]
    rows_ref, columns_ref, shift_ref, weight_ref = targets[held:]
    copies = [
        pltpu.make_async_copy(source, target, done.at[number])
        for number, (source, target) in enumerate(zip(sources, targets))
    ]
    for copy in copies:
        copy.start()
    probe_ref = targets[0]
    side = probe_ref.shape[1]
    slots = probes_ref.shape[0]
    width = density_ref.shape[1] - side
    density_ref[...] = jnp.zeros_like(density_ref)
    for copy in copies[:1] + copies[held:]:
        copy.wait()
    places = lax.broadcasted_iota(jnp.int32, slots_ref.shape[1:], 0)
    for slot in range(slots):
        live = jnp.where(slot < count_ref[0, 0], 1, 0)
        numbers = jnp.where(places == 0, rows_ref[0, slot], columns_ref[0, slot])
        slots_ref[slot] = jnp.where(places == 2, live, numbers)
        turn = lax.rem(rows_ref[0, slot], side)
        probe = [
            pltpu.roll(pltpu.roll(probe_ref[part], columns_ref[0, slot], 0), turn, 1)
            for part in range(2)
        ]
        for part in range(2):
            probes_ref[slot, part] = probe[part]
        masks = slot_masks(rows_ref, columns_ref, count_ref, slot, side)
        place(density_ref, 0, probe[0] * probe[0] + probe[1] * probe[1], masks, width)
    places = lax.broadcasted_iota(jnp.int32, rays_ref.shape, 0)
    lanes = lax.broadcasted_iota(jnp.int32, rays_ref.shape, 1)
    rays = jnp.zeros(rays_ref.shape, jnp.float32)
    for row in range(shift_ref.shape[0]):
        for angle in range(shift_ref.shape[1]):
            shift = shift_ref[row, angle].astype(jnp.float32)
            here = lanes == angle
            rays = jnp.where(here & (places == 2 * row), shift, rays)
            rays = jnp.where(here & (places == 2 * row + 1), weight_ref[row, angle], rays)
    rays_ref[...] = rays
    for copy in copies[1:held]:
        copy.wait()


def patch_kernel(
    probes_ref,
    density_ref,
    slots_ref,
    rays_ref,
    plane_ref,
    intensity_ref,
    volume_ref,
    forward_high_ref,
    forward_low_ref,
    inverse_high_ref,
    inverse_low_ref,
    plane_a_ref,
    plane_b_ref,
    own_ref,
    rim_a_ref,
    rim_b_ref,
    row_a_ref,
    row_b_ref,
    wide,
    totals,
):
    width = volume_ref.shape[2]
    slots, _, side, _ = probes_ref.shape
    even = scan_is_even()
    at_a = pl.multiple_of(jnp.where(even, 2 * width, 0), width)
    at_b = pl.multiple_of(jnp.where(even, 0, 2 * width), width)
    for part in range(2):
        at = slice(part * width, (part + 1) * width)
        wide[part, width : 2 * width] = plane_ref[at]
        wide[part, pl.ds(at_a, width)] = plane_a_ref[at]
        wide[part, pl.ds(at_b, width)] = plane_b_ref[at]
    forward = (forward_high_ref[...], forward_low_ref[...])
    inverse = (inverse_high_ref[...], inverse_low_ref[...])
    waves, masks = [], []
    lanes = lax.broadcasted_iota(jnp.int32, (side, side), 1)
    sublanes = lax.broadcasted_iota(jnp.int32, (side, side), 0)
    for slot in range(slots):
        probe = probes_ref[slot]
        row, column, live = (
            jnp.broadcast_to(slots_ref[slot, number : number + 1], (side, side))
            for number in range(3)
        )
        near_lanes, near_columns = lanes >= row, sublanes >= column
        masks.append((near_lanes, near_columns, live > 0))
        window = []
        for part in range(2):
            near = jnp.where(near_lanes, wide[part, :side, :side], wide[part, :side, side:])
            wrapped = jnp.where(
                near_lanes[:width], wide[part, side:, :side], wide[part, side:, side:]
            )
            wrapped = jnp.concatenate([wrapped, near[width:]], axis=0)
            window.append(jnp.where(near_columns, near, wrapped))
        wave_real = probe[0] * window[0] - probe[1] * window[1]
        wave_imaginary = probe[0] * window[1] + probe[1] * window[0]
        waves.append(jnp.concatenate([wave_real, wave_imaginary], axis=1))
    half = product(split(jnp.concatenate(waves, axis=0)), inverse)
    half = jnp.concatenate(
        [
            jnp.concatenate(
                [half[slot * side : (slot + 1) * side, part * side : (part + 1) * side] for slot in range(slots)],
                axis=1,
            )
            for part in range(2)
        ],
        axis=0,
    )
    far = product(forward, split(half))
    far_real, far_imaginary = far[:side], far[side:]
    intensity = jnp.concatenate(
        [intensity_ref[0, slot].astype(jnp.float32) for slot in range(slots)], axis=1
    )
    factor = 1.0 - amplitude_step * (
        far_real * far_real + far_imaginary * far_imaginary - intensity
    )
    corrected = jnp.concatenate([far_real * factor, far_imaginary * factor], axis=0)
    half = product(inverse, split(corrected))
    half = jnp.concatenate(
        [
            jnp.concatenate(
                [half[part * side : (part + 1) * side, slot * side : (slot + 1) * side] for part in range(2)],
                axis=1,
            )
            for slot in range(slots)
        ],
        axis=0,
    )
    near = product(split(half), forward)
    totals[:2] = jnp.zeros_like(totals[:2])
    totals[2:] = density_ref[...]
    for slot in range(slots):
        probe = probes_ref[slot]
        near_real = near[slot * side : (slot + 1) * side, :side]
        near_imaginary = near[slot * side : (slot + 1) * side, side:]
        place(totals, 0, probe[0] * near_real + probe[1] * near_imaginary, masks[slot], width)
        place(totals, 1, probe[0] * near_imaginary - probe[1] * near_real, masks[slot], width)
    own_ref[...] = totals[:, width : 2 * width]
    for rim_ref, at in ((rim_a_ref, at_a), (rim_b_ref, at_b)):
        for part in range(totals.shape[0]):
            rim_ref[part * width : (part + 1) * width] = totals[part, pl.ds(at, width)]
    first_tile = tile_is_first()
    count = volume_ref.shape[1]
    for channel in range(2):
        rows = []
        for row in (0, count - 1):
            before, after = edges_of(plane_a_ref, plane_b_ref, channel * count + row, width)
            rows.append((volume_ref[channel, row], jnp.concatenate([before, after], axis=0)))
        for low, row_ref in ((jnp.logical_not(first_tile), row_a_ref), (first_tile, row_b_ref)):
            row_ref[channel, :width] = jnp.where(low, rows[0][0], rows[1][0])
            row_ref[channel, width : width + 2] = jnp.where(low, rows[0][1], rows[1][1])
            row_ref[channel, width + SUBLANES :] = rays_ref[...]


def fold_kernel(
    own_ref, rim_a_ref, rim_b_ref, projected_ref, dual_ref, rays_ref, row_ref, object_ref, residual_ref
):
    width = own_ref.shape[1]
    sums = [
        own_ref[part]
        + rim_a_ref[part * width : (part + 1) * width]
        + rim_b_ref[part * width : (part + 1) * width]
        for part in range(3)
    ]
    for part in range(2):
        target = projected_ref[0, part]
        dual = dual_ref[0, part]
        updated = (sums[part] + penalty * (target - dual)) / (sums[2] + penalty)
        object_ref[0, part] = updated
        residual_ref[part * width : (part + 1) * width] = target - updated - dual
    residual_ref[2 * width : 2 * width + SUBLANES] = rays_ref[...]
    residual_ref[2 * width + SUBLANES :] = row_ref[0, width + SUBLANES :]


def variation_kernel(
    volume_ref, plane_a_ref, plane_b_ref, row_a_ref, row_b_ref, base_ref, padded, norms
):
    width = volume_ref.shape[2]
    length = volume_ref.shape[3]
    count = volume_ref.shape[1]
    margin = 8
    first_tile = tile_is_first()
    lanes = lax.broadcasted_iota(jnp.int32, (width, length), 1)
    first_lane = lanes == 0
    last_lane = lanes == length - 1
    for channel in range(2):
        for row in range(count):
            before, after = edges_of(plane_a_ref, plane_b_ref, channel * count + row, width)
            padded[row + 1, margin : margin + width] = volume_ref[channel, row]
            padded[row + 1, margin - 1 : margin] = before
            padded[row + 1, margin + width : margin + width + 1] = after
        row_a, row_b = row_a_ref[channel], row_b_ref[channel]
        for row, beside in (
            (0, jnp.where(first_tile, row_b, row_a)),
            (count + 1, jnp.where(first_tile, row_a, row_b)),
        ):
            padded[row, margin : margin + width] = beside[:width]
            padded[row, margin - 1 : margin] = beside[width : width + 1]
            padded[row, margin + width : margin + width + 1] = beside[width + 1 : width + 2]
        previous_y = None
        for row in range(count + 1):
            here = padded[row, margin : margin + width]
            along_y = padded[row + 1, margin : margin + width] - here
            along_x = padded[row, margin + 1 : margin + width + 1] - here
            along_z = jnp.where(last_lane, 0.0, pltpu.roll(here, length - 1, 1)) - here
            inverse = lax.rsqrt(
                along_y * along_y + along_x * along_x + along_z * along_z + smoothing * smoothing
            )
            norm_y = along_y * inverse
            if row > 0:
                norm_x = along_x * inverse
                norm_z = along_z * inverse
                corner = padded[row, margin - 1 : margin]
                corner_y = padded[row + 1, margin - 1 : margin] - corner
                corner_x = here[:1] - corner
                corner_z = (
                    jnp.where(last_lane[:1], 0.0, pltpu.roll(corner, length - 1, 1)) - corner
                )
                corner_norm = corner_x * lax.rsqrt(
                    corner_y * corner_y
                    + corner_x * corner_x
                    + corner_z * corner_z
                    + smoothing * smoothing
                )
                norms[margin : margin + width] = norm_x
                norms[margin - 1 : margin] = corner_norm
                behind_x = norms[margin - 1 : margin + width - 1]
                ahead = here * lax.rsqrt(here * here + smoothing * smoothing)
                behind_z = jnp.where(first_lane, ahead, pltpu.roll(norm_z, 1, 1))
                divergence = (
                    norm_y - previous_y + (norm_x - behind_x) + (norm_z - behind_z)
                )
                base_ref[channel, row - 1] = here + (step_size * tv_weight) * divergence
            previous_y = norm_y


def spread_kernel(shift_ref, weight_ref, base_ref, beside_ref, keep_ref, send_ref, padded):
    width = base_ref.shape[2]
    count = base_ref.shape[1]
    columns, tiles = keep_ref.shape[0], lax.axis_size("tile")
    me, tile, scan = lax.axis_index("angle"), lax.axis_index("tile"), lax.axis_index("scan")
    upper = me >= columns // 2
    chunks = [slice(at, at + LANES) for at in range(0, base_ref.shape[3], LANES)]
    exists = jnp.where(upper, scan < lax.axis_size("scan") - 1, scan > 0).astype(jnp.float32)
    own_at = pl.multiple_of(jnp.where(upper, 0, width), width)
    beside_at = pl.multiple_of(jnp.where(upper, width, 0), width)
    for row in range(count):
        for channel in range(2):
            for chunk, at in enumerate(chunks):
                padded[row, channel, chunk, pl.ds(own_at, width)] = base_ref[channel, row, :, at]
                padded[row, channel, chunk, pl.ds(beside_at, width)] = (
                    beside_ref[channel, row, :, at] * exists
                )
    for turn in range(columns):
        for flip, out_ref in ((0, keep_ref), (1, send_ref)):
            angle = lax.rem(me + turn, columns) * tiles + (tile if flip == 0 else 1 - tile)
            for channel in range(2):
                for chunk, at in enumerate(chunks):
                    total = jnp.zeros((width, LANES), jnp.float32)
                    for row in range(count):
                        start = jnp.where(upper, 0, width) + shift_ref[row, angle]
                        fraction = weight_ref[row, angle]
                        total += (1.0 - fraction) * padded[row, channel, chunk, pl.ds(start, width)]
                        total += fraction * padded[row, channel, chunk, pl.ds(start + 1, width)]
                    out_ref[turn, channel, :, at] = total


def operator_kernel(*refs):
    packed_refs, (high_ref, low_ref) = refs[:-2], refs[-2:]
    tiles = lax.axis_size("tile")
    columns = len(packed_refs)
    rows_out, reach = high_ref.shape[1:]
    width = reach // 3
    count = rows_out // (2 * width) - 1
    me, tile, scan = lax.axis_index("angle"), lax.axis_index("tile"), lax.axis_index("scan")

    def taps(shape, first, table, row, step):
        lanes = lax.broadcasted_iota(jnp.int32, shape, 1)
        sublanes = lax.broadcasted_iota(jnp.int32, shape, 0)
        offset = (lanes - sublanes).astype(jnp.float32) - first
        shift = step * table[2 * row : 2 * row + 1]
        fraction = table[2 * row + 1 : 2 * row + 2]
        return jnp.where(offset == shift, 1.0 - fraction, 0.0) + jnp.where(
            offset == shift + step, fraction, 0.0
        )

    def angle_of(turn, flip):
        return lax.rem(me + turn, columns) * tiles + (tile if flip == 0 else 1 - tile)

    def table_of(turn, flip, angle):
        at = 2 * width + SUBLANES * flip
        tile_of = packed_refs[turn][at : at + SUBLANES]
        lanes = lax.broadcasted_iota(jnp.int32, tile_of.shape, 1)
        return jnp.sum(jnp.where(lanes == angle, tile_of, 0.0), axis=1, keepdims=True)

    cells = lax.broadcasted_iota(jnp.int32, (width, 2 * width), 1)
    forward = []
    backward = [[] for _ in range(columns)]
    for turn in range(columns):
        upper = lax.rem(me + turn, columns) >= columns // 2
        base_at = jnp.where(upper, 0, width)
        first_cell = jnp.where(upper, 0, jnp.where(scan > 0, 0, width))
        end_cell = jnp.where(upper & (scan == lax.axis_size("scan") - 1), width, 2 * width)
        inside = (cells >= first_cell) & (cells < end_cell)
        for flip in range(tiles):
            for row in range(count):
                parts = []
                for own in range(tiles):
                    table = table_of(turn, flip, angle_of(0, own))
                    part = taps((width, 2 * width), base_at.astype(jnp.float32), table, row, 1.0)
                    parts.append(jnp.where(inside, part, 0.0))
                forward.append(jnp.concatenate(parts, axis=0))
                for source in range(columns):
                    table = table_of(turn, flip, angle_of(source, 0))
                    first = (width - base_at).astype(jnp.float32)
                    backward[source].append(taps((2 * width, reach), first, table, row, -1.0))
    left = split(jnp.concatenate(forward, axis=1))
    for source in range(columns):
        both = product(left, split(jnp.concatenate(backward[source], axis=0)))
        blocks = [both]
        for flip in range(tiles):
            for row in range(count):
                table = table_of(0, flip, angle_of(source, 0))
                blocks.append(taps((width, reach), float(width), table, row, -1.0))
        high_ref[source], low_ref[source] = split(jnp.concatenate(blocks, axis=0))


def apply_kernel(here_ref, side_a_ref, side_b_ref, high_ref, low_ref, keep_ref, own_ref, send_ref, wide):
    width = keep_ref.shape[1]
    columns = here_ref.shape[0]
    count = own_ref.shape[1]
    even = scan_is_even()
    at_a = pl.multiple_of(jnp.where(even, 2 * width, 0), width)
    at_b = pl.multiple_of(jnp.where(even, 0, 2 * width), width)
    for source in range(columns):
        for channel in range(2):
            at = slice(channel * width, (channel + 1) * width)
            wide[source, channel, width : 2 * width] = here_ref[source, at]
            wide[source, channel, pl.ds(at_a, width)] = side_a_ref[source, at]
            wide[source, channel, pl.ds(at_b, width)] = side_b_ref[source, at]
    for channel in range(2):
        total = 0.0
        for source in range(columns):
            total += product((high_ref[source], low_ref[source]), split(wide[source, channel]))
        keep_ref[channel] = total[:width]
        send_ref[channel * width : (channel + 1) * width] = total[width : 2 * width]
        for row in range(count):
            at = (2 + row) * width
            own_ref[channel, row] = total[at : at + width]
            target = (2 + channel * count + row) * width
            send_ref[target : target + width] = total[at + count * width : at + (count + 1) * width]


def volume_kernel(own_ref, received_ref, base_ref, volume_ref):
    count, width = own_ref.shape[1:3]
    for channel in range(2):
        for row in range(count):
            at = (2 + channel * count + row) * width
            descent = own_ref[channel, row] + received_ref[at : at + width]
            volume_ref[channel, row] = base_ref[channel, row] - step_size * descent


def finish_kernel(*refs):
    keep_ref, received_ref, object_ref, dual_ref = refs[:4]
    spreads, (dual_out_ref, projected_ref) = refs[4:-2], refs[-2:]
    width = keep_ref.shape[1]
    for channel in range(2):
        received = received_ref[channel * width : (channel + 1) * width]
        projection = -step_size * (keep_ref[channel] + received)
        for spread_ref in spreads:
            projection = projection + spread_ref[channel]
        projected_ref[0, channel] = projection
        dual_out_ref[0, channel] = dual_ref[0, channel] + object_ref[0, channel] - projection


def call(
    kernel, shapes, operands, scratch, flops, scalars=0, staged=(), numbers=(), copies=0, kind=jnp.float32, kinds={}
):
    held = sum(operand.nbytes for operand in operands[scalars:] + staged)
    held += 4 * sum(math.prod(shape) for shape in shapes)
    own = 4 * sum(math.prod(shape) for shape in scratch)
    outputs = [
        jax.ShapeDtypeStruct(shape, kinds.get(number, kind)) for number, shape in enumerate(shapes)
    ]
    scratch_shapes = [pltpu.VMEM(shape, jnp.float32) for shape in scratch]
    if staged and not copies:
        outputs += [jax.ShapeDtypeStruct(array.shape, array.dtype) for array in staged]
        copies = len(staged) + len(numbers)
        scratch_shapes += [pltpu.SMEM(array.shape, array.dtype) for array in numbers]
    staged += numbers
    if copies:
        scratch_shapes.append(pltpu.SemaphoreType.DMA((copies,)))
    in_specs = [SMEM] * scalars + [VMEM] * (len(operands) - scalars) + [HBM] * len(staged)
    return pl.pallas_call(
        kernel,
        out_shape=outputs,
        in_specs=in_specs,
        out_specs=[VMEM] * len(outputs),
        scratch_shapes=scratch_shapes,
        compiler_params=pltpu.CompilerParams(vmem_limit_bytes=held + own + SPARE_BYTES),
        cost_estimate=pl.CostEstimate(flops=flops, bytes_accessed=held, transcendentals=0),
    )(*operands, *(pltpu.with_memory_space_constraint(array, pltpu.HBM) for array in staged))


def body(
    transmission,
    scaled_dual,
    projected,
    volume,
    intensities,
    probe_wave,
    slot_first_rows,
    slot_first_columns,
    patch_counts,
    shift_table,
    tap_weight,
):
    width, length = transmission.shape[2:]
    count = volume.shape[1]
    scans, columns, tiles = (lax.axis_size(axis) for axis in ("scan", "angle", "tile"))
    rounds = [[(i, i + 1) for i in range(first, scans - 1, 2)] for first in (0, 1)]
    both = [pairs + [(target, source) for source, target in pairs] for pairs in rounds]
    swap = [(0, 1), (1, 0)]

    def exchange(block, number):
        return lax.ppermute(block, "scan", both[number])

    def across(block):
        return lax.ppermute(block, "tile", swap)

    edges = 2 * 2 * count
    (plane,) = call(
        pack_kernel,
        [(2 * width + -(-edges // SUBLANES) * SUBLANES, length)],
        (),
        [(edges, SUBLANES, length)],
        10**5,
        staged=(transmission, volume),
        copies=2 + edges,
    )
    plane_a = exchange(plane, 0)
    plane_b = exchange(plane, 1)
    tables = [jnp.asarray(table) for table in dft_tables(probe_wave.shape[1])]
    slots = slot_first_rows.shape[1]
    side = probe_wave.shape[1]
    probes, density, slot_numbers, rays, _, *held = call(
        prepare_kernel,
        [
            (slots, 2, side, side),
            (1, 3 * width, length),
            (slots, SUBLANES, side),
            (SUBLANES, length),
        ],
        (patch_counts,),
        [],
        10**7,
        1,
        (probe_wave, intensities, volume, *tables),
        (slot_first_rows, slot_first_columns, shift_table.T, tap_weight.T),
        kinds={2: jnp.int32},
    )
    volume_here = held[1]
    turns = [[(i, (i - turn) % columns) for i in range(columns)] for turn in range(columns)]
    own, rim_a, rim_b, row_a, row_b = call(
        patch_kernel,
        [(3, width, length)]
        + [(3 * width, length)] * 2
        + [(2, width + 2 * SUBLANES, length)] * 2,
        (probes, density, slot_numbers, rays, plane, *held, plane_a, plane_b),
        [(2, 3 * width, length), (3, 3 * width, length)],
        10**9,
    )
    rim_a = exchange(rim_a, 0)
    rim_b = exchange(rim_b, 1)
    bridge = [(i * tiles + 1, (i + 1) * tiles) for i in range(columns - 1)]
    bridge += [(target, source) for source, target in bridge]
    row_b = lax.ppermute(row_b, ("angle", "tile"), bridge)
    row_a = across(row_a)
    new_transmission, residual = call(
        fold_kernel,
        [transmission.shape, (2 * width + 2 * SUBLANES, length)],
        (own, rim_a, rim_b, projected, scaled_dual, rays, row_a),
        [],
        10**6,
    )
    by_column = [residual]
    for turn in range(1, columns):
        by_column.append(lax.ppermute(residual, "angle", turns[turn]))
    (base,) = call(
        variation_kernel,
        [volume.shape],
        (volume_here, plane_a, plane_b, row_a, row_b),
        [(count + 2, width + 16, length), (width + 16, length)],
        10**7,
    )
    lower = range(columns // 2)
    route = []
    for scan in range(scans):
        for column in range(columns):
            target = scan + 1 if column in lower else scan - 1
            if 0 <= target < scans:
                route.append((scan * columns + column, target * columns + column))
    beside = lax.ppermute(base, ("scan", "angle"), route)
    here = jnp.stack(by_column)
    side_a = exchange(here, 0)
    side_b = exchange(here, 1)
    high, low = call(
        operator_kernel,
        [(columns, (2 + 2 * count) * width, 3 * width)] * 2,
        tuple(by_column),
        [],
        10**8,
        kind=jnp.bfloat16,
    )
    block = (columns, 2, width, length)
    keep, send = call(
        spread_kernel,
        [block, block],
        (shift_table.T, tap_weight.T, base, beside),
        [(count, 2, length // LANES, 2 * width, LANES)],
        10**7,
        2,
    )
    received = across(send)
    spreads = [keep[0], received[0]]
    for turn in range(1, columns):
        route = [(i, (i + turn) % columns) for i in range(columns)]
        spreads.append(lax.ppermute(keep[turn] + received[turn], "angle", route))
    keep, own, send = call(
        apply_kernel,
        [(2, width, length), volume.shape, ((2 + 2 * count) * width, length)],
        (here, side_a, side_b, high, low),
        [(columns, 2, 3 * width, length)],
        10**9,
    )
    received = across(send)
    (new_volume,) = call(volume_kernel, [volume.shape], (own, received, base), [], 10**6)
    new_dual, new_projected = call(
        finish_kernel,
        [transmission.shape] * 2,
        (keep, received, new_transmission, scaled_dual, *spreads),
        [],
        10**6,
    )
    return (new_transmission, new_dual, new_volume, new_projected)


def solution(mesh):
    plane = P(("groups", "angle", "tile"), None, "scan", None)
    cells = P("groups", ("angle", "tile"), "scan", None)
    slots = P(("groups", "angle", "tile"), "scan")
    return jax.shard_map(
        body,
        mesh=mesh,
        in_specs=(
            plane,
            plane,
            plane,
            cells,
            P(("groups", "angle", "tile"), "scan", None, None),
            P("groups", None, None),
            slots,
            slots,
            slots,
            P(None, ("angle", "tile")),
            P(None, ("angle", "tile")),
        ),
        out_specs=(plane, plane, cells, plane),
        check_vma=False,
    )
```

```python
import math

import jax
import jax.numpy as jnp
import numpy as np
from jax import lax
from jax.experimental import pallas as pl
from jax.experimental.pallas import tpu as pltpu
from jax.sharding import PartitionSpec as P


penalty = 4.0
amplitude_step = 0.25
tv_weight = 1.0
smoothing = 0.05
step_size = 0.008

VMEM = pl.BlockSpec(memory_space=pltpu.VMEM)
SMEM = pl.BlockSpec(memory_space=pltpu.SMEM)
HBM = pl.BlockSpec(memory_space=pltpu.MemorySpace.HBM)
LANES = 128
SUBLANES = 8
SPARE_BYTES = 8 << 20


def split(values):
    high = values.astype(jnp.bfloat16)
    return (high, (values - high.astype(jnp.float32)).astype(jnp.bfloat16))


def product(left, right):
    total = jnp.dot(left[0], right[0], preferred_element_type=jnp.float32)
    total += jnp.dot(left[0], right[1], preferred_element_type=jnp.float32)
    return total + jnp.dot(left[1], right[0], preferred_element_type=jnp.float32)


def dft_tables(length):
    grid_ids = np.arange(length)
    radians = (grid_ids[:, None] * grid_ids[None, :] % length) * (2.0 * math.pi / length)
    cosine = np.cos(radians) / math.sqrt(length)
    sine = np.sin(radians) / math.sqrt(length)
    forward = np.block([[cosine, sine], [-sine, cosine]])
    tables = []
    for table in (forward, forward.T):
        high = table.astype(jnp.bfloat16)
        tables += [high, (table - high.astype(np.float64)).astype(jnp.bfloat16)]
    return tables


def tile_is_first():
    return lax.axis_index("tile") == 0


def scan_is_even():
    return lax.rem(lax.axis_index("scan"), 2) == 0


def pack_kernel(plane_ref, volume_ref, packed_ref, slabs, done):
    width = plane_ref.shape[2]
    count = volume_ref.shape[1]
    copies = [
        (plane_ref.at[0, channel], packed_ref.at[channel * width : (channel + 1) * width])
        for channel in range(2)
    ]
    for channel in range(2):
        for row in range(count):
            for side, at in enumerate((0, width - SUBLANES)):
                source = volume_ref.at[channel, row, at : at + SUBLANES]
                copies.append((source, slabs.at[(channel * count + row) * 2 + side]))
    copies = [
        pltpu.make_async_copy(source, target, done.at[number])
        for number, (source, target) in enumerate(copies)
    ]
    for copy in copies:
        copy.start()
    for copy in copies[2:]:
        copy.wait()
    for edge in range(slabs.shape[0]):
        take = 0 if edge % 2 == 0 else SUBLANES - 1
        packed_ref[2 * width + edge : 2 * width + edge + 1] = slabs[edge, take : take + 1]
    for copy in copies[:2]:
        copy.wait()


def edges_of(plane_a_ref, plane_b_ref, number, width):
    even = scan_is_even()
    at = 2 * width + 2 * number
    first_a, last_a = plane_a_ref[at : at + 1], plane_a_ref[at + 1 : at + 2]
    first_b, last_b = plane_b_ref[at : at + 1], plane_b_ref[at + 1 : at + 2]
    return (jnp.where(even, last_b, last_a), jnp.where(even, first_a, first_b))


def slot_masks(rows_ref, columns_ref, count_ref, slot, side):
    lanes = lax.broadcasted_iota(jnp.int32, (side, side), 1)
    sublanes = lax.broadcasted_iota(jnp.int32, (side, side), 0)
    near_lanes = lanes >= rows_ref[0, slot]
    near_columns = sublanes >= columns_ref[0, slot]
    return (near_lanes, near_columns, jnp.full((side, side), slot < count_ref[0, 0]))


def place(totals, part, term, masks, width):
    side = term.shape[0]
    near_lanes, near_columns, live = masks
    inner = live & near_columns
    outer = (live & jnp.logical_not(near_columns))[:width]
    for start, lane_mask in ((0, near_lanes), (side, jnp.logical_not(near_lanes))):
        at = slice(start, start + side)
        totals[part, :side, at] += jnp.where(inner & lane_mask, term, 0.0)
        totals[part, side:, at] += jnp.where(outer & lane_mask[:width], term[:width], 0.0)


def prepare_kernel(count_ref, *refs):
    held = (len(refs) - 13) // 2
    sources = refs[: held + 4]
    probes_ref, density_ref, slots_ref, rays_ref = refs[held + 4 : held + 8]
    targets, done = refs[held + 8 : -1], refs[-1]
    rows_ref, columns_ref, shift_ref, weight_ref = targets[held:]
    copies = [
        pltpu.make_async_copy(source, target, done.at[number])
        for number, (source, target) in enumerate(zip(sources, targets))
    ]
    for copy in copies:
        copy.start()
    probe_ref = targets[0]
    side = probe_ref.shape[1]
    slots = probes_ref.shape[0]
    width = density_ref.shape[1] - side
    density_ref[...] = jnp.zeros_like(density_ref)
    for copy in copies[:1] + copies[held:]:
        copy.wait()
    places = lax.broadcasted_iota(jnp.int32, slots_ref.shape[1:], 0)
    for slot in range(slots):
        live = jnp.where(slot < count_ref[0, 0], 1, 0)
        numbers = jnp.where(places == 0, rows_ref[0, slot], columns_ref[0, slot])
        slots_ref[slot] = jnp.where(places == 2, live, numbers)
        turn = lax.rem(rows_ref[0, slot], side)
        probe = [
            pltpu.roll(pltpu.roll(probe_ref[part], columns_ref[0, slot], 0), turn, 1)
            for part in range(2)
        ]
        for part in range(2):
            probes_ref[slot, part] = probe[part]
        masks = slot_masks(rows_ref, columns_ref, count_ref, slot, side)
        place(density_ref, 0, probe[0] * probe[0] + probe[1] * probe[1], masks, width)
    places = lax.broadcasted_iota(jnp.int32, rays_ref.shape, 0)
    lanes = lax.broadcasted_iota(jnp.int32, rays_ref.shape, 1)
    rays = jnp.zeros(rays_ref.shape, jnp.float32)
    for row in range(shift_ref.shape[0]):
        for angle in range(shift_ref.shape[1]):
            shift = shift_ref[row, angle].astype(jnp.float32)
            here = lanes == angle
            rays = jnp.where(here & (places == 2 * row), shift, rays)
            rays = jnp.where(here & (places == 2 * row + 1), weight_ref[row, angle], rays)
    rays_ref[...] = rays
    for copy in copies[1:held]:
        copy.wait()


def patch_kernel(
    probes_ref,
    density_ref,
    slots_ref,
    rays_ref,
    plane_ref,
    intensity_ref,
    volume_ref,
    forward_high_ref,
    forward_low_ref,
    inverse_high_ref,
    inverse_low_ref,
    plane_a_ref,
    plane_b_ref,
    own_ref,
    rim_a_ref,
    rim_b_ref,
    row_a_ref,
    row_b_ref,
    wide,
    totals,
):
    width = volume_ref.shape[2]
    slots, _, side, _ = probes_ref.shape
    even = scan_is_even()
    at_a = pl.multiple_of(jnp.where(even, 2 * width, 0), width)
    at_b = pl.multiple_of(jnp.where(even, 0, 2 * width), width)
    for part in range(2):
        at = slice(part * width, (part + 1) * width)
        wide[part, width : 2 * width] = plane_ref[at]
        wide[part, pl.ds(at_a, width)] = plane_a_ref[at]
        wide[part, pl.ds(at_b, width)] = plane_b_ref[at]
    forward = (forward_high_ref[...], forward_low_ref[...])
    inverse = (inverse_high_ref[...], inverse_low_ref[...])
    waves, masks = [], []
    lanes = lax.broadcasted_iota(jnp.int32, (side, side), 1)
    sublanes = lax.broadcasted_iota(jnp.int32, (side, side), 0)
    for slot in range(slots):
        probe = probes_ref[slot]
        row, column, live = (
            jnp.broadcast_to(slots_ref[slot, number : number + 1], (side, side))
            for number in range(3)
        )
        near_lanes, near_columns = lanes >= row, sublanes >= column
        masks.append((near_lanes, near_columns, live > 0))
        window = []
        for part in range(2):
            near = jnp.where(near_lanes, wide[part, :side, :side], wide[part, :side, side:])
            wrapped = jnp.where(
                near_lanes[:width], wide[part, side:, :side], wide[part, side:, side:]
            )
            wrapped = jnp.concatenate([wrapped, near[width:]], axis=0)
            window.append(jnp.where(near_columns, near, wrapped))
        wave_real = probe[0] * window[0] - probe[1] * window[1]
        wave_imaginary = probe[0] * window[1] + probe[1] * window[0]
        waves.append(jnp.concatenate([wave_real, wave_imaginary], axis=1))
    half = product(split(jnp.concatenate(waves, axis=0)), inverse)
    half = jnp.concatenate(
        [
            jnp.concatenate(
                [half[slot * side : (slot + 1) * side, part * side : (part + 1) * side] for slot in range(slots)],
                axis=1,
            )
            for part in range(2)
        ],
        axis=0,
    )
    far = product(forward, split(half))
    far_real, far_imaginary = far[:side], far[side:]
    intensity = jnp.concatenate(
        [intensity_ref[0, slot].astype(jnp.float32) for slot in range(slots)], axis=1
    )
    factor = 1.0 - amplitude_step * (
        far_real * far_real + far_imaginary * far_imaginary - intensity
    )
    corrected = jnp.concatenate([far_real * factor, far_imaginary * factor], axis=0)
    half = product(inverse, split(corrected))
    half = jnp.concatenate(
        [
            jnp.concatenate(
                [half[part * side : (part + 1) * side, slot * side : (slot + 1) * side] for part in range(2)],
                axis=1,
            )
            for slot in range(slots)
        ],
        axis=0,
    )
    near = product(split(half), forward)
    totals[:2] = jnp.zeros_like(totals[:2])
    totals[2:] = density_ref[...]
    for slot in range(slots):
        probe = probes_ref[slot]
        near_real = near[slot * side : (slot + 1) * side, :side]
        near_imaginary = near[slot * side : (slot + 1) * side, side:]
        place(totals, 0, probe[0] * near_real + probe[1] * near_imaginary, masks[slot], width)
        place(totals, 1, probe[0] * near_imaginary - probe[1] * near_real, masks[slot], width)
    own_ref[...] = totals[:, width : 2 * width]
    for rim_ref, at in ((rim_a_ref, at_a), (rim_b_ref, at_b)):
        for part in range(totals.shape[0]):
            rim_ref[part * width : (part + 1) * width] = totals[part, pl.ds(at, width)]
    first_tile = tile_is_first()
    count = volume_ref.shape[1]
    for channel in range(2):
        rows = []
        for row in (0, count - 1):
            before, after = edges_of(plane_a_ref, plane_b_ref, channel * count + row, width)
            rows.append((volume_ref[channel, row], jnp.concatenate([before, after], axis=0)))
        for low, row_ref in ((jnp.logical_not(first_tile), row_a_ref), (first_tile, row_b_ref)):
            row_ref[channel, :width] = jnp.where(low, rows[0][0], rows[1][0])
            row_ref[channel, width : width + 2] = jnp.where(low, rows[0][1], rows[1][1])
            row_ref[channel, width + SUBLANES :] = rays_ref[...]


def fold_kernel(
    own_ref, rim_a_ref, rim_b_ref, projected_ref, dual_ref, rays_ref, row_ref, object_ref, residual_ref
):
    width = own_ref.shape[1]
    sums = [
        own_ref[part]
        + rim_a_ref[part * width : (part + 1) * width]
        + rim_b_ref[part * width : (part + 1) * width]
        for part in range(3)
    ]
    for part in range(2):
        target = projected_ref[0, part]
        dual = dual_ref[0, part]
        updated = (sums[part] + penalty * (target - dual)) / (sums[2] + penalty)
        object_ref[0, part] = updated
        residual_ref[part * width : (part + 1) * width] = target - updated - dual
    residual_ref[2 * width : 2 * width + SUBLANES] = rays_ref[...]
    residual_ref[2 * width + SUBLANES :] = row_ref[0, width + SUBLANES :]


def variation_kernel(
    volume_ref, plane_a_ref, plane_b_ref, row_a_ref, row_b_ref, base_ref, padded, norms
):
    width = volume_ref.shape[2]
    length = volume_ref.shape[3]
    count = volume_ref.shape[1]
    margin = 8
    first_tile = tile_is_first()
    lanes = lax.broadcasted_iota(jnp.int32, (width, length), 1)
    first_lane = lanes == 0
    last_lane = lanes == length - 1
    for channel in range(2):
        for row in range(count):
            before, after = edges_of(plane_a_ref, plane_b_ref, channel * count + row, width)
            padded[row + 1, margin : margin + width] = volume_ref[channel, row]
            padded[row + 1, margin - 1 : margin] = before
            padded[row + 1, margin + width : margin + width + 1] = after
        row_a, row_b = row_a_ref[channel], row_b_ref[channel]
        for row, beside in (
            (0, jnp.where(first_tile, row_b, row_a)),
            (count + 1, jnp.where(first_tile, row_a, row_b)),
        ):
            padded[row, margin : margin + width] = beside[:width]
            padded[row, margin - 1 : margin] = beside[width : width + 1]
            padded[row, margin + width : margin + width + 1] = beside[width + 1 : width + 2]
        previous_y = None
        for row in range(count + 1):
            here = padded[row, margin : margin + width]
            along_y = padded[row + 1, margin : margin + width] - here
            along_x = padded[row, margin + 1 : margin + width + 1] - here
            along_z = jnp.where(last_lane, 0.0, pltpu.roll(here, length - 1, 1)) - here
            inverse = lax.rsqrt(
                along_y * along_y + along_x * along_x + along_z * along_z + smoothing * smoothing
            )
            norm_y = along_y * inverse
            if row > 0:
                norm_x = along_x * inverse
                norm_z = along_z * inverse
                corner = padded[row, margin - 1 : margin]
                corner_y = padded[row + 1, margin - 1 : margin] - corner
                corner_x = here[:1] - corner
                corner_z = (
                    jnp.where(last_lane[:1], 0.0, pltpu.roll(corner, length - 1, 1)) - corner
                )
                corner_norm = corner_x * lax.rsqrt(
                    corner_y * corner_y
                    + corner_x * corner_x
                    + corner_z * corner_z
                    + smoothing * smoothing
                )
                norms[margin : margin + width] = norm_x
                norms[margin - 1 : margin] = corner_norm
                behind_x = norms[margin - 1 : margin + width - 1]
                ahead = here * lax.rsqrt(here * here + smoothing * smoothing)
                behind_z = jnp.where(first_lane, ahead, pltpu.roll(norm_z, 1, 1))
                divergence = (
                    norm_y - previous_y + (norm_x - behind_x) + (norm_z - behind_z)
                )
                base_ref[channel, row - 1] = here + (step_size * tv_weight) * divergence
            previous_y = norm_y


def spread_kernel(
    shift_ref, weight_ref, base_ref, beside_ref, object_ref, keep_ref, send_ref, object_out_ref, padded
):
    object_out_ref[...] = object_ref[...]
    width = base_ref.shape[2]
    count = base_ref.shape[1]
    columns, tiles = keep_ref.shape[0], lax.axis_size("tile")
    me, tile, scan = lax.axis_index("angle"), lax.axis_index("tile"), lax.axis_index("scan")
    upper = me >= columns // 2
    chunks = [slice(at, at + LANES) for at in range(0, base_ref.shape[3], LANES)]
    exists = jnp.where(upper, scan < lax.axis_size("scan") - 1, scan > 0).astype(jnp.float32)
    own_at = pl.multiple_of(jnp.where(upper, 0, width), width)
    beside_at = pl.multiple_of(jnp.where(upper, width, 0), width)
    for row in range(count):
        for channel in range(2):
            for chunk, at in enumerate(chunks):
                padded[row, channel, chunk, pl.ds(own_at, width)] = base_ref[channel, row, :, at]
                padded[row, channel, chunk, pl.ds(beside_at, width)] = (
                    beside_ref[channel, row, :, at] * exists
                )
    for turn in range(columns):
        for flip, out_ref in ((0, keep_ref), (1, send_ref)):
            angle = lax.rem(me + turn, columns) * tiles + (tile if flip == 0 else 1 - tile)
            for channel in range(2):
                for chunk, at in enumerate(chunks):
                    total = jnp.zeros((width, LANES), jnp.float32)
                    for row in range(count):
                        start = jnp.where(upper, 0, width) + shift_ref[row, angle]
                        fraction = weight_ref[row, angle]
                        total += (1.0 - fraction) * padded[row, channel, chunk, pl.ds(start, width)]
                        total += fraction * padded[row, channel, chunk, pl.ds(start + 1, width)]
                    out_ref[turn, channel, :, at] = total


def operator_kernel(*refs):
    packed_refs, (high_ref, low_ref) = refs[:-2], refs[-2:]
    tiles = lax.axis_size("tile")
    columns = len(packed_refs)
    rows_out, reach = high_ref.shape[1:]
    width = reach // 3
    count = rows_out // (2 * width) - 1
    me, tile, scan = lax.axis_index("angle"), lax.axis_index("tile"), lax.axis_index("scan")

    def taps(shape, first, table, row, step):
        lanes = lax.broadcasted_iota(jnp.int32, shape, 1)
        sublanes = lax.broadcasted_iota(jnp.int32, shape, 0)
        offset = (lanes - sublanes).astype(jnp.float32) - first
        shift = step * table[2 * row : 2 * row + 1]
        fraction = table[2 * row + 1 : 2 * row + 2]
        return jnp.where(offset == shift, 1.0 - fraction, 0.0) + jnp.where(
            offset == shift + step, fraction, 0.0
        )

    def angle_of(turn, flip):
        return lax.rem(me + turn, columns) * tiles + (tile if flip == 0 else 1 - tile)

    def table_of(turn, flip, angle):
        at = 2 * width + SUBLANES * flip
        tile_of = packed_refs[turn][at : at + SUBLANES]
        lanes = lax.broadcasted_iota(jnp.int32, tile_of.shape, 1)
        return jnp.sum(jnp.where(lanes == angle, tile_of, 0.0), axis=1, keepdims=True)

    cells = lax.broadcasted_iota(jnp.int32, (width, 2 * width), 1)
    forward = []
    backward = [[] for _ in range(columns)]
    for turn in range(columns):
        upper = lax.rem(me + turn, columns) >= columns // 2
        base_at = jnp.where(upper, 0, width)
        first_cell = jnp.where(upper, 0, jnp.where(scan > 0, 0, width))
        end_cell = jnp.where(upper & (scan == lax.axis_size("scan") - 1), width, 2 * width)
        inside = (cells >= first_cell) & (cells < end_cell)
        for flip in range(tiles):
            for row in range(count):
                parts = []
                for own in range(tiles):
                    table = table_of(turn, flip, angle_of(0, own))
                    part = taps((width, 2 * width), base_at.astype(jnp.float32), table, row, 1.0)
                    parts.append(jnp.where(inside, part, 0.0))
                forward.append(jnp.concatenate(parts, axis=0))
                for source in range(columns):
                    table = table_of(turn, flip, angle_of(source, 0))
                    first = (width - base_at).astype(jnp.float32)
                    backward[source].append(taps((2 * width, reach), first, table, row, -1.0))
    left = split(jnp.concatenate(forward, axis=1))
    for source in range(columns):
        both = product(left, split(jnp.concatenate(backward[source], axis=0)))
        blocks = [both]
        for flip in range(tiles):
            for row in range(count):
                table = table_of(0, flip, angle_of(source, 0))
                blocks.append(taps((width, reach), float(width), table, row, -1.0))
        high_ref[source], low_ref[source] = split(jnp.concatenate(blocks, axis=0))


def apply_kernel(here_ref, side_a_ref, side_b_ref, high_ref, low_ref, keep_ref, own_ref, send_ref, wide):
    width = keep_ref.shape[1]
    columns = here_ref.shape[0]
    count = own_ref.shape[1]
    even = scan_is_even()
    at_a = pl.multiple_of(jnp.where(even, 2 * width, 0), width)
    at_b = pl.multiple_of(jnp.where(even, 0, 2 * width), width)
    for source in range(columns):
        for channel in range(2):
            at = slice(channel * width, (channel + 1) * width)
            wide[source, channel, width : 2 * width] = here_ref[source, at]
            wide[source, channel, pl.ds(at_a, width)] = side_a_ref[source, at]
            wide[source, channel, pl.ds(at_b, width)] = side_b_ref[source, at]
    for channel in range(2):
        total = 0.0
        for source in range(columns):
            total += product((high_ref[source], low_ref[source]), split(wide[source, channel]))
        keep_ref[channel] = total[:width]
        send_ref[channel * width : (channel + 1) * width] = total[width : 2 * width]
        for row in range(count):
            at = (2 + row) * width
            own_ref[channel, row] = total[at : at + width]
            target = (2 + channel * count + row) * width
            send_ref[target : target + width] = total[at + count * width : at + (count + 1) * width]


def finish_kernel(*refs):
    keep_ref, own_ref, received_ref, base_ref, object_ref, dual_ref = refs[:6]
    spreads, (dual_out_ref, volume_ref, projected_ref) = refs[6:-3], refs[-3:]
    count, width = own_ref.shape[1:3]
    for channel in range(2):
        received = received_ref[channel * width : (channel + 1) * width]
        projection = -step_size * (keep_ref[channel] + received)
        for spread_ref in spreads:
            projection = projection + spread_ref[channel]
        projected_ref[0, channel] = projection
        dual_out_ref[0, channel] = dual_ref[0, channel] + object_ref[0, channel] - projection
        for row in range(count):
            at = (2 + channel * count + row) * width
            descent = own_ref[channel, row] + received_ref[at : at + width]
            volume_ref[channel, row] = base_ref[channel, row] - step_size * descent


def call(
    kernel, shapes, operands, scratch, flops, scalars=0, staged=(), numbers=(), copies=0, kind=jnp.float32, kinds={}
):
    held = sum(operand.nbytes for operand in operands[scalars:] + staged)
    held += 4 * sum(math.prod(shape) for shape in shapes)
    own = 4 * sum(math.prod(shape) for shape in scratch)
    outputs = [
        jax.ShapeDtypeStruct(shape, kinds.get(number, kind)) for number, shape in enumerate(shapes)
    ]
    scratch_shapes = [pltpu.VMEM(shape, jnp.float32) for shape in scratch]
    if staged and not copies:
        outputs += [jax.ShapeDtypeStruct(array.shape, array.dtype) for array in staged]
        copies = len(staged) + len(numbers)
        scratch_shapes += [pltpu.SMEM(array.shape, array.dtype) for array in numbers]
    staged += numbers
    if copies:
        scratch_shapes.append(pltpu.SemaphoreType.DMA((copies,)))
    in_specs = [SMEM] * scalars + [VMEM] * (len(operands) - scalars) + [HBM] * len(staged)
    return pl.pallas_call(
        kernel,
        out_shape=outputs,
        in_specs=in_specs,
        out_specs=[VMEM] * len(outputs),
        scratch_shapes=scratch_shapes,
        compiler_params=pltpu.CompilerParams(vmem_limit_bytes=held + own + SPARE_BYTES),
        cost_estimate=pl.CostEstimate(flops=flops, bytes_accessed=held, transcendentals=0),
    )(*operands, *(pltpu.with_memory_space_constraint(array, pltpu.HBM) for array in staged))


def body(
    transmission,
    scaled_dual,
    projected,
    volume,
    intensities,
    probe_wave,
    slot_first_rows,
    slot_first_columns,
    patch_counts,
    shift_table,
    tap_weight,
):
    width, length = transmission.shape[2:]
    count = volume.shape[1]
    scans, columns, tiles = (lax.axis_size(axis) for axis in ("scan", "angle", "tile"))
    rounds = [[(i, i + 1) for i in range(first, scans - 1, 2)] for first in (0, 1)]
    both = [pairs + [(target, source) for source, target in pairs] for pairs in rounds]
    swap = [(0, 1), (1, 0)]

    def exchange(block, number):
        return lax.ppermute(block, "scan", both[number])

    def across(block):
        return lax.ppermute(block, "tile", swap)

    edges = 2 * 2 * count
    (plane,) = call(
        pack_kernel,
        [(2 * width + -(-edges // SUBLANES) * SUBLANES, length)],
        (),
        [(edges, SUBLANES, length)],
        10**5,
        staged=(transmission, volume),
        copies=2 + edges,
    )
    plane_a = exchange(plane, 0)
    plane_b = exchange(plane, 1)
    tables = [jnp.asarray(table) for table in dft_tables(probe_wave.shape[1])]
    slots = slot_first_rows.shape[1]
    side = probe_wave.shape[1]
    probes, density, slot_numbers, rays, _, *held = call(
        prepare_kernel,
        [
            (slots, 2, side, side),
            (1, 3 * width, length),
            (slots, SUBLANES, side),
            (SUBLANES, length),
        ],
        (patch_counts,),
        [],
        10**7,
        1,
        (probe_wave, intensities, volume, *tables),
        (slot_first_rows, slot_first_columns, shift_table.T, tap_weight.T),
        kinds={2: jnp.int32},
    )
    volume_here = held[1]
    turns = [[(i, (i - turn) % columns) for i in range(columns)] for turn in range(columns)]
    own, rim_a, rim_b, row_a, row_b = call(
        patch_kernel,
        [(3, width, length)]
        + [(3 * width, length)] * 2
        + [(2, width + 2 * SUBLANES, length)] * 2,
        (probes, density, slot_numbers, rays, plane, *held, plane_a, plane_b),
        [(2, 3 * width, length), (3, 3 * width, length)],
        10**9,
    )
    rim_a = exchange(rim_a, 0)
    rim_b = exchange(rim_b, 1)
    bridge = [(i * tiles + 1, (i + 1) * tiles) for i in range(columns - 1)]
    bridge += [(target, source) for source, target in bridge]
    row_b = lax.ppermute(row_b, ("angle", "tile"), bridge)
    row_a = across(row_a)
    updated, residual = call(
        fold_kernel,
        [transmission.shape, (2 * width + 2 * SUBLANES, length)],
        (own, rim_a, rim_b, projected, scaled_dual, rays, row_a),
        [],
        10**6,
    )
    by_column = [residual]
    for turn in range(1, columns):
        by_column.append(lax.ppermute(residual, "angle", turns[turn]))
    (base,) = call(
        variation_kernel,
        [volume.shape],
        (volume_here, plane_a, plane_b, row_a, row_b),
        [(count + 2, width + 16, length), (width + 16, length)],
        10**7,
    )
    lower = range(columns // 2)
    route = []
    for scan in range(scans):
        for column in range(columns):
            target = scan + 1 if column in lower else scan - 1
            if 0 <= target < scans:
                route.append((scan * columns + column, target * columns + column))
    beside = lax.ppermute(base, ("scan", "angle"), route)
    here = jnp.stack(by_column)
    side_a = exchange(here, 0)
    side_b = exchange(here, 1)
    high, low = call(
        operator_kernel,
        [(columns, (2 + 2 * count) * width, 3 * width)] * 2,
        tuple(by_column),
        [],
        10**8,
        kind=jnp.bfloat16,
    )
    block = (columns, 2, width, length)
    keep, send, new_transmission = call(
        spread_kernel,
        [block, block, transmission.shape],
        (shift_table.T, tap_weight.T, base, beside, updated),
        [(count, 2, length // LANES, 2 * width, LANES)],
        10**7,
        2,
    )
    received = across(send)
    spreads = [keep[0], received[0]]
    for turn in range(1, columns):
        route = [(i, (i + turn) % columns) for i in range(columns)]
        spreads.append(lax.ppermute(keep[turn] + received[turn], "angle", route))
    keep, own, send = call(
        apply_kernel,
        [(2, width, length), volume.shape, ((2 + 2 * count) * width, length)],
        (here, side_a, side_b, high, low),
        [(columns, 2, 3 * width, length)],
        10**9,
    )
    received = across(send)
    new_dual, new_volume, new_projected = call(
        finish_kernel,
        [transmission.shape, volume.shape, transmission.shape],
        (keep, own, received, base, updated, scaled_dual, *spreads),
        [],
        10**6,
    )
    return (new_transmission, new_dual, new_volume, new_projected)


def solution(mesh):
    plane = P(("groups", "angle", "tile"), None, "scan", None)
    cells = P("groups", ("angle", "tile"), "scan", None)
    slots = P(("groups", "angle", "tile"), "scan")
    return jax.shard_map(
        body,
        mesh=mesh,
        in_specs=(
            plane,
            plane,
            plane,
            cells,
            P(("groups", "angle", "tile"), "scan", None, None),
            P("groups", None, None),
            slots,
            slots,
            slots,
            P(None, ("angle", "tile")),
            P(None, ("angle", "tile")),
        ),
        out_specs=(plane, plane, cells, plane),
        check_vma=False,
    )
```

```python
import math

import jax
import jax.numpy as jnp
import numpy as np
from jax import lax
from jax.experimental import pallas as pl
from jax.experimental.pallas import tpu as pltpu
from jax.sharding import PartitionSpec as P


penalty = 4.0
amplitude_step = 0.25
tv_weight = 1.0
smoothing = 0.05
step_size = 0.008

VMEM = pl.BlockSpec(memory_space=pltpu.VMEM)
SMEM = pl.BlockSpec(memory_space=pltpu.SMEM)
HBM = pl.BlockSpec(memory_space=pltpu.MemorySpace.HBM)
LANES = 128
SUBLANES = 8
SPARE_BYTES = 8 << 20


def split(values):
    high = values.astype(jnp.bfloat16)
    return (high, (values - high.astype(jnp.float32)).astype(jnp.bfloat16))


def product(left, right):
    total = jnp.dot(left[0], right[0], preferred_element_type=jnp.float32)
    total += jnp.dot(left[0], right[1], preferred_element_type=jnp.float32)
    return total + jnp.dot(left[1], right[0], preferred_element_type=jnp.float32)


def dft_tables(length):
    grid_ids = np.arange(length)
    radians = (grid_ids[:, None] * grid_ids[None, :] % length) * (2.0 * math.pi / length)
    cosine = np.cos(radians) / math.sqrt(length)
    sine = np.sin(radians) / math.sqrt(length)
    forward = np.block([[cosine, sine], [-sine, cosine]])
    tables = []
    for table in (forward, forward.T):
        high = table.astype(jnp.bfloat16)
        tables += [high, (table - high.astype(np.float64)).astype(jnp.bfloat16)]
    return tables


def tile_is_first():
    return lax.axis_index("tile") == 0


def scan_is_even():
    return lax.rem(lax.axis_index("scan"), 2) == 0


def pack_kernel(plane_ref, volume_ref, packed_ref, slabs, done):
    width = plane_ref.shape[2]
    count = volume_ref.shape[1]
    copies = [
        (plane_ref.at[0, channel], packed_ref.at[channel * width : (channel + 1) * width])
        for channel in range(2)
    ]
    for channel in range(2):
        for row in range(count):
            for side, at in enumerate((0, width - SUBLANES)):
                source = volume_ref.at[channel, row, at : at + SUBLANES]
                copies.append((source, slabs.at[(channel * count + row) * 2 + side]))
    copies = [
        pltpu.make_async_copy(source, target, done.at[number])
        for number, (source, target) in enumerate(copies)
    ]
    for copy in copies:
        copy.start()
    for copy in copies[2:]:
        copy.wait()
    for edge in range(slabs.shape[0]):
        take = 0 if edge % 2 == 0 else SUBLANES - 1
        packed_ref[2 * width + edge : 2 * width + edge + 1] = slabs[edge, take : take + 1]
    for copy in copies[:2]:
        copy.wait()


def edges_of(plane_a_ref, plane_b_ref, number, width):
    even = scan_is_even()
    at = 2 * width + 2 * number
    first_a, last_a = plane_a_ref[at : at + 1], plane_a_ref[at + 1 : at + 2]
    first_b, last_b = plane_b_ref[at : at + 1], plane_b_ref[at + 1 : at + 2]
    return (jnp.where(even, last_b, last_a), jnp.where(even, first_a, first_b))


def slot_masks(rows_ref, columns_ref, count_ref, slot, side):
    lanes = lax.broadcasted_iota(jnp.int32, (side, side), 1)
    sublanes = lax.broadcasted_iota(jnp.int32, (side, side), 0)
    near_lanes = lanes >= rows_ref[0, slot]
    near_columns = sublanes >= columns_ref[0, slot]
    return (near_lanes, near_columns, jnp.full((side, side), slot < count_ref[0, 0]))


def place(totals, part, term, masks, width):
    side = term.shape[0]
    near_lanes, near_columns, live = masks
    inner = live & near_columns
    outer = (live & jnp.logical_not(near_columns))[:width]
    for start, lane_mask in ((0, near_lanes), (side, jnp.logical_not(near_lanes))):
        at = slice(start, start + side)
        totals[part, :side, at] += jnp.where(inner & lane_mask, term, 0.0)
        totals[part, side:, at] += jnp.where(outer & lane_mask[:width], term[:width], 0.0)


def prepare_kernel(count_ref, *refs):
    held = (len(refs) - 13) // 2
    sources = refs[: held + 4]
    probes_ref, density_ref, slots_ref, rays_ref = refs[held + 4 : held + 8]
    targets, done = refs[held + 8 : -1], refs[-1]
    rows_ref, columns_ref, shift_ref, weight_ref = targets[held:]
    copies = [
        pltpu.make_async_copy(source, target, done.at[number])
        for number, (source, target) in enumerate(zip(sources, targets))
    ]
    for copy in copies:
        copy.start()
    probe_ref = targets[0]
    side = probe_ref.shape[1]
    slots = probes_ref.shape[0]
    width = density_ref.shape[1] - side
    density_ref[...] = jnp.zeros_like(density_ref)
    for copy in copies[:1] + copies[held:]:
        copy.wait()
    places = lax.broadcasted_iota(jnp.int32, slots_ref.shape[1:], 0)
    for slot in range(slots):
        live = jnp.where(slot < count_ref[0, 0], 1, 0)
        numbers = jnp.where(places == 0, rows_ref[0, slot], columns_ref[0, slot])
        slots_ref[slot] = jnp.where(places == 2, live, numbers)
        turn = lax.rem(rows_ref[0, slot], side)
        probe = [
            pltpu.roll(pltpu.roll(probe_ref[part], columns_ref[0, slot], 0), turn, 1)
            for part in range(2)
        ]
        for part in range(2):
            probes_ref[slot, part] = probe[part]
        masks = slot_masks(rows_ref, columns_ref, count_ref, slot, side)
        place(density_ref, 0, probe[0] * probe[0] + probe[1] * probe[1], masks, width)
    places = lax.broadcasted_iota(jnp.int32, rays_ref.shape, 0)
    lanes = lax.broadcasted_iota(jnp.int32, rays_ref.shape, 1)
    rays = jnp.zeros(rays_ref.shape, jnp.float32)
    for row in range(shift_ref.shape[0]):
        for angle in range(shift_ref.shape[1]):
            shift = shift_ref[row, angle].astype(jnp.float32)
            here = lanes == angle
            rays = jnp.where(here & (places == 2 * row), shift, rays)
            rays = jnp.where(here & (places == 2 * row + 1), weight_ref[row, angle], rays)
    rays_ref[...] = rays
    for copy in copies[1:held]:
        copy.wait()


def patch_kernel(
    probes_ref,
    density_ref,
    slots_ref,
    plane_ref,
    intensity_ref,
    volume_ref,
    forward_high_ref,
    forward_low_ref,
    inverse_high_ref,
    inverse_low_ref,
    plane_a_ref,
    plane_b_ref,
    own_ref,
    rim_a_ref,
    rim_b_ref,
    row_a_ref,
    row_b_ref,
    wide,
    totals,
):
    width = volume_ref.shape[2]
    slots, _, side, _ = probes_ref.shape
    even = scan_is_even()
    at_a = pl.multiple_of(jnp.where(even, 2 * width, 0), width)
    at_b = pl.multiple_of(jnp.where(even, 0, 2 * width), width)
    for part in range(2):
        at = slice(part * width, (part + 1) * width)
        wide[part, width : 2 * width] = plane_ref[at]
        wide[part, pl.ds(at_a, width)] = plane_a_ref[at]
        wide[part, pl.ds(at_b, width)] = plane_b_ref[at]
    forward = (forward_high_ref[...], forward_low_ref[...])
    inverse = (inverse_high_ref[...], inverse_low_ref[...])
    waves, masks = [], []
    lanes = lax.broadcasted_iota(jnp.int32, (side, side), 1)
    sublanes = lax.broadcasted_iota(jnp.int32, (side, side), 0)
    for slot in range(slots):
        probe = probes_ref[slot]
        row, column, live = (
            jnp.broadcast_to(slots_ref[slot, number : number + 1], (side, side))
            for number in range(3)
        )
        near_lanes, near_columns = lanes >= row, sublanes >= column
        masks.append((near_lanes, near_columns, live > 0))
        window = []
        for part in range(2):
            near = jnp.where(near_lanes, wide[part, :side, :side], wide[part, :side, side:])
            wrapped = jnp.where(
                near_lanes[:width], wide[part, side:, :side], wide[part, side:, side:]
            )
            wrapped = jnp.concatenate([wrapped, near[width:]], axis=0)
            window.append(jnp.where(near_columns, near, wrapped))
        wave_real = probe[0] * window[0] - probe[1] * window[1]
        wave_imaginary = probe[0] * window[1] + probe[1] * window[0]
        waves.append(jnp.concatenate([wave_real, wave_imaginary], axis=1))
    half = product(split(jnp.concatenate(waves, axis=0)), inverse)
    half = jnp.concatenate(
        [
            jnp.concatenate(
                [half[slot * side : (slot + 1) * side, part * side : (part + 1) * side] for slot in range(slots)],
                axis=1,
            )
            for part in range(2)
        ],
        axis=0,
    )
    far = product(forward, split(half))
    far_real, far_imaginary = far[:side], far[side:]
    intensity = jnp.concatenate(
        [intensity_ref[0, slot].astype(jnp.float32) for slot in range(slots)], axis=1
    )
    factor = 1.0 - amplitude_step * (
        far_real * far_real + far_imaginary * far_imaginary - intensity
    )
    corrected = jnp.concatenate([far_real * factor, far_imaginary * factor], axis=0)
    half = product(inverse, split(corrected))
    half = jnp.concatenate(
        [
            jnp.concatenate(
                [half[part * side : (part + 1) * side, slot * side : (slot + 1) * side] for part in range(2)],
                axis=1,
            )
            for slot in range(slots)
        ],
        axis=0,
    )
    near = product(split(half), forward)
    totals[:2] = jnp.zeros_like(totals[:2])
    totals[2:] = density_ref[...]
    for slot in range(slots):
        probe = probes_ref[slot]
        near_real = near[slot * side : (slot + 1) * side, :side]
        near_imaginary = near[slot * side : (slot + 1) * side, side:]
        place(totals, 0, probe[0] * near_real + probe[1] * near_imaginary, masks[slot], width)
        place(totals, 1, probe[0] * near_imaginary - probe[1] * near_real, masks[slot], width)
    own_ref[...] = totals[:, width : 2 * width]
    for rim_ref, at in ((rim_a_ref, at_a), (rim_b_ref, at_b)):
        for part in range(totals.shape[0]):
            rim_ref[part * width : (part + 1) * width] = totals[part, pl.ds(at, width)]
    first_tile = tile_is_first()
    count = volume_ref.shape[1]
    for channel in range(2):
        rows = []
        for row in (0, count - 1):
            before, after = edges_of(plane_a_ref, plane_b_ref, channel * count + row, width)
            rows.append((volume_ref[channel, row], jnp.concatenate([before, after], axis=0)))
        for low, row_ref in ((jnp.logical_not(first_tile), row_a_ref), (first_tile, row_b_ref)):
            row_ref[channel, :width] = jnp.where(low, rows[0][0], rows[1][0])
            row_ref[channel, width : width + 2] = jnp.where(low, rows[0][1], rows[1][1])


def fold_kernel(
    own_ref, rim_a_ref, rim_b_ref, projected_ref, dual_ref, rays_ref, too_ref, object_ref, residual_ref
):
    width = own_ref.shape[1]
    sums = [
        own_ref[part]
        + rim_a_ref[part * width : (part + 1) * width]
        + rim_b_ref[part * width : (part + 1) * width]
        for part in range(3)
    ]
    for part in range(2):
        target = projected_ref[0, part]
        dual = dual_ref[0, part]
        updated = (sums[part] + penalty * (target - dual)) / (sums[2] + penalty)
        object_ref[0, part] = updated
        residual_ref[part * width : (part + 1) * width] = target - updated - dual
    residual_ref[2 * width : 2 * width + SUBLANES] = rays_ref[...]
    residual_ref[2 * width + SUBLANES :] = too_ref[...]


def variation_kernel(
    volume_ref, plane_a_ref, plane_b_ref, row_a_ref, row_b_ref, base_ref, padded, norms
):
    width = volume_ref.shape[2]
    length = volume_ref.shape[3]
    count = volume_ref.shape[1]
    margin = 8
    first_tile = tile_is_first()
    lanes = lax.broadcasted_iota(jnp.int32, (width, length), 1)
    first_lane = lanes == 0
    last_lane = lanes == length - 1
    for channel in range(2):
        for row in range(count):
            before, after = edges_of(plane_a_ref, plane_b_ref, channel * count + row, width)
            padded[row + 1, margin : margin + width] = volume_ref[channel, row]
            padded[row + 1, margin - 1 : margin] = before
            padded[row + 1, margin + width : margin + width + 1] = after
        row_a, row_b = row_a_ref[channel], row_b_ref[channel]
        for row, beside in (
            (0, jnp.where(first_tile, row_b, row_a)),
            (count + 1, jnp.where(first_tile, row_a, row_b)),
        ):
            padded[row, margin : margin + width] = beside[:width]
            padded[row, margin - 1 : margin] = beside[width : width + 1]
            padded[row, margin + width : margin + width + 1] = beside[width + 1 : width + 2]
        previous_y = None
        for row in range(count + 1):
            here = padded[row, margin : margin + width]
            along_y = padded[row + 1, margin : margin + width] - here
            along_x = padded[row, margin + 1 : margin + width + 1] - here
            along_z = jnp.where(last_lane, 0.0, pltpu.roll(here, length - 1, 1)) - here
            inverse = lax.rsqrt(
                along_y * along_y + along_x * along_x + along_z * along_z + smoothing * smoothing
            )
            norm_y = along_y * inverse
            if row > 0:
                norm_x = along_x * inverse
                norm_z = along_z * inverse
                corner = padded[row, margin - 1 : margin]
                corner_y = padded[row + 1, margin - 1 : margin] - corner
                corner_x = here[:1] - corner
                corner_z = (
                    jnp.where(last_lane[:1], 0.0, pltpu.roll(corner, length - 1, 1)) - corner
                )
                corner_norm = corner_x * lax.rsqrt(
                    corner_y * corner_y
                    + corner_x * corner_x
                    + corner_z * corner_z
                    + smoothing * smoothing
                )
                norms[margin : margin + width] = norm_x
                norms[margin - 1 : margin] = corner_norm
                behind_x = norms[margin - 1 : margin + width - 1]
                ahead = here * lax.rsqrt(here * here + smoothing * smoothing)
                behind_z = jnp.where(first_lane, ahead, pltpu.roll(norm_z, 1, 1))
                divergence = (
                    norm_y - previous_y + (norm_x - behind_x) + (norm_z - behind_z)
                )
                base_ref[channel, row - 1] = here + (step_size * tv_weight) * divergence
            previous_y = norm_y


def spread_kernel(
    shift_ref, weight_ref, base_ref, beside_ref, keep_ref, send_ref, padded
):
    width = base_ref.shape[2]
    count = base_ref.shape[1]
    columns, tiles = keep_ref.shape[0], lax.axis_size("tile")
    me, tile, scan = lax.axis_index("angle"), lax.axis_index("tile"), lax.axis_index("scan")
    upper = me >= columns // 2
    chunks = [slice(at, at + LANES) for at in range(0, base_ref.shape[3], LANES)]
    exists = jnp.where(upper, scan < lax.axis_size("scan") - 1, scan > 0).astype(jnp.float32)
    own_at = pl.multiple_of(jnp.where(upper, 0, width), width)
    beside_at = pl.multiple_of(jnp.where(upper, width, 0), width)
    for row in range(count):
        for channel in range(2):
            for chunk, at in enumerate(chunks):
                padded[row, channel, chunk, pl.ds(own_at, width)] = base_ref[channel, row, :, at]
                padded[row, channel, chunk, pl.ds(beside_at, width)] = (
                    beside_ref[channel, row, :, at] * exists
                )
    for turn in range(columns):
        for flip, out_ref in ((0, keep_ref), (1, send_ref)):
            angle = lax.rem(me + turn, columns) * tiles + (tile if flip == 0 else 1 - tile)
            for channel in range(2):
                for chunk, at in enumerate(chunks):
                    total = jnp.zeros((width, LANES), jnp.float32)
                    for row in range(count):
                        start = jnp.where(upper, 0, width) + shift_ref[row, angle]
                        fraction = weight_ref[row, angle]
                        total += (1.0 - fraction) * padded[row, channel, chunk, pl.ds(start, width)]
                        total += fraction * padded[row, channel, chunk, pl.ds(start + 1, width)]
                    out_ref[turn, channel, :, at] = total


def operator_kernel(*refs):
    packed_refs, (object_ref, high_ref, low_ref, object_out_ref) = refs[:-4], refs[-4:]
    object_out_ref[...] = object_ref[...]
    tiles = lax.axis_size("tile")
    columns = len(packed_refs)
    rows_out, reach = high_ref.shape[1:]
    width = reach // 3
    count = rows_out // (2 * width) - 1
    me, tile, scan = lax.axis_index("angle"), lax.axis_index("tile"), lax.axis_index("scan")

    def taps(shape, first, table, row, step):
        lanes = lax.broadcasted_iota(jnp.int32, shape, 1)
        sublanes = lax.broadcasted_iota(jnp.int32, shape, 0)
        offset = (lanes - sublanes).astype(jnp.float32) - first
        shift = step * table[2 * row : 2 * row + 1]
        fraction = table[2 * row + 1 : 2 * row + 2]
        return jnp.where(offset == shift, 1.0 - fraction, 0.0) + jnp.where(
            offset == shift + step, fraction, 0.0
        )

    def angle_of(turn, flip):
        return lax.rem(me + turn, columns) * tiles + (tile if flip == 0 else 1 - tile)

    def table_of(turn, flip, angle):
        at = 2 * width + SUBLANES * flip
        tile_of = packed_refs[turn][at : at + SUBLANES]
        lanes = lax.broadcasted_iota(jnp.int32, tile_of.shape, 1)
        return jnp.sum(jnp.where(lanes == angle, tile_of, 0.0), axis=1, keepdims=True)

    cells = lax.broadcasted_iota(jnp.int32, (width, 2 * width), 1)
    forward = []
    backward = [[] for _ in range(columns)]
    for turn in range(columns):
        upper = lax.rem(me + turn, columns) >= columns // 2
        base_at = jnp.where(upper, 0, width)
        first_cell = jnp.where(upper, 0, jnp.where(scan > 0, 0, width))
        end_cell = jnp.where(upper & (scan == lax.axis_size("scan") - 1), width, 2 * width)
        inside = (cells >= first_cell) & (cells < end_cell)
        for flip in range(tiles):
            for row in range(count):
                parts = []
                for own in range(tiles):
                    table = table_of(turn, flip, angle_of(0, own))
                    part = taps((width, 2 * width), base_at.astype(jnp.float32), table, row, 1.0)
                    parts.append(jnp.where(inside, part, 0.0))
                forward.append(jnp.concatenate(parts, axis=0))
                for source in range(columns):
                    table = table_of(turn, flip, angle_of(source, 0))
                    first = (width - base_at).astype(jnp.float32)
                    backward[source].append(taps((2 * width, reach), first, table, row, -1.0))
    left = split(jnp.concatenate(forward, axis=1))
    for source in range(columns):
        both = product(left, split(jnp.concatenate(backward[source], axis=0)))
        blocks = [both]
        for flip in range(tiles):
            for row in range(count):
                table = table_of(0, flip, angle_of(source, 0))
                blocks.append(taps((width, reach), float(width), table, row, -1.0))
        high_ref[source], low_ref[source] = split(jnp.concatenate(blocks, axis=0))


def apply_kernel(here_ref, side_a_ref, side_b_ref, high_ref, low_ref, keep_ref, own_ref, send_ref, wide):
    width = keep_ref.shape[1]
    columns = here_ref.shape[0]
    count = own_ref.shape[1]
    even = scan_is_even()
    at_a = pl.multiple_of(jnp.where(even, 2 * width, 0), width)
    at_b = pl.multiple_of(jnp.where(even, 0, 2 * width), width)
    for source in range(columns):
        for channel in range(2):
            at = slice(channel * width, (channel + 1) * width)
            wide[source, channel, width : 2 * width] = here_ref[source, at]
            wide[source, channel, pl.ds(at_a, width)] = side_a_ref[source, at]
            wide[source, channel, pl.ds(at_b, width)] = side_b_ref[source, at]
    for channel in range(2):
        total = 0.0
        for source in range(columns):
            total += product((high_ref[source], low_ref[source]), split(wide[source, channel]))
        keep_ref[channel] = total[:width]
        send_ref[channel * width : (channel + 1) * width] = total[width : 2 * width]
        for row in range(count):
            at = (2 + row) * width
            own_ref[channel, row] = total[at : at + width]
            target = (2 + channel * count + row) * width
            send_ref[target : target + width] = total[at + count * width : at + (count + 1) * width]


def finish_kernel(*refs):
    keep_ref, own_ref, received_ref, base_ref, object_ref, dual_ref = refs[:6]
    spreads, (dual_out_ref, volume_ref, projected_ref) = refs[6:-3], refs[-3:]
    count, width = own_ref.shape[1:3]
    for channel in range(2):
        received = received_ref[channel * width : (channel + 1) * width]
        projection = -step_size * (keep_ref[channel] + received)
        for spread_ref in spreads:
            projection = projection + spread_ref[channel]
        projected_ref[0, channel] = projection
        dual_out_ref[0, channel] = dual_ref[0, channel] + object_ref[0, channel] - projection
        for row in range(count):
            at = (2 + channel * count + row) * width
            descent = own_ref[channel, row] + received_ref[at : at + width]
            volume_ref[channel, row] = base_ref[channel, row] - step_size * descent


def call(
    kernel, shapes, operands, scratch, flops, scalars=0, staged=(), numbers=(), copies=0, kind=jnp.float32, kinds={}
):
    held = sum(operand.nbytes for operand in operands[scalars:] + staged)
    held += 4 * sum(math.prod(shape) for shape in shapes)
    own = 4 * sum(math.prod(shape) for shape in scratch)
    outputs = [
        jax.ShapeDtypeStruct(shape, kinds.get(number, kind)) for number, shape in enumerate(shapes)
    ]
    scratch_shapes = [pltpu.VMEM(shape, jnp.float32) for shape in scratch]
    if staged and not copies:
        outputs += [jax.ShapeDtypeStruct(array.shape, array.dtype) for array in staged]
        copies = len(staged) + len(numbers)
        scratch_shapes += [pltpu.SMEM(array.shape, array.dtype) for array in numbers]
    staged += numbers
    if copies:
        scratch_shapes.append(pltpu.SemaphoreType.DMA((copies,)))
    in_specs = [SMEM] * scalars + [VMEM] * (len(operands) - scalars) + [HBM] * len(staged)
    return pl.pallas_call(
        kernel,
        out_shape=outputs,
        in_specs=in_specs,
        out_specs=[VMEM] * len(outputs),
        scratch_shapes=scratch_shapes,
        compiler_params=pltpu.CompilerParams(vmem_limit_bytes=held + own + SPARE_BYTES),
        cost_estimate=pl.CostEstimate(flops=flops, bytes_accessed=held, transcendentals=0),
    )(*operands, *(pltpu.with_memory_space_constraint(array, pltpu.HBM) for array in staged))


def body(
    transmission,
    scaled_dual,
    projected,
    volume,
    intensities,
    probe_wave,
    slot_first_rows,
    slot_first_columns,
    patch_counts,
    shift_table,
    tap_weight,
):
    width, length = transmission.shape[2:]
    count = volume.shape[1]
    scans, columns, tiles = (lax.axis_size(axis) for axis in ("scan", "angle", "tile"))
    rounds = [[(i, i + 1) for i in range(first, scans - 1, 2)] for first in (0, 1)]
    both = [pairs + [(target, source) for source, target in pairs] for pairs in rounds]
    swap = [(0, 1), (1, 0)]

    def exchange(block, number):
        return lax.ppermute(block, "scan", both[number])

    def across(block):
        return lax.ppermute(block, "tile", swap)

    edges = 2 * 2 * count
    (plane,) = call(
        pack_kernel,
        [(2 * width + -(-edges // SUBLANES) * SUBLANES, length)],
        (),
        [(edges, SUBLANES, length)],
        10**5,
        staged=(transmission, volume),
        copies=2 + edges,
    )
    plane_a = exchange(plane, 0)
    plane_b = exchange(plane, 1)
    tables = [jnp.asarray(table) for table in dft_tables(probe_wave.shape[1])]
    slots = slot_first_rows.shape[1]
    side = probe_wave.shape[1]
    probes, density, slot_numbers, rays, _, *held = call(
        prepare_kernel,
        [
            (slots, 2, side, side),
            (1, 3 * width, length),
            (slots, SUBLANES, side),
            (SUBLANES, length),
        ],
        (patch_counts,),
        [],
        10**7,
        1,
        (probe_wave, intensities, volume, *tables),
        (slot_first_rows, slot_first_columns, shift_table.T, tap_weight.T),
        kinds={2: jnp.int32},
    )
    volume_here = held[1]
    turns = [[(i, (i - turn) % columns) for i in range(columns)] for turn in range(columns)]
    rays_too = across(rays)
    own, rim_a, rim_b, row_a, row_b = call(
        patch_kernel,
        [(3, width, length)]
        + [(3 * width, length)] * 2
        + [(2, width + SUBLANES, length)] * 2,
        (probes, density, slot_numbers, plane, *held, plane_a, plane_b),
        [(2, 3 * width, length), (3, 3 * width, length)],
        10**9,
    )
    rim_a = exchange(rim_a, 0)
    rim_b = exchange(rim_b, 1)
    bridge = [(i * tiles + 1, (i + 1) * tiles) for i in range(columns - 1)]
    bridge += [(target, source) for source, target in bridge]
    row_b = lax.ppermute(row_b, ("angle", "tile"), bridge)
    row_a = across(row_a)
    updated, residual = call(
        fold_kernel,
        [transmission.shape, (2 * width + 2 * SUBLANES, length)],
        (own, rim_a, rim_b, projected, scaled_dual, rays, rays_too),
        [],
        10**6,
    )
    by_column = [residual]
    for turn in range(1, columns):
        by_column.append(lax.ppermute(residual, "angle", turns[turn]))
    (base,) = call(
        variation_kernel,
        [volume.shape],
        (volume_here, plane_a, plane_b, row_a, row_b),
        [(count + 2, width + 16, length), (width + 16, length)],
        10**7,
    )
    lower = range(columns // 2)
    route = []
    for scan in range(scans):
        for column in range(columns):
            target = scan + 1 if column in lower else scan - 1
            if 0 <= target < scans:
                route.append((scan * columns + column, target * columns + column))
    beside = lax.ppermute(base, ("scan", "angle"), route)
    here = jnp.stack(by_column)
    side_a = exchange(here, 0)
    side_b = exchange(here, 1)
    high, low, new_transmission = call(
        operator_kernel,
        [(columns, (2 + 2 * count) * width, 3 * width)] * 2 + [transmission.shape],
        (*by_column, updated),
        [],
        10**8,
        kind=jnp.bfloat16,
        kinds={2: jnp.float32},
    )
    block = (columns, 2, width, length)
    keep, send = call(
        spread_kernel,
        [block, block],
        (shift_table.T, tap_weight.T, base, beside),
        [(count, 2, length // LANES, 2 * width, LANES)],
        10**7,
        2,
    )
    received = across(send)
    spreads = [keep[0], received[0]]
    for turn in range(1, columns):
        route = [(i, (i + turn) % columns) for i in range(columns)]
        spreads.append(lax.ppermute(keep[turn] + received[turn], "angle", route))
    keep, own, send = call(
        apply_kernel,
        [(2, width, length), volume.shape, ((2 + 2 * count) * width, length)],
        (here, side_a, side_b, high, low),
        [(columns, 2, 3 * width, length)],
        10**9,
    )
    received = across(send)
    new_dual, new_volume, new_projected = call(
        finish_kernel,
        [transmission.shape, volume.shape, transmission.shape],
        (keep, own, received, base, updated, scaled_dual, *spreads),
        [],
        10**6,
    )
    return (new_transmission, new_dual, new_volume, new_projected)


def solution(mesh):
    plane = P(("groups", "angle", "tile"), None, "scan", None)
    cells = P("groups", ("angle", "tile"), "scan", None)
    slots = P(("groups", "angle", "tile"), "scan")
    return jax.shard_map(
        body,
        mesh=mesh,
        in_specs=(
            plane,
            plane,
            plane,
            cells,
            P(("groups", "angle", "tile"), "scan", None, None),
            P("groups", None, None),
            slots,
            slots,
            slots,
            P(None, ("angle", "tile")),
            P(None, ("angle", "tile")),
        ),
        out_specs=(plane, plane, cells, plane),
        check_vma=False,
    )
```

```python
import math

import jax
import jax.numpy as jnp
import numpy as np
from jax import lax
from jax.experimental import pallas as pl
from jax.experimental.pallas import tpu as pltpu
from jax.sharding import PartitionSpec as P


penalty = 4.0
amplitude_step = 0.25
tv_weight = 1.0
smoothing = 0.05
step_size = 0.008

VMEM = pl.BlockSpec(memory_space=pltpu.VMEM)
SMEM = pl.BlockSpec(memory_space=pltpu.SMEM)
HBM = pl.BlockSpec(memory_space=pltpu.MemorySpace.HBM)
LANES = 128
SUBLANES = 8
SPARE_BYTES = 8 << 20


def split(values):
    high = values.astype(jnp.bfloat16)
    return (high, (values - high.astype(jnp.float32)).astype(jnp.bfloat16))


def product(left, right):
    total = jnp.dot(left[0], right[0], preferred_element_type=jnp.float32)
    total += jnp.dot(left[0], right[1], preferred_element_type=jnp.float32)
    return total + jnp.dot(left[1], right[0], preferred_element_type=jnp.float32)


def dft_tables(length):
    grid_ids = np.arange(length)
    radians = (grid_ids[:, None] * grid_ids[None, :] % length) * (2.0 * math.pi / length)
    cosine = np.cos(radians) / math.sqrt(length)
    sine = np.sin(radians) / math.sqrt(length)
    forward = np.block([[cosine, sine], [-sine, cosine]])
    tables = []
    for table in (forward, forward.T):
        high = table.astype(jnp.bfloat16)
        tables += [high, (table - high.astype(np.float64)).astype(jnp.bfloat16)]
    return tables


def tile_is_first():
    return lax.axis_index("tile") == 0


def scan_is_even():
    return lax.rem(lax.axis_index("scan"), 2) == 0


def pack_kernel(plane_ref, volume_ref, packed_ref, slabs, done):
    width = plane_ref.shape[2]
    count = volume_ref.shape[1]
    copies = [
        (plane_ref.at[0, channel], packed_ref.at[channel * width : (channel + 1) * width])
        for channel in range(2)
    ]
    for channel in range(2):
        for row in range(count):
            for side, at in enumerate((0, width - SUBLANES)):
                source = volume_ref.at[channel, row, at : at + SUBLANES]
                copies.append((source, slabs.at[(channel * count + row) * 2 + side]))
    copies = [
        pltpu.make_async_copy(source, target, done.at[number])
        for number, (source, target) in enumerate(copies)
    ]
    for copy in copies:
        copy.start()
    for copy in copies[2:]:
        copy.wait()
    for edge in range(slabs.shape[0]):
        take = 0 if edge % 2 == 0 else SUBLANES - 1
        packed_ref[2 * width + edge : 2 * width + edge + 1] = slabs[edge, take : take + 1]
    for copy in copies[:2]:
        copy.wait()


def has_second():
    scan = lax.axis_index("scan")
    return (scan > 0) & (scan < lax.axis_size("scan") - 1)


def edges_of(plane_a_ref, plane_b_ref, number, width):
    even = scan_is_even()
    at = 2 * width + 2 * number
    first_a, last_a = plane_a_ref[at : at + 1], plane_a_ref[at + 1 : at + 2]
    first_b, last_b = (
        jnp.where(has_second(), plane_b_ref[edge : edge + 1], 0.0) for edge in (at, at + 1)
    )
    return (jnp.where(even, last_b, last_a), jnp.where(even, first_a, first_b))


def slot_masks(rows_ref, columns_ref, count_ref, slot, side):
    lanes = lax.broadcasted_iota(jnp.int32, (side, side), 1)
    sublanes = lax.broadcasted_iota(jnp.int32, (side, side), 0)
    near_lanes = lanes >= rows_ref[0, slot]
    near_columns = sublanes >= columns_ref[0, slot]
    return (near_lanes, near_columns, jnp.full((side, side), slot < count_ref[0, 0]))


def place(totals, part, term, masks, width):
    side = term.shape[0]
    near_lanes, near_columns, live = masks
    inner = live & near_columns
    outer = (live & jnp.logical_not(near_columns))[:width]
    for start, lane_mask in ((0, near_lanes), (side, jnp.logical_not(near_lanes))):
        at = slice(start, start + side)
        totals[part, :side, at] += jnp.where(inner & lane_mask, term, 0.0)
        totals[part, side:, at] += jnp.where(outer & lane_mask[:width], term[:width], 0.0)


def prepare_kernel(count_ref, *refs):
    held = (len(refs) - 13) // 2
    sources = refs[: held + 4]
    probes_ref, density_ref, slots_ref, rays_ref = refs[held + 4 : held + 8]
    targets, done = refs[held + 8 : -1], refs[-1]
    rows_ref, columns_ref, shift_ref, weight_ref = targets[held:]
    copies = [
        pltpu.make_async_copy(source, target, done.at[number])
        for number, (source, target) in enumerate(zip(sources, targets))
    ]
    for copy in copies:
        copy.start()
    probe_ref = targets[0]
    side = probe_ref.shape[1]
    slots = probes_ref.shape[0]
    width = density_ref.shape[1] - side
    density_ref[...] = jnp.zeros_like(density_ref)
    for copy in copies[:1] + copies[held:]:
        copy.wait()
    places = lax.broadcasted_iota(jnp.int32, slots_ref.shape[1:], 0)
    for slot in range(slots):
        live = jnp.where(slot < count_ref[0, 0], 1, 0)
        numbers = jnp.where(places == 0, rows_ref[0, slot], columns_ref[0, slot])
        slots_ref[slot] = jnp.where(places == 2, live, numbers)
        turn = lax.rem(rows_ref[0, slot], side)
        probe = [
            pltpu.roll(pltpu.roll(probe_ref[part], columns_ref[0, slot], 0), turn, 1)
            for part in range(2)
        ]
        for part in range(2):
            probes_ref[slot, part] = probe[part]
        masks = slot_masks(rows_ref, columns_ref, count_ref, slot, side)
        place(density_ref, 0, probe[0] * probe[0] + probe[1] * probe[1], masks, width)
    places = lax.broadcasted_iota(jnp.int32, rays_ref.shape, 0)
    lanes = lax.broadcasted_iota(jnp.int32, rays_ref.shape, 1)
    rays = jnp.zeros(rays_ref.shape, jnp.float32)
    for row in range(shift_ref.shape[0]):
        for angle in range(shift_ref.shape[1]):
            shift = shift_ref[row, angle].astype(jnp.float32)
            here = lanes == angle
            rays = jnp.where(here & (places == 2 * row), shift, rays)
            rays = jnp.where(here & (places == 2 * row + 1), weight_ref[row, angle], rays)
    rays_ref[...] = rays
    for copy in copies[1:held]:
        copy.wait()


def patch_kernel(
    probes_ref,
    density_ref,
    slots_ref,
    plane_ref,
    intensity_ref,
    volume_ref,
    forward_high_ref,
    forward_low_ref,
    inverse_high_ref,
    inverse_low_ref,
    plane_a_ref,
    plane_b_ref,
    own_ref,
    rim_a_ref,
    rim_b_ref,
    row_a_ref,
    row_b_ref,
    wide,
    totals,
):
    width = volume_ref.shape[2]
    slots, _, side, _ = probes_ref.shape
    even = scan_is_even()
    at_a = pl.multiple_of(jnp.where(even, 2 * width, 0), width)
    at_b = pl.multiple_of(jnp.where(even, 0, 2 * width), width)
    for part in range(2):
        at = slice(part * width, (part + 1) * width)
        wide[part, width : 2 * width] = plane_ref[at]
        wide[part, pl.ds(at_a, width)] = plane_a_ref[at]
        wide[part, pl.ds(at_b, width)] = jnp.where(has_second(), plane_b_ref[at], 0.0)
    forward = (forward_high_ref[...], forward_low_ref[...])
    inverse = (inverse_high_ref[...], inverse_low_ref[...])
    waves, masks = [], []
    lanes = lax.broadcasted_iota(jnp.int32, (side, side), 1)
    sublanes = lax.broadcasted_iota(jnp.int32, (side, side), 0)
    for slot in range(slots):
        probe = probes_ref[slot]
        row, column, live = (
            jnp.broadcast_to(slots_ref[slot, number : number + 1], (side, side))
            for number in range(3)
        )
        near_lanes, near_columns = lanes >= row, sublanes >= column
        masks.append((near_lanes, near_columns, live > 0))
        window = []
        for part in range(2):
            near = jnp.where(near_lanes, wide[part, :side, :side], wide[part, :side, side:])
            wrapped = jnp.where(
                near_lanes[:width], wide[part, side:, :side], wide[part, side:, side:]
            )
            wrapped = jnp.concatenate([wrapped, near[width:]], axis=0)
            window.append(jnp.where(near_columns, near, wrapped))
        wave_real = probe[0] * window[0] - probe[1] * window[1]
        wave_imaginary = probe[0] * window[1] + probe[1] * window[0]
        waves.append(jnp.concatenate([wave_real, wave_imaginary], axis=1))
    half = product(split(jnp.concatenate(waves, axis=0)), inverse)
    half = jnp.concatenate(
        [
            jnp.concatenate(
                [half[slot * side : (slot + 1) * side, part * side : (part + 1) * side] for slot in range(slots)],
                axis=1,
            )
            for part in range(2)
        ],
        axis=0,
    )
    far = product(forward, split(half))
    far_real, far_imaginary = far[:side], far[side:]
    intensity = jnp.concatenate(
        [intensity_ref[0, slot].astype(jnp.float32) for slot in range(slots)], axis=1
    )
    factor = 1.0 - amplitude_step * (
        far_real * far_real + far_imaginary * far_imaginary - intensity
    )
    corrected = jnp.concatenate([far_real * factor, far_imaginary * factor], axis=0)
    half = product(inverse, split(corrected))
    half = jnp.concatenate(
        [
            jnp.concatenate(
                [half[part * side : (part + 1) * side, slot * side : (slot + 1) * side] for part in range(2)],
                axis=1,
            )
            for slot in range(slots)
        ],
        axis=0,
    )
    near = product(split(half), forward)
    totals[:2] = jnp.zeros_like(totals[:2])
    totals[2:] = density_ref[...]
    for slot in range(slots):
        probe = probes_ref[slot]
        near_real = near[slot * side : (slot + 1) * side, :side]
        near_imaginary = near[slot * side : (slot + 1) * side, side:]
        place(totals, 0, probe[0] * near_real + probe[1] * near_imaginary, masks[slot], width)
        place(totals, 1, probe[0] * near_imaginary - probe[1] * near_real, masks[slot], width)
    own_ref[...] = totals[:, width : 2 * width]
    for rim_ref, at in ((rim_a_ref, at_a), (rim_b_ref, at_b)):
        for part in range(totals.shape[0]):
            rim_ref[part * width : (part + 1) * width] = totals[part, pl.ds(at, width)]
    first_tile = tile_is_first()
    count = volume_ref.shape[1]
    for channel in range(2):
        rows = []
        for row in (0, count - 1):
            before, after = edges_of(plane_a_ref, plane_b_ref, channel * count + row, width)
            rows.append((volume_ref[channel, row], jnp.concatenate([before, after], axis=0)))
        for low, row_ref in ((jnp.logical_not(first_tile), row_a_ref), (first_tile, row_b_ref)):
            row_ref[channel, :width] = jnp.where(low, rows[0][0], rows[1][0])
            row_ref[channel, width : width + 2] = jnp.where(low, rows[0][1], rows[1][1])


def fold_kernel(
    own_ref, rim_a_ref, rim_b_ref, projected_ref, dual_ref, rays_ref, too_ref, object_ref, residual_ref
):
    width = own_ref.shape[1]
    second = has_second()
    sums = [
        own_ref[part]
        + rim_a_ref[part * width : (part + 1) * width]
        + jnp.where(second, rim_b_ref[part * width : (part + 1) * width], 0.0)
        for part in range(3)
    ]
    for part in range(2):
        target = projected_ref[0, part]
        dual = dual_ref[0, part]
        updated = (sums[part] + penalty * (target - dual)) / (sums[2] + penalty)
        object_ref[0, part] = updated
        residual_ref[part * width : (part + 1) * width] = target - updated - dual
    residual_ref[2 * width : 2 * width + SUBLANES] = rays_ref[...]
    residual_ref[2 * width + SUBLANES :] = too_ref[...]


def variation_kernel(
    volume_ref, plane_a_ref, plane_b_ref, row_a_ref, row_b_ref, base_ref, padded, norms
):
    width = volume_ref.shape[2]
    length = volume_ref.shape[3]
    count = volume_ref.shape[1]
    margin = 8
    first_tile = tile_is_first()
    place = lax.axis_index("angle") * 2 + lax.axis_index("tile")
    bridged = (place > 0) & (place < 2 * lax.axis_size("angle") - 1)
    lanes = lax.broadcasted_iota(jnp.int32, (width, length), 1)
    first_lane = lanes == 0
    last_lane = lanes == length - 1
    for channel in range(2):
        for row in range(count):
            before, after = edges_of(plane_a_ref, plane_b_ref, channel * count + row, width)
            padded[row + 1, margin : margin + width] = volume_ref[channel, row]
            padded[row + 1, margin - 1 : margin] = before
            padded[row + 1, margin + width : margin + width + 1] = after
        row_a, row_b = row_a_ref[channel], jnp.where(bridged, row_b_ref[channel], 0.0)
        for row, beside in (
            (0, jnp.where(first_tile, row_b, row_a)),
            (count + 1, jnp.where(first_tile, row_a, row_b)),
        ):
            padded[row, margin : margin + width] = beside[:width]
            padded[row, margin - 1 : margin] = beside[width : width + 1]
            padded[row, margin + width : margin + width + 1] = beside[width + 1 : width + 2]
        previous_y = None
        for row in range(count + 1):
            here = padded[row, margin : margin + width]
            along_y = padded[row + 1, margin : margin + width] - here
            along_x = padded[row, margin + 1 : margin + width + 1] - here
            along_z = jnp.where(last_lane, 0.0, pltpu.roll(here, length - 1, 1)) - here
            inverse = lax.rsqrt(
                along_y * along_y + along_x * along_x + along_z * along_z + smoothing * smoothing
            )
            norm_y = along_y * inverse
            if row > 0:
                norm_x = along_x * inverse
                norm_z = along_z * inverse
                corner = padded[row, margin - 1 : margin]
                corner_y = padded[row + 1, margin - 1 : margin] - corner
                corner_x = here[:1] - corner
                corner_z = (
                    jnp.where(last_lane[:1], 0.0, pltpu.roll(corner, length - 1, 1)) - corner
                )
                corner_norm = corner_x * lax.rsqrt(
                    corner_y * corner_y
                    + corner_x * corner_x
                    + corner_z * corner_z
                    + smoothing * smoothing
                )
                norms[margin : margin + width] = norm_x
                norms[margin - 1 : margin] = corner_norm
                behind_x = norms[margin - 1 : margin + width - 1]
                ahead = here * lax.rsqrt(here * here + smoothing * smoothing)
                behind_z = jnp.where(first_lane, ahead, pltpu.roll(norm_z, 1, 1))
                divergence = (
                    norm_y - previous_y + (norm_x - behind_x) + (norm_z - behind_z)
                )
                base_ref[channel, row - 1] = here + (step_size * tv_weight) * divergence
            previous_y = norm_y


def spread_kernel(
    shift_ref, weight_ref, base_ref, beside_ref, keep_ref, send_ref, padded
):
    width = base_ref.shape[2]
    count = base_ref.shape[1]
    columns, tiles = keep_ref.shape[0], lax.axis_size("tile")
    me, tile, scan = lax.axis_index("angle"), lax.axis_index("tile"), lax.axis_index("scan")
    upper = me >= columns // 2
    chunks = [slice(at, at + LANES) for at in range(0, base_ref.shape[3], LANES)]
    exists = jnp.where(upper, scan < lax.axis_size("scan") - 1, scan > 0).astype(jnp.float32)
    own_at = pl.multiple_of(jnp.where(upper, 0, width), width)
    beside_at = pl.multiple_of(jnp.where(upper, width, 0), width)
    for row in range(count):
        for channel in range(2):
            for chunk, at in enumerate(chunks):
                padded[row, channel, chunk, pl.ds(own_at, width)] = base_ref[channel, row, :, at]
                padded[row, channel, chunk, pl.ds(beside_at, width)] = (
                    beside_ref[channel, row, :, at] * exists
                )
    for turn in range(columns):
        for flip, out_ref in ((0, keep_ref), (1, send_ref)):
            angle = lax.rem(me + turn, columns) * tiles + (tile if flip == 0 else 1 - tile)
            for channel in range(2):
                for chunk, at in enumerate(chunks):
                    total = jnp.zeros((width, LANES), jnp.float32)
                    for row in range(count):
                        start = jnp.where(upper, 0, width) + shift_ref[row, angle]
                        fraction = weight_ref[row, angle]
                        total += (1.0 - fraction) * padded[row, channel, chunk, pl.ds(start, width)]
                        total += fraction * padded[row, channel, chunk, pl.ds(start + 1, width)]
                    out_ref[turn, channel, :, at] = total


def operator_kernel(*refs):
    packed_refs, (object_ref, high_ref, low_ref, object_out_ref) = refs[:-4], refs[-4:]
    object_out_ref[...] = object_ref[...]
    tiles = lax.axis_size("tile")
    columns = len(packed_refs)
    rows_out, reach = high_ref.shape[1:]
    width = reach // 3
    count = rows_out // (2 * width) - 1
    me, tile, scan = lax.axis_index("angle"), lax.axis_index("tile"), lax.axis_index("scan")

    def taps(shape, first, table, row, step):
        lanes = lax.broadcasted_iota(jnp.int32, shape, 1)
        sublanes = lax.broadcasted_iota(jnp.int32, shape, 0)
        offset = (lanes - sublanes).astype(jnp.float32) - first
        shift = step * table[2 * row : 2 * row + 1]
        fraction = table[2 * row + 1 : 2 * row + 2]
        return jnp.where(offset == shift, 1.0 - fraction, 0.0) + jnp.where(
            offset == shift + step, fraction, 0.0
        )

    def angle_of(turn, flip):
        return lax.rem(me + turn, columns) * tiles + (tile if flip == 0 else 1 - tile)

    def table_of(turn, flip, angle):
        at = 2 * width + SUBLANES * flip
        tile_of = packed_refs[turn][at : at + SUBLANES]
        lanes = lax.broadcasted_iota(jnp.int32, tile_of.shape, 1)
        return jnp.sum(jnp.where(lanes == angle, tile_of, 0.0), axis=1, keepdims=True)

    cells = lax.broadcasted_iota(jnp.int32, (width, 2 * width), 1)
    forward = []
    backward = [[] for _ in range(columns)]
    for turn in range(columns):
        upper = lax.rem(me + turn, columns) >= columns // 2
        base_at = jnp.where(upper, 0, width)
        first_cell = jnp.where(upper, 0, jnp.where(scan > 0, 0, width))
        end_cell = jnp.where(upper & (scan == lax.axis_size("scan") - 1), width, 2 * width)
        inside = (cells >= first_cell) & (cells < end_cell)
        for flip in range(tiles):
            for row in range(count):
                parts = []
                for own in range(tiles):
                    table = table_of(turn, flip, angle_of(0, own))
                    part = taps((width, 2 * width), base_at.astype(jnp.float32), table, row, 1.0)
                    parts.append(jnp.where(inside, part, 0.0))
                forward.append(jnp.concatenate(parts, axis=0))
                for source in range(columns):
                    table = table_of(turn, flip, angle_of(source, 0))
                    first = (width - base_at).astype(jnp.float32)
                    backward[source].append(taps((2 * width, reach), first, table, row, -1.0))
    left = split(jnp.concatenate(forward, axis=1))
    for source in range(columns):
        both = product(left, split(jnp.concatenate(backward[source], axis=0)))
        blocks = [both]
        for flip in range(tiles):
            for row in range(count):
                table = table_of(0, flip, angle_of(source, 0))
                blocks.append(taps((width, reach), float(width), table, row, -1.0))
        high_ref[source], low_ref[source] = split(jnp.concatenate(blocks, axis=0))


def apply_kernel(here_ref, side_a_ref, side_b_ref, high_ref, low_ref, keep_ref, own_ref, send_ref, wide):
    width = keep_ref.shape[1]
    columns = here_ref.shape[0]
    count = own_ref.shape[1]
    even = scan_is_even()
    at_a = pl.multiple_of(jnp.where(even, 2 * width, 0), width)
    at_b = pl.multiple_of(jnp.where(even, 0, 2 * width), width)
    for source in range(columns):
        for channel in range(2):
            at = slice(channel * width, (channel + 1) * width)
            wide[source, channel, width : 2 * width] = here_ref[source, at]
            wide[source, channel, pl.ds(at_a, width)] = side_a_ref[source, at]
            wide[source, channel, pl.ds(at_b, width)] = jnp.where(
                has_second(), side_b_ref[source, at], 0.0
            )
    for channel in range(2):
        total = 0.0
        for source in range(columns):
            total += product((high_ref[source], low_ref[source]), split(wide[source, channel]))
        keep_ref[channel] = total[:width]
        send_ref[channel * width : (channel + 1) * width] = total[width : 2 * width]
        for row in range(count):
            at = (2 + row) * width
            own_ref[channel, row] = total[at : at + width]
            target = (2 + channel * count + row) * width
            send_ref[target : target + width] = total[at + count * width : at + (count + 1) * width]


def finish_kernel(*refs):
    keep_ref, own_ref, received_ref, base_ref, object_ref, dual_ref = refs[:6]
    spreads, (dual_out_ref, volume_ref, projected_ref) = refs[6:-3], refs[-3:]
    count, width = own_ref.shape[1:3]
    for channel in range(2):
        received = received_ref[channel * width : (channel + 1) * width]
        projection = -step_size * (keep_ref[channel] + received)
        for spread_ref in spreads:
            projection = projection + spread_ref[channel]
        projected_ref[0, channel] = projection
        dual_out_ref[0, channel] = dual_ref[0, channel] + object_ref[0, channel] - projection
        for row in range(count):
            at = (2 + channel * count + row) * width
            descent = own_ref[channel, row] + received_ref[at : at + width]
            volume_ref[channel, row] = base_ref[channel, row] - step_size * descent


def call(
    kernel, shapes, operands, scratch, flops, scalars=0, staged=(), numbers=(), copies=0, kind=jnp.float32, kinds={}
):
    held = sum(operand.nbytes for operand in operands[scalars:] + staged)
    held += 4 * sum(math.prod(shape) for shape in shapes)
    own = 4 * sum(math.prod(shape) for shape in scratch)
    outputs = [
        jax.ShapeDtypeStruct(shape, kinds.get(number, kind)) for number, shape in enumerate(shapes)
    ]
    scratch_shapes = [pltpu.VMEM(shape, jnp.float32) for shape in scratch]
    if staged and not copies:
        outputs += [jax.ShapeDtypeStruct(array.shape, array.dtype) for array in staged]
        copies = len(staged) + len(numbers)
        scratch_shapes += [pltpu.SMEM(array.shape, array.dtype) for array in numbers]
    staged += numbers
    if copies:
        scratch_shapes.append(pltpu.SemaphoreType.DMA((copies,)))
    in_specs = [SMEM] * scalars + [VMEM] * (len(operands) - scalars) + [HBM] * len(staged)
    return pl.pallas_call(
        kernel,
        out_shape=outputs,
        in_specs=in_specs,
        out_specs=[VMEM] * len(outputs),
        scratch_shapes=scratch_shapes,
        compiler_params=pltpu.CompilerParams(vmem_limit_bytes=held + own + SPARE_BYTES),
        cost_estimate=pl.CostEstimate(flops=flops, bytes_accessed=held, transcendentals=0),
    )(*operands, *(pltpu.with_memory_space_constraint(array, pltpu.HBM) for array in staged))


def body(
    transmission,
    scaled_dual,
    projected,
    volume,
    intensities,
    probe_wave,
    slot_first_rows,
    slot_first_columns,
    patch_counts,
    shift_table,
    tap_weight,
):
    width, length = transmission.shape[2:]
    count = volume.shape[1]
    scans, columns, tiles = (lax.axis_size(axis) for axis in ("scan", "angle", "tile"))
    assert scans % 2 == 0 and columns % 2 == 0 and tiles == 2
    rounds = []
    for first in (0, 1):
        pairs = [(i, i + 1) for i in range(first, scans - 1, 2)]
        route = [(s * columns + x, d * columns + x) for s, d in pairs for x in range(columns)]
        route += [(target, source) for source, target in route]
        ends = {i for i in range(scans)} - {i for pair in pairs for i in pair}
        for scan in sorted(ends):
            route += [(scan * columns + x, scan * columns + (x ^ 1)) for x in range(columns)]
        rounds.append(route)
    swap = [(0, 1), (1, 0)]

    def exchange(block, number):
        return lax.ppermute(block, ("scan", "angle"), rounds[number])

    def across(block):
        return lax.ppermute(block, "tile", swap)

    edges = 2 * 2 * count
    (plane,) = call(
        pack_kernel,
        [(2 * width + -(-edges // SUBLANES) * SUBLANES, length)],
        (),
        [(edges, SUBLANES, length)],
        10**5,
        staged=(transmission, volume),
        copies=2 + edges,
    )
    plane_a = exchange(plane, 0)
    plane_b = exchange(plane, 1)
    tables = [jnp.asarray(table) for table in dft_tables(probe_wave.shape[1])]
    slots = slot_first_rows.shape[1]
    side = probe_wave.shape[1]
    probes, density, slot_numbers, rays, _, *held = call(
        prepare_kernel,
        [
            (slots, 2, side, side),
            (1, 3 * width, length),
            (slots, SUBLANES, side),
            (SUBLANES, length),
        ],
        (patch_counts,),
        [],
        10**7,
        1,
        (probe_wave, intensities, volume, *tables),
        (slot_first_rows, slot_first_columns, shift_table.T, tap_weight.T),
        kinds={2: jnp.int32},
    )
    volume_here = held[1]
    turns = [[(i, (i - turn) % columns) for i in range(columns)] for turn in range(columns)]
    rays_too = across(rays)
    own, rim_a, rim_b, row_a, row_b = call(
        patch_kernel,
        [(3, width, length)]
        + [(3 * width, length)] * 2
        + [(2, width + SUBLANES, length)] * 2,
        (probes, density, slot_numbers, plane, *held, plane_a, plane_b),
        [(2, 3 * width, length), (3, 3 * width, length)],
        10**9,
    )
    rim_a = exchange(rim_a, 0)
    rim_b = exchange(rim_b, 1)
    bridge = [(i * tiles + 1, (i + 1) * tiles) for i in range(columns - 1)]
    bridge.append((0, columns * tiles - 1))
    bridge += [(target, source) for source, target in bridge]
    row_b = lax.ppermute(row_b, ("angle", "tile"), bridge)
    row_a = across(row_a)
    updated, residual = call(
        fold_kernel,
        [transmission.shape, (2 * width + 2 * SUBLANES, length)],
        (own, rim_a, rim_b, projected, scaled_dual, rays, rays_too),
        [],
        10**6,
    )
    by_column = [residual]
    for turn in range(1, columns):
        by_column.append(lax.ppermute(residual, "angle", turns[turn]))
    (base,) = call(
        variation_kernel,
        [volume.shape],
        (volume_here, plane_a, plane_b, row_a, row_b),
        [(count + 2, width + 16, length), (width + 16, length)],
        10**7,
    )
    route = []
    for scan in range(scans):
        for column in range(columns):
            lower = column < columns // 2
            target = scan + 1 if lower else scan - 1
            turned = column
            if not 0 <= target < scans:
                target, turned = scan, (column + columns // 2) % columns
            route.append((scan * columns + column, target * columns + turned))
    beside = lax.ppermute(base, ("scan", "angle"), route)
    here = jnp.stack(by_column)
    side_a = exchange(here, 0)
    side_b = exchange(here, 1)
    high, low, new_transmission = call(
        operator_kernel,
        [(columns, (2 + 2 * count) * width, 3 * width)] * 2 + [transmission.shape],
        (*by_column, updated),
        [],
        10**8,
        kind=jnp.bfloat16,
        kinds={2: jnp.float32},
    )
    block = (columns, 2, width, length)
    keep, send = call(
        spread_kernel,
        [block, block],
        (shift_table.T, tap_weight.T, base, beside),
        [(count, 2, length // LANES, 2 * width, LANES)],
        10**7,
        2,
    )
    received = across(send)
    spreads = [keep[0], received[0]]
    for turn in range(1, columns):
        route = [(i, (i + turn) % columns) for i in range(columns)]
        spreads.append(lax.ppermute(keep[turn] + received[turn], "angle", route))
    keep, own, send = call(
        apply_kernel,
        [(2, width, length), volume.shape, ((2 + 2 * count) * width, length)],
        (here, side_a, side_b, high, low),
        [(columns, 2, 3 * width, length)],
        10**9,
    )
    received = across(send)
    new_dual, new_volume, new_projected = call(
        finish_kernel,
        [transmission.shape, volume.shape, transmission.shape],
        (keep, own, received, base, updated, scaled_dual, *spreads),
        [],
        10**6,
    )
    return (new_transmission, new_dual, new_volume, new_projected)


def solution(mesh):
    plane = P(("groups", "angle", "tile"), None, "scan", None)
    cells = P("groups", ("angle", "tile"), "scan", None)
    slots = P(("groups", "angle", "tile"), "scan")
    return jax.shard_map(
        body,
        mesh=mesh,
        in_specs=(
            plane,
            plane,
            plane,
            cells,
            P(("groups", "angle", "tile"), "scan", None, None),
            P("groups", None, None),
            slots,
            slots,
            slots,
            P(None, ("angle", "tile")),
            P(None, ("angle", "tile")),
        ),
        out_specs=(plane, plane, cells, plane),
        check_vma=False,
    )
```

```python
import math

import jax
import jax.numpy as jnp
import numpy as np
from jax import lax
from jax.experimental import pallas as pl
from jax.experimental.pallas import tpu as pltpu
from jax.sharding import PartitionSpec as P


penalty = 4.0
amplitude_step = 0.25
tv_weight = 1.0
smoothing = 0.05
step_size = 0.008

VMEM = pl.BlockSpec(memory_space=pltpu.VMEM)
SMEM = pl.BlockSpec(memory_space=pltpu.SMEM)
HBM = pl.BlockSpec(memory_space=pltpu.MemorySpace.HBM)
LANES = 128
SUBLANES = 8
SPARE_BYTES = 8 << 20


def split(values):
    high = values.astype(jnp.bfloat16)
    return (high, (values - high.astype(jnp.float32)).astype(jnp.bfloat16))


def product(left, right):
    total = jnp.dot(left[0], right[0], preferred_element_type=jnp.float32)
    total += jnp.dot(left[0], right[1], preferred_element_type=jnp.float32)
    return total + jnp.dot(left[1], right[0], preferred_element_type=jnp.float32)


def dft_tables(length):
    grid_ids = np.arange(length)
    radians = (grid_ids[:, None] * grid_ids[None, :] % length) * (2.0 * math.pi / length)
    cosine = np.cos(radians) / math.sqrt(length)
    sine = np.sin(radians) / math.sqrt(length)
    forward = np.block([[cosine, sine], [-sine, cosine]])
    tables = []
    for table in (forward, forward.T):
        high = table.astype(jnp.bfloat16)
        tables += [high, (table - high.astype(np.float64)).astype(jnp.bfloat16)]
    return tables


def tile_is_first():
    return lax.axis_index("tile") == 0


def scan_is_even():
    return lax.rem(lax.axis_index("scan"), 2) == 0


def pack_kernel(plane_ref, volume_ref, packed_ref, slabs, done):
    width = plane_ref.shape[2]
    count = volume_ref.shape[1]
    copies = [
        (plane_ref.at[0, channel], packed_ref.at[channel * width : (channel + 1) * width])
        for channel in range(2)
    ]
    for channel in range(2):
        for row in range(count):
            for side, at in enumerate((0, width - SUBLANES)):
                source = volume_ref.at[channel, row, at : at + SUBLANES]
                copies.append((source, slabs.at[(channel * count + row) * 2 + side]))
    copies = [
        pltpu.make_async_copy(source, target, done.at[number])
        for number, (source, target) in enumerate(copies)
    ]
    for copy in copies:
        copy.start()
    for copy in copies[2:]:
        copy.wait()
    for edge in range(slabs.shape[0]):
        take = 0 if edge % 2 == 0 else SUBLANES - 1
        packed_ref[2 * width + edge : 2 * width + edge + 1] = slabs[edge, take : take + 1]
    for copy in copies[:2]:
        copy.wait()


def has_second():
    scan = lax.axis_index("scan")
    return (scan > 0) & (scan < lax.axis_size("scan") - 1)


def edges_of(plane_a_ref, plane_b_ref, number, width):
    even = scan_is_even()
    at = 2 * width + 2 * number
    first_a, last_a = plane_a_ref[at : at + 1], plane_a_ref[at + 1 : at + 2]
    first_b, last_b = (
        jnp.where(has_second(), plane_b_ref[edge : edge + 1], 0.0) for edge in (at, at + 1)
    )
    return (jnp.where(even, last_b, last_a), jnp.where(even, first_a, first_b))


def slot_masks(rows_ref, columns_ref, count_ref, slot, side):
    lanes = lax.broadcasted_iota(jnp.int32, (side, side), 1)
    sublanes = lax.broadcasted_iota(jnp.int32, (side, side), 0)
    near_lanes = lanes >= rows_ref[0, slot]
    near_columns = sublanes >= columns_ref[0, slot]
    return (near_lanes, near_columns, jnp.full((side, side), slot < count_ref[0, 0]))


def place(totals, part, term, masks, width):
    side = term.shape[0]
    near_lanes, near_columns, live = masks
    inner = live & near_columns
    outer = (live & jnp.logical_not(near_columns))[:width]
    for start, lane_mask in ((0, near_lanes), (side, jnp.logical_not(near_lanes))):
        at = slice(start, start + side)
        totals[part, :side, at] += jnp.where(inner & lane_mask, term, 0.0)
        totals[part, side:, at] += jnp.where(outer & lane_mask[:width], term[:width], 0.0)


def prepare_kernel(count_ref, *refs):
    held = (len(refs) - 13) // 2
    sources = refs[: held + 4]
    probes_ref, density_ref, slots_ref, rays_ref = refs[held + 4 : held + 8]
    targets, done = refs[held + 8 : -1], refs[-1]
    rows_ref, columns_ref, shift_ref, weight_ref = targets[held:]
    copies = [
        pltpu.make_async_copy(source, target, done.at[number])
        for number, (source, target) in enumerate(zip(sources, targets))
    ]
    for copy in copies:
        copy.start()
    probe_ref = targets[0]
    side = probe_ref.shape[1]
    slots = probes_ref.shape[0]
    width = density_ref.shape[1] - side
    density_ref[...] = jnp.zeros_like(density_ref)
    for copy in copies[:1] + copies[held:]:
        copy.wait()
    places = lax.broadcasted_iota(jnp.int32, slots_ref.shape[1:], 0)
    for slot in range(slots):
        live = jnp.where(slot < count_ref[0, 0], 1, 0)
        numbers = jnp.where(places == 0, rows_ref[0, slot], columns_ref[0, slot])
        slots_ref[slot] = jnp.where(places == 2, live, numbers)
        turn = lax.rem(rows_ref[0, slot], side)
        probe = [
            pltpu.roll(pltpu.roll(probe_ref[part], columns_ref[0, slot], 0), turn, 1)
            for part in range(2)
        ]
        for part in range(2):
            probes_ref[slot, part] = probe[part]
        masks = slot_masks(rows_ref, columns_ref, count_ref, slot, side)
        place(density_ref, 0, probe[0] * probe[0] + probe[1] * probe[1], masks, width)
    places = lax.broadcasted_iota(jnp.int32, rays_ref.shape, 0)
    lanes = lax.broadcasted_iota(jnp.int32, rays_ref.shape, 1)
    rays = jnp.zeros(rays_ref.shape, jnp.float32)
    for row in range(shift_ref.shape[0]):
        for angle in range(shift_ref.shape[1]):
            shift = shift_ref[row, angle].astype(jnp.float32)
            here = lanes == angle
            rays = jnp.where(here & (places == 2 * row), shift, rays)
            rays = jnp.where(here & (places == 2 * row + 1), weight_ref[row, angle], rays)
    rays_ref[...] = rays
    for copy in copies[1:held]:
        copy.wait()


def patch_kernel(
    probes_ref,
    density_ref,
    slots_ref,
    plane_ref,
    intensity_ref,
    volume_ref,
    forward_high_ref,
    forward_low_ref,
    inverse_high_ref,
    inverse_low_ref,
    plane_a_ref,
    plane_b_ref,
    own_ref,
    rim_a_ref,
    rim_b_ref,
    row_a_ref,
    row_b_ref,
    wide,
    totals,
):
    width = volume_ref.shape[2]
    slots, _, side, _ = probes_ref.shape
    even = scan_is_even()
    at_a = pl.multiple_of(jnp.where(even, 2 * width, 0), width)
    at_b = pl.multiple_of(jnp.where(even, 0, 2 * width), width)
    for part in range(2):
        at = slice(part * width, (part + 1) * width)
        wide[part, width : 2 * width] = plane_ref[at]
        wide[part, pl.ds(at_a, width)] = plane_a_ref[at]
        wide[part, pl.ds(at_b, width)] = jnp.where(has_second(), plane_b_ref[at], 0.0)
    forward = (forward_high_ref[...], forward_low_ref[...])
    inverse = (inverse_high_ref[...], inverse_low_ref[...])
    waves, masks = [], []
    lanes = lax.broadcasted_iota(jnp.int32, (side, side), 1)
    sublanes = lax.broadcasted_iota(jnp.int32, (side, side), 0)
    for slot in range(slots):
        probe = probes_ref[slot]
        row, column, live = (
            jnp.broadcast_to(slots_ref[slot, number : number + 1], (side, side))
            for number in range(3)
        )
        near_lanes, near_columns = lanes >= row, sublanes >= column
        masks.append((near_lanes, near_columns, live > 0))
        window = []
        for part in range(2):
            near = jnp.where(near_lanes, wide[part, :side, :side], wide[part, :side, side:])
            wrapped = jnp.where(
                near_lanes[:width], wide[part, side:, :side], wide[part, side:, side:]
            )
            wrapped = jnp.concatenate([wrapped, near[width:]], axis=0)
            window.append(jnp.where(near_columns, near, wrapped))
        wave_real = probe[0] * window[0] - probe[1] * window[1]
        wave_imaginary = probe[0] * window[1] + probe[1] * window[0]
        waves.append(jnp.concatenate([wave_real, wave_imaginary], axis=1))
    half = product(split(jnp.concatenate(waves, axis=0)), inverse)
    half = jnp.concatenate(
        [
            jnp.concatenate(
                [half[slot * side : (slot + 1) * side, part * side : (part + 1) * side] for slot in range(slots)],
                axis=1,
            )
            for part in range(2)
        ],
        axis=0,
    )
    far = product(forward, split(half))
    far_real, far_imaginary = far[:side], far[side:]
    intensity = jnp.concatenate(
        [intensity_ref[0, slot].astype(jnp.float32) for slot in range(slots)], axis=1
    )
    factor = 1.0 - amplitude_step * (
        far_real * far_real + far_imaginary * far_imaginary - intensity
    )
    corrected = jnp.concatenate([far_real * factor, far_imaginary * factor], axis=0)
    half = product(inverse, split(corrected))
    half = jnp.concatenate(
        [
            jnp.concatenate(
                [half[part * side : (part + 1) * side, slot * side : (slot + 1) * side] for part in range(2)],
                axis=1,
            )
            for slot in range(slots)
        ],
        axis=0,
    )
    near = product(split(half), forward)
    totals[:2] = jnp.zeros_like(totals[:2])
    totals[2:] = density_ref[...]
    for slot in range(slots):
        probe = probes_ref[slot]
        near_real = near[slot * side : (slot + 1) * side, :side]
        near_imaginary = near[slot * side : (slot + 1) * side, side:]
        place(totals, 0, probe[0] * near_real + probe[1] * near_imaginary, masks[slot], width)
        place(totals, 1, probe[0] * near_imaginary - probe[1] * near_real, masks[slot], width)
    own_ref[...] = totals[:, width : 2 * width]
    for rim_ref, at in ((rim_a_ref, at_a), (rim_b_ref, at_b)):
        for part in range(totals.shape[0]):
            rim_ref[part * width : (part + 1) * width] = totals[part, pl.ds(at, width)]
    first_tile = tile_is_first()
    count = volume_ref.shape[1]
    for channel in range(2):
        rows = []
        for row in (0, count - 1):
            before, after = edges_of(plane_a_ref, plane_b_ref, channel * count + row, width)
            rows.append((volume_ref[channel, row], jnp.concatenate([before, after], axis=0)))
        for low, row_ref in ((jnp.logical_not(first_tile), row_a_ref), (first_tile, row_b_ref)):
            row_ref[channel, :width] = jnp.where(low, rows[0][0], rows[1][0])
            row_ref[channel, width : width + 2] = jnp.where(low, rows[0][1], rows[1][1])


def fold_kernel(
    own_ref, rim_a_ref, rim_b_ref, projected_ref, dual_ref, rays_ref, too_ref, object_ref, residual_ref
):
    width = own_ref.shape[1]
    second = has_second()
    sums = [
        own_ref[part]
        + rim_a_ref[part * width : (part + 1) * width]
        + jnp.where(second, rim_b_ref[part * width : (part + 1) * width], 0.0)
        for part in range(3)
    ]
    for part in range(2):
        target = projected_ref[0, part]
        dual = dual_ref[0, part]
        updated = (sums[part] + penalty * (target - dual)) / (sums[2] + penalty)
        object_ref[0, part] = updated
        residual_ref[part * width : (part + 1) * width] = target - updated - dual
    residual_ref[2 * width : 2 * width + SUBLANES] = rays_ref[...]
    residual_ref[2 * width + SUBLANES :] = too_ref[...]


def variation_kernel(
    volume_ref, plane_a_ref, plane_b_ref, row_a_ref, row_b_ref, base_ref, padded, norms
):
    width = volume_ref.shape[2]
    length = volume_ref.shape[3]
    count = volume_ref.shape[1]
    margin = 8
    first_tile = tile_is_first()
    place = lax.axis_index("angle") * 2 + lax.axis_index("tile")
    bridged = (place > 0) & (place < 2 * lax.axis_size("angle") - 1)
    lanes = lax.broadcasted_iota(jnp.int32, (width, length), 1)
    first_lane = lanes == 0
    last_lane = lanes == length - 1
    for channel in range(2):
        for row in range(count):
            before, after = edges_of(plane_a_ref, plane_b_ref, channel * count + row, width)
            padded[row + 1, margin : margin + width] = volume_ref[channel, row]
            padded[row + 1, margin - 1 : margin] = before
            padded[row + 1, margin + width : margin + width + 1] = after
        row_a, row_b = row_a_ref[channel], jnp.where(bridged, row_b_ref[channel], 0.0)
        for row, beside in (
            (0, jnp.where(first_tile, row_b, row_a)),
            (count + 1, jnp.where(first_tile, row_a, row_b)),
        ):
            padded[row, margin : margin + width] = beside[:width]
            padded[row, margin - 1 : margin] = beside[width : width + 1]
            padded[row, margin + width : margin + width + 1] = beside[width + 1 : width + 2]
        previous_y = None
        for row in range(count + 1):
            here = padded[row, margin : margin + width]
            along_y = padded[row + 1, margin : margin + width] - here
            along_x = padded[row, margin + 1 : margin + width + 1] - here
            along_z = jnp.where(last_lane, 0.0, pltpu.roll(here, length - 1, 1)) - here
            inverse = lax.rsqrt(
                along_y * along_y + along_x * along_x + along_z * along_z + smoothing * smoothing
            )
            norm_y = along_y * inverse
            if row > 0:
                norm_x = along_x * inverse
                norm_z = along_z * inverse
                corner = padded[row, margin - 1 : margin]
                corner_y = padded[row + 1, margin - 1 : margin] - corner
                corner_x = here[:1] - corner
                corner_z = (
                    jnp.where(last_lane[:1], 0.0, pltpu.roll(corner, length - 1, 1)) - corner
                )
                corner_norm = corner_x * lax.rsqrt(
                    corner_y * corner_y
                    + corner_x * corner_x
                    + corner_z * corner_z
                    + smoothing * smoothing
                )
                norms[margin : margin + width] = norm_x
                norms[margin - 1 : margin] = corner_norm
                behind_x = norms[margin - 1 : margin + width - 1]
                ahead = here * lax.rsqrt(here * here + smoothing * smoothing)
                behind_z = jnp.where(first_lane, ahead, pltpu.roll(norm_z, 1, 1))
                divergence = (
                    norm_y - previous_y + (norm_x - behind_x) + (norm_z - behind_z)
                )
                base_ref[channel, row - 1] = here + (step_size * tv_weight) * divergence
            previous_y = norm_y


def spread_kernel(
    shift_ref, weight_ref, base_ref, beside_ref, keep_ref, send_ref, padded
):
    width = base_ref.shape[2]
    count = base_ref.shape[1]
    columns, tiles = keep_ref.shape[0], lax.axis_size("tile")
    me, tile, scan = lax.axis_index("angle"), lax.axis_index("tile"), lax.axis_index("scan")
    upper = me >= columns // 2
    chunks = [slice(at, at + LANES) for at in range(0, base_ref.shape[3], LANES)]
    exists = jnp.where(upper, scan < lax.axis_size("scan") - 1, scan > 0).astype(jnp.float32)
    own_at = pl.multiple_of(jnp.where(upper, 0, width), width)
    beside_at = pl.multiple_of(jnp.where(upper, width, 0), width)
    for row in range(count):
        for channel in range(2):
            for chunk, at in enumerate(chunks):
                padded[row, channel, chunk, pl.ds(own_at, width)] = base_ref[channel, row, :, at]
                padded[row, channel, chunk, pl.ds(beside_at, width)] = (
                    beside_ref[channel, row, :, at] * exists
                )
    for turn in range(columns):
        for flip, out_ref in ((0, keep_ref), (1, send_ref)):
            angle = lax.rem(me + turn, columns) * tiles + (tile if flip == 0 else 1 - tile)
            for channel in range(2):
                for chunk, at in enumerate(chunks):
                    total = jnp.zeros((width, LANES), jnp.float32)
                    for row in range(count):
                        start = jnp.where(upper, 0, width) + shift_ref[row, angle]
                        fraction = weight_ref[row, angle]
                        total += (1.0 - fraction) * padded[row, channel, chunk, pl.ds(start, width)]
                        total += fraction * padded[row, channel, chunk, pl.ds(start + 1, width)]
                    out_ref[turn, channel, :, at] = total


def operator_kernel(*refs):
    packed_refs, (object_ref, high_ref, low_ref, object_out_ref) = refs[:-4], refs[-4:]
    object_out_ref[...] = object_ref[...]
    tiles = lax.axis_size("tile")
    columns = len(packed_refs)
    rows_out, reach = high_ref.shape[1:]
    width = reach // 3
    count = rows_out // (2 * width) - 1
    me, tile, scan = lax.axis_index("angle"), lax.axis_index("tile"), lax.axis_index("scan")

    def taps(shape, first, table, row, step):
        lanes = lax.broadcasted_iota(jnp.int32, shape, 1)
        sublanes = lax.broadcasted_iota(jnp.int32, shape, 0)
        offset = (lanes - sublanes).astype(jnp.float32) - first
        shift = step * table[2 * row : 2 * row + 1]
        fraction = table[2 * row + 1 : 2 * row + 2]
        return jnp.where(offset == shift, 1.0 - fraction, 0.0) + jnp.where(
            offset == shift + step, fraction, 0.0
        )

    def angle_of(turn, flip):
        return lax.rem(me + turn, columns) * tiles + (tile if flip == 0 else 1 - tile)

    def table_of(turn, flip, angle):
        at = 2 * width + SUBLANES * flip
        tile_of = packed_refs[turn][at : at + SUBLANES]
        lanes = lax.broadcasted_iota(jnp.int32, tile_of.shape, 1)
        return jnp.sum(jnp.where(lanes == angle, tile_of, 0.0), axis=1, keepdims=True)

    cells = lax.broadcasted_iota(jnp.int32, (width, 2 * width), 1)
    forward = []
    backward = [[] for _ in range(columns)]
    for turn in range(columns):
        upper = lax.rem(me + turn, columns) >= columns // 2
        base_at = jnp.where(upper, 0, width)
        first_cell = jnp.where(upper, 0, jnp.where(scan > 0, 0, width))
        end_cell = jnp.where(upper & (scan == lax.axis_size("scan") - 1), width, 2 * width)
        inside = (cells >= first_cell) & (cells < end_cell)
        for flip in range(tiles):
            for row in range(count):
                parts = []
                for own in range(tiles):
                    table = table_of(turn, flip, angle_of(0, own))
                    part = taps((width, 2 * width), base_at.astype(jnp.float32), table, row, 1.0)
                    parts.append(jnp.where(inside, part, 0.0))
                forward.append(jnp.concatenate(parts, axis=0))
                for source in range(columns):
                    table = table_of(turn, flip, angle_of(source, 0))
                    first = (width - base_at).astype(jnp.float32)
                    backward[source].append(taps((2 * width, reach), first, table, row, -1.0))
    left = split(jnp.concatenate(forward, axis=1))
    for source in range(columns):
        both = product(left, split(jnp.concatenate(backward[source], axis=0)))
        blocks = [both]
        for flip in range(tiles):
            for row in range(count):
                table = table_of(0, flip, angle_of(source, 0))
                blocks.append(taps((width, reach), float(width), table, row, -1.0))
        high_ref[source], low_ref[source] = split(jnp.concatenate(blocks, axis=0))


def apply_kernel(here_ref, side_a_ref, side_b_ref, high_ref, low_ref, keep_ref, own_ref, send_ref, wide):
    width = keep_ref.shape[1]
    columns = here_ref.shape[0]
    count = own_ref.shape[1]
    even = scan_is_even()
    at_a = pl.multiple_of(jnp.where(even, 2 * width, 0), width)
    at_b = pl.multiple_of(jnp.where(even, 0, 2 * width), width)
    for source in range(columns):
        for channel in range(2):
            at = slice(channel * width, (channel + 1) * width)
            wide[source, channel, width : 2 * width] = here_ref[source, at]
            wide[source, channel, pl.ds(at_a, width)] = side_a_ref[source, at]
            wide[source, channel, pl.ds(at_b, width)] = jnp.where(
                has_second(), side_b_ref[source, at], 0.0
            )
    for channel in range(2):
        total = 0.0
        for source in range(columns):
            total += product((high_ref[source], low_ref[source]), split(wide[source, channel]))
        keep_ref[channel] = total[:width]
        send_ref[channel * width : (channel + 1) * width] = total[width : 2 * width]
        for row in range(count):
            at = (2 + row) * width
            own_ref[channel, row] = total[at : at + width]
            target = (2 + channel * count + row) * width
            send_ref[target : target + width] = total[at + count * width : at + (count + 1) * width]


def finish_kernel(*refs):
    keep_ref, own_ref, received_ref, base_ref, object_ref, dual_ref = refs[:6]
    spreads, (dual_out_ref, volume_ref, projected_ref) = refs[6:-3], refs[-3:]
    count, width = own_ref.shape[1:3]
    for channel in range(2):
        received = received_ref[channel * width : (channel + 1) * width]
        projection = -step_size * (keep_ref[channel] + received)
        for spread_ref in spreads:
            projection = projection + spread_ref[channel]
        projected_ref[0, channel] = projection
        dual_out_ref[0, channel] = dual_ref[0, channel] + object_ref[0, channel] - projection
        for row in range(count):
            at = (2 + channel * count + row) * width
            descent = own_ref[channel, row] + received_ref[at : at + width]
            volume_ref[channel, row] = base_ref[channel, row] - step_size * descent


def call(
    kernel, shapes, operands, scratch, flops, scalars=0, staged=(), numbers=(), copies=0, kind=jnp.float32, kinds={}
):
    held = sum(operand.nbytes for operand in operands[scalars:] + staged)
    held += 4 * sum(math.prod(shape) for shape in shapes)
    own = 4 * sum(math.prod(shape) for shape in scratch)
    outputs = [
        jax.ShapeDtypeStruct(shape, kinds.get(number, kind)) for number, shape in enumerate(shapes)
    ]
    scratch_shapes = [pltpu.VMEM(shape, jnp.float32) for shape in scratch]
    if staged and not copies:
        outputs += [jax.ShapeDtypeStruct(array.shape, array.dtype) for array in staged]
        copies = len(staged) + len(numbers)
        scratch_shapes += [pltpu.SMEM(array.shape, array.dtype) for array in numbers]
    staged += numbers
    if copies:
        scratch_shapes.append(pltpu.SemaphoreType.DMA((copies,)))
    in_specs = [SMEM] * scalars + [VMEM] * (len(operands) - scalars) + [HBM] * len(staged)
    return pl.pallas_call(
        kernel,
        out_shape=outputs,
        in_specs=in_specs,
        out_specs=[VMEM] * len(outputs),
        scratch_shapes=scratch_shapes,
        compiler_params=pltpu.CompilerParams(vmem_limit_bytes=held + own + SPARE_BYTES),
        cost_estimate=pl.CostEstimate(flops=flops, bytes_accessed=held, transcendentals=0),
    )(*operands, *(pltpu.with_memory_space_constraint(array, pltpu.HBM) for array in staged))


def body(
    transmission,
    scaled_dual,
    projected,
    volume,
    intensities,
    probe_wave,
    slot_first_rows,
    slot_first_columns,
    patch_counts,
    shift_table,
    tap_weight,
):
    width, length = transmission.shape[2:]
    count = volume.shape[1]
    scans, columns, tiles = (lax.axis_size(axis) for axis in ("scan", "angle", "tile"))
    assert scans % 2 == 0 and columns % 2 == 0 and tiles == 2 and lax.axis_size("groups") % 2 == 0
    rounds = []
    for first in (0, 1):
        pairs = [(i, i + 1) for i in range(first, scans - 1, 2)]
        route = [(s * tiles + t, d * tiles + t) for s, d in pairs for t in range(tiles)]
        route += [(target, source) for source, target in route]
        ends = {i for i in range(scans)} - {i for pair in pairs for i in pair}
        for scan in sorted(ends):
            route += [(scan * tiles + t, scan * tiles + 1 - t) for t in range(tiles)]
        rounds.append(route)
    swap = [(0, 1), (1, 0)]

    def exchange(block, number):
        return lax.ppermute(block, ("scan", "tile"), rounds[number])

    def across(block):
        return lax.ppermute(block, "tile", swap)

    edges = 2 * 2 * count
    (plane,) = call(
        pack_kernel,
        [(2 * width + -(-edges // SUBLANES) * SUBLANES, length)],
        (),
        [(edges, SUBLANES, length)],
        10**5,
        staged=(transmission, volume),
        copies=2 + edges,
    )
    plane_a = exchange(plane, 0)
    plane_b = exchange(plane, 1)
    tables = [jnp.asarray(table) for table in dft_tables(probe_wave.shape[1])]
    slots = slot_first_rows.shape[1]
    side = probe_wave.shape[1]
    probes, density, slot_numbers, rays, _, *held = call(
        prepare_kernel,
        [
            (slots, 2, side, side),
            (1, 3 * width, length),
            (slots, SUBLANES, side),
            (SUBLANES, length),
        ],
        (patch_counts,),
        [],
        10**7,
        1,
        (probe_wave, intensities, volume, *tables),
        (slot_first_rows, slot_first_columns, shift_table.T, tap_weight.T),
        kinds={2: jnp.int32},
    )
    volume_here = held[1]
    turns = [[(i, (i - turn) % columns) for i in range(columns)] for turn in range(columns)]
    rays_too = across(rays)
    own, rim_a, rim_b, row_a, row_b = call(
        patch_kernel,
        [(3, width, length)]
        + [(3 * width, length)] * 2
        + [(2, width + SUBLANES, length)] * 2,
        (probes, density, slot_numbers, plane, *held, plane_a, plane_b),
        [(2, 3 * width, length), (3, 3 * width, length)],
        10**9,
    )
    rim_a = exchange(rim_a, 0)
    rim_b = exchange(rim_b, 1)
    per_group, groups = columns * tiles, lax.axis_size("groups")
    bridge = []
    for group in range(groups):
        at = group * per_group
        pairs = [(at + i * tiles + 1, at + (i + 1) * tiles) for i in range(columns - 1)]
        bridge += pairs + [(target, source) for source, target in pairs]
        beyond = (groups - 1 - group) * per_group
        for outer in (0, per_group - 1):
            bridge.append((at + outer, beyond + outer))
    row_b = lax.ppermute(row_b, ("groups", "angle", "tile"), bridge)
    row_a = across(row_a)
    updated, residual = call(
        fold_kernel,
        [transmission.shape, (2 * width + 2 * SUBLANES, length)],
        (own, rim_a, rim_b, projected, scaled_dual, rays, rays_too),
        [],
        10**6,
    )
    by_column = [residual]
    for turn in range(1, columns):
        by_column.append(lax.ppermute(residual, "angle", turns[turn]))
    (base,) = call(
        variation_kernel,
        [volume.shape],
        (volume_here, plane_a, plane_b, row_a, row_b),
        [(count + 2, width + 16, length), (width + 16, length)],
        10**7,
    )
    route = []
    for scan in range(scans):
        for column in range(columns):
            lower = column < columns // 2
            target = scan + 1 if lower else scan - 1
            turned = column
            if not 0 <= target < scans:
                target, turned = scan, (column + columns // 2) % columns
            route.append((scan * columns + column, target * columns + turned))
    beside = lax.ppermute(base, ("scan", "angle"), route)
    here = jnp.stack(by_column)
    side_a = exchange(here, 0)
    side_b = exchange(here, 1)
    high, low, new_transmission = call(
        operator_kernel,
        [(columns, (2 + 2 * count) * width, 3 * width)] * 2 + [transmission.shape],
        (*by_column, updated),
        [],
        10**8,
        kind=jnp.bfloat16,
        kinds={2: jnp.float32},
    )
    block = (columns, 2, width, length)
    keep, send = call(
        spread_kernel,
        [block, block],
        (shift_table.T, tap_weight.T, base, beside),
        [(count, 2, length // LANES, 2 * width, LANES)],
        10**7,
        2,
    )
    received = across(send)
    spreads = [keep[0], received[0]]
    for turn in range(1, columns):
        route = [(i, (i + turn) % columns) for i in range(columns)]
        spreads.append(lax.ppermute(keep[turn] + received[turn], "angle", route))
    keep, own, send = call(
        apply_kernel,
        [(2, width, length), volume.shape, ((2 + 2 * count) * width, length)],
        (here, side_a, side_b, high, low),
        [(columns, 2, 3 * width, length)],
        10**9,
    )
    received = across(send)
    new_dual, new_volume, new_projected = call(
        finish_kernel,
        [transmission.shape, volume.shape, transmission.shape],
        (keep, own, received, base, updated, scaled_dual, *spreads),
        [],
        10**6,
    )
    return (new_transmission, new_dual, new_volume, new_projected)


def solution(mesh):
    plane = P(("groups", "angle", "tile"), None, "scan", None)
    cells = P("groups", ("angle", "tile"), "scan", None)
    slots = P(("groups", "angle", "tile"), "scan")
    return jax.shard_map(
        body,
        mesh=mesh,
        in_specs=(
            plane,
            plane,
            plane,
            cells,
            P(("groups", "angle", "tile"), "scan", None, None),
            P("groups", None, None),
            slots,
            slots,
            slots,
            P(None, ("angle", "tile")),
            P(None, ("angle", "tile")),
        ),
        out_specs=(plane, plane, cells, plane),
        check_vma=False,
    )
```

```python
import math

import jax
import jax.numpy as jnp
import numpy as np
from jax import lax
from jax.experimental import pallas as pl
from jax.experimental.pallas import tpu as pltpu
from jax.sharding import PartitionSpec as P


penalty = 4.0
amplitude_step = 0.25
tv_weight = 1.0
smoothing = 0.05
step_size = 0.008

VMEM = pl.BlockSpec(memory_space=pltpu.VMEM)
SMEM = pl.BlockSpec(memory_space=pltpu.SMEM)
HBM = pl.BlockSpec(memory_space=pltpu.MemorySpace.HBM)
LANES = 128
SUBLANES = 8
SPARE_BYTES = 8 << 20


def split(values):
    high = values.astype(jnp.bfloat16)
    return (high, (values - high.astype(jnp.float32)).astype(jnp.bfloat16))


def product(left, right):
    total = jnp.dot(left[0], right[0], preferred_element_type=jnp.float32)
    total += jnp.dot(left[0], right[1], preferred_element_type=jnp.float32)
    return total + jnp.dot(left[1], right[0], preferred_element_type=jnp.float32)


def dft_tables(length):
    grid_ids = np.arange(length)
    radians = (grid_ids[:, None] * grid_ids[None, :] % length) * (2.0 * math.pi / length)
    cosine = np.cos(radians) / math.sqrt(length)
    sine = np.sin(radians) / math.sqrt(length)
    forward = np.block([[cosine, sine], [-sine, cosine]])
    tables = []
    for table in (forward, forward.T):
        high = table.astype(jnp.bfloat16)
        tables += [high, (table - high.astype(np.float64)).astype(jnp.bfloat16)]
    return tables


def tile_is_first():
    return lax.axis_index("tile") == 0


def scan_is_even():
    return lax.rem(lax.axis_index("scan"), 2) == 0


def pack_kernel(plane_ref, volume_ref, packed_ref, slabs, done):
    width = plane_ref.shape[2]
    count = volume_ref.shape[1]
    copies = [
        (plane_ref.at[0, channel], packed_ref.at[channel * width : (channel + 1) * width])
        for channel in range(2)
    ]
    for channel in range(2):
        for row in range(count):
            for side, at in enumerate((0, width - SUBLANES)):
                source = volume_ref.at[channel, row, at : at + SUBLANES]
                copies.append((source, slabs.at[(channel * count + row) * 2 + side]))
    copies = [
        pltpu.make_async_copy(source, target, done.at[number])
        for number, (source, target) in enumerate(copies)
    ]
    for copy in copies:
        copy.start()
    for copy in copies[2:]:
        copy.wait()
    for edge in range(slabs.shape[0]):
        take = 0 if edge % 2 == 0 else SUBLANES - 1
        packed_ref[2 * width + edge : 2 * width + edge + 1] = slabs[edge, take : take + 1]
    for copy in copies[:2]:
        copy.wait()


def has_second():
    scan = lax.axis_index("scan")
    return (scan > 0) & (scan < lax.axis_size("scan") - 1)


def edges_of(plane_a_ref, plane_b_ref, number, width):
    even = scan_is_even()
    at = 2 * width + 2 * number
    first_a, last_a = plane_a_ref[at : at + 1], plane_a_ref[at + 1 : at + 2]
    first_b, last_b = (
        jnp.where(has_second(), plane_b_ref[edge : edge + 1], 0.0) for edge in (at, at + 1)
    )
    return (jnp.where(even, last_b, last_a), jnp.where(even, first_a, first_b))


def slot_masks(rows_ref, columns_ref, count_ref, slot, side):
    lanes = lax.broadcasted_iota(jnp.int32, (side, side), 1)
    sublanes = lax.broadcasted_iota(jnp.int32, (side, side), 0)
    near_lanes = lanes >= rows_ref[0, slot]
    near_columns = sublanes >= columns_ref[0, slot]
    return (near_lanes, near_columns, jnp.full((side, side), slot < count_ref[0, 0]))


def place(totals, part, term, masks, width):
    side = term.shape[0]
    near_lanes, near_columns, live = masks
    inner = live & near_columns
    outer = (live & jnp.logical_not(near_columns))[:width]
    for start, lane_mask in ((0, near_lanes), (side, jnp.logical_not(near_lanes))):
        at = slice(start, start + side)
        totals[part, :side, at] += jnp.where(inner & lane_mask, term, 0.0)
        totals[part, side:, at] += jnp.where(outer & lane_mask[:width], term[:width], 0.0)


def prepare_kernel(count_ref, *refs):
    held = (len(refs) - 13) // 2
    sources = refs[: held + 4]
    probes_ref, density_ref, slots_ref, rays_ref = refs[held + 4 : held + 8]
    targets, done = refs[held + 8 : -1], refs[-1]
    rows_ref, columns_ref, shift_ref, weight_ref = targets[held:]
    copies = [
        pltpu.make_async_copy(source, target, done.at[number])
        for number, (source, target) in enumerate(zip(sources, targets))
    ]
    for copy in copies:
        copy.start()
    probe_ref = targets[0]
    side = probe_ref.shape[1]
    slots = probes_ref.shape[0]
    width = density_ref.shape[1] - side
    density_ref[...] = jnp.zeros_like(density_ref)
    for copy in copies[:1] + copies[held:]:
        copy.wait()
    places = lax.broadcasted_iota(jnp.int32, slots_ref.shape[1:], 0)
    for slot in range(slots):
        live = jnp.where(slot < count_ref[0, 0], 1, 0)
        numbers = jnp.where(places == 0, rows_ref[0, slot], columns_ref[0, slot])
        slots_ref[slot] = jnp.where(places == 2, live, numbers)
        turn = lax.rem(rows_ref[0, slot], side)
        probe = [
            pltpu.roll(pltpu.roll(probe_ref[part], columns_ref[0, slot], 0), turn, 1)
            for part in range(2)
        ]
        for part in range(2):
            probes_ref[slot, part] = probe[part]
        masks = slot_masks(rows_ref, columns_ref, count_ref, slot, side)
        place(density_ref, 0, probe[0] * probe[0] + probe[1] * probe[1], masks, width)
    places = lax.broadcasted_iota(jnp.int32, rays_ref.shape, 0)
    lanes = lax.broadcasted_iota(jnp.int32, rays_ref.shape, 1)
    rays = jnp.zeros(rays_ref.shape, jnp.float32)
    for row in range(shift_ref.shape[0]):
        for angle in range(shift_ref.shape[1]):
            shift = shift_ref[row, angle].astype(jnp.float32)
            here = lanes == angle
            rays = jnp.where(here & (places == 2 * row), shift, rays)
            rays = jnp.where(here & (places == 2 * row + 1), weight_ref[row, angle], rays)
    rays_ref[...] = rays
    for copy in copies[1:held]:
        copy.wait()


def patch_kernel(
    probes_ref,
    density_ref,
    slots_ref,
    plane_ref,
    intensity_ref,
    volume_ref,
    forward_high_ref,
    forward_low_ref,
    inverse_high_ref,
    inverse_low_ref,
    plane_a_ref,
    plane_b_ref,
    own_ref,
    rim_a_ref,
    rim_b_ref,
    row_a_ref,
    row_b_ref,
    wide,
    totals,
):
    width = volume_ref.shape[2]
    slots, _, side, _ = probes_ref.shape
    even = scan_is_even()
    at_a = pl.multiple_of(jnp.where(even, 2 * width, 0), width)
    at_b = pl.multiple_of(jnp.where(even, 0, 2 * width), width)
    for part in range(2):
        at = slice(part * width, (part + 1) * width)
        wide[part, width : 2 * width] = plane_ref[at]
        wide[part, pl.ds(at_a, width)] = plane_a_ref[at]
        wide[part, pl.ds(at_b, width)] = jnp.where(has_second(), plane_b_ref[at], 0.0)
    forward = (forward_high_ref[...], forward_low_ref[...])
    inverse = (inverse_high_ref[...], inverse_low_ref[...])
    waves, masks = [], []
    lanes = lax.broadcasted_iota(jnp.int32, (side, side), 1)
    sublanes = lax.broadcasted_iota(jnp.int32, (side, side), 0)
    for slot in range(slots):
        probe = probes_ref[slot]
        row, column, live = (
            jnp.broadcast_to(slots_ref[slot, number : number + 1], (side, side))
            for number in range(3)
        )
        near_lanes, near_columns = lanes >= row, sublanes >= column
        masks.append((near_lanes, near_columns, live > 0))
        window = []
        for part in range(2):
            near = jnp.where(near_lanes, wide[part, :side, :side], wide[part, :side, side:])
            wrapped = jnp.where(
                near_lanes[:width], wide[part, side:, :side], wide[part, side:, side:]
            )
            wrapped = jnp.concatenate([wrapped, near[width:]], axis=0)
            window.append(jnp.where(near_columns, near, wrapped))
        wave_real = probe[0] * window[0] - probe[1] * window[1]
        wave_imaginary = probe[0] * window[1] + probe[1] * window[0]
        waves.append(jnp.concatenate([wave_real, wave_imaginary], axis=1))
    half = product(split(jnp.concatenate(waves, axis=0)), inverse)
    half = jnp.concatenate(
        [
            jnp.concatenate(
                [half[slot * side : (slot + 1) * side, part * side : (part + 1) * side] for slot in range(slots)],
                axis=1,
            )
            for part in range(2)
        ],
        axis=0,
    )
    far = product(forward, split(half))
    far_real, far_imaginary = far[:side], far[side:]
    intensity = jnp.concatenate(
        [intensity_ref[0, slot].astype(jnp.float32) for slot in range(slots)], axis=1
    )
    factor = 1.0 - amplitude_step * (
        far_real * far_real + far_imaginary * far_imaginary - intensity
    )
    corrected = jnp.concatenate([far_real * factor, far_imaginary * factor], axis=0)
    half = product(inverse, split(corrected))
    half = jnp.concatenate(
        [
            jnp.concatenate(
                [half[part * side : (part + 1) * side, slot * side : (slot + 1) * side] for part in range(2)],
                axis=1,
            )
            for slot in range(slots)
        ],
        axis=0,
    )
    near = product(split(half), forward)
    totals[:2] = jnp.zeros_like(totals[:2])
    totals[2:] = density_ref[...]
    for slot in range(slots):
        probe = probes_ref[slot]
        near_real = near[slot * side : (slot + 1) * side, :side]
        near_imaginary = near[slot * side : (slot + 1) * side, side:]
        place(totals, 0, probe[0] * near_real + probe[1] * near_imaginary, masks[slot], width)
        place(totals, 1, probe[0] * near_imaginary - probe[1] * near_real, masks[slot], width)
    own_ref[...] = totals[:, width : 2 * width]
    for rim_ref, at in ((rim_a_ref, at_a), (rim_b_ref, at_b)):
        for part in range(totals.shape[0]):
            rim_ref[part * width : (part + 1) * width] = totals[part, pl.ds(at, width)]
    first_tile = tile_is_first()
    count = volume_ref.shape[1]
    for channel in range(2):
        rows = []
        for row in (0, count - 1):
            before, after = edges_of(plane_a_ref, plane_b_ref, channel * count + row, width)
            rows.append((volume_ref[channel, row], jnp.concatenate([before, after], axis=0)))
        for low, row_ref in ((jnp.logical_not(first_tile), row_a_ref), (first_tile, row_b_ref)):
            row_ref[channel, :width] = jnp.where(low, rows[0][0], rows[1][0])
            row_ref[channel, width : width + 2] = jnp.where(low, rows[0][1], rows[1][1])


def fold_kernel(
    own_ref, rim_a_ref, rim_b_ref, projected_ref, dual_ref, rays_ref, too_ref, object_ref, residual_ref
):
    width = own_ref.shape[1]
    second = has_second()
    sums = [
        own_ref[part]
        + rim_a_ref[part * width : (part + 1) * width]
        + jnp.where(second, rim_b_ref[part * width : (part + 1) * width], 0.0)
        for part in range(3)
    ]
    for part in range(2):
        target = projected_ref[0, part]
        dual = dual_ref[0, part]
        updated = (sums[part] + penalty * (target - dual)) / (sums[2] + penalty)
        object_ref[0, part] = updated
        residual_ref[part * width : (part + 1) * width] = target - updated - dual
    residual_ref[2 * width : 2 * width + SUBLANES] = rays_ref[...]
    residual_ref[2 * width + SUBLANES :] = too_ref[...]


def variation_kernel(
    volume_ref, plane_a_ref, plane_b_ref, row_a_ref, row_b_ref, base_ref, padded, norms
):
    width = volume_ref.shape[2]
    length = volume_ref.shape[3]
    count = volume_ref.shape[1]
    margin = 8
    first_tile = tile_is_first()
    place = lax.axis_index("angle") * 2 + lax.axis_index("tile")
    bridged = (place > 0) & (place < 2 * lax.axis_size("angle") - 1)
    lanes = lax.broadcasted_iota(jnp.int32, (width, length), 1)
    first_lane = lanes == 0
    last_lane = lanes == length - 1
    for channel in range(2):
        for row in range(count):
            before, after = edges_of(plane_a_ref, plane_b_ref, channel * count + row, width)
            padded[row + 1, margin : margin + width] = volume_ref[channel, row]
            padded[row + 1, margin - 1 : margin] = before
            padded[row + 1, margin + width : margin + width + 1] = after
        row_a, row_b = row_a_ref[channel], jnp.where(bridged, row_b_ref[channel], 0.0)
        for row, beside in (
            (0, jnp.where(first_tile, row_b, row_a)),
            (count + 1, jnp.where(first_tile, row_a, row_b)),
        ):
            padded[row, margin : margin + width] = beside[:width]
            padded[row, margin - 1 : margin] = beside[width : width + 1]
            padded[row, margin + width : margin + width + 1] = beside[width + 1 : width + 2]
        previous_y = None
        for row in range(count + 1):
            here = padded[row, margin : margin + width]
            along_y = padded[row + 1, margin : margin + width] - here
            along_x = padded[row, margin + 1 : margin + width + 1] - here
            along_z = jnp.where(last_lane, 0.0, pltpu.roll(here, length - 1, 1)) - here
            inverse = lax.rsqrt(
                along_y * along_y + along_x * along_x + along_z * along_z + smoothing * smoothing
            )
            norm_y = along_y * inverse
            if row > 0:
                norm_x = along_x * inverse
                norm_z = along_z * inverse
                corner = padded[row, margin - 1 : margin]
                corner_y = padded[row + 1, margin - 1 : margin] - corner
                corner_x = here[:1] - corner
                corner_z = (
                    jnp.where(last_lane[:1], 0.0, pltpu.roll(corner, length - 1, 1)) - corner
                )
                corner_norm = corner_x * lax.rsqrt(
                    corner_y * corner_y
                    + corner_x * corner_x
                    + corner_z * corner_z
                    + smoothing * smoothing
                )
                norms[margin : margin + width] = norm_x
                norms[margin - 1 : margin] = corner_norm
                behind_x = norms[margin - 1 : margin + width - 1]
                ahead = here * lax.rsqrt(here * here + smoothing * smoothing)
                behind_z = jnp.where(first_lane, ahead, pltpu.roll(norm_z, 1, 1))
                divergence = (
                    norm_y - previous_y + (norm_x - behind_x) + (norm_z - behind_z)
                )
                base_ref[channel, row - 1] = here + (step_size * tv_weight) * divergence
            previous_y = norm_y


def spread_kernel(
    shift_ref, weight_ref, base_ref, beside_ref, _, keep_ref, send_ref, padded
):
    width = base_ref.shape[2]
    count = base_ref.shape[1]
    columns, tiles = keep_ref.shape[0], lax.axis_size("tile")
    me, tile, scan = lax.axis_index("angle"), lax.axis_index("tile"), lax.axis_index("scan")
    upper = me >= columns // 2
    chunks = [slice(at, at + LANES) for at in range(0, base_ref.shape[3], LANES)]
    exists = jnp.where(upper, scan < lax.axis_size("scan") - 1, scan > 0).astype(jnp.float32)
    own_at = pl.multiple_of(jnp.where(upper, 0, width), width)
    beside_at = pl.multiple_of(jnp.where(upper, width, 0), width)
    for row in range(count):
        for channel in range(2):
            for chunk, at in enumerate(chunks):
                padded[row, channel, chunk, pl.ds(own_at, width)] = base_ref[channel, row, :, at]
                padded[row, channel, chunk, pl.ds(beside_at, width)] = (
                    beside_ref[channel, row, :, at] * exists
                )
    for turn in range(columns):
        for flip, out_ref in ((0, keep_ref), (1, send_ref)):
            angle = lax.rem(me + turn, columns) * tiles + (tile if flip == 0 else 1 - tile)
            for channel in range(2):
                for chunk, at in enumerate(chunks):
                    total = jnp.zeros((width, LANES), jnp.float32)
                    for row in range(count):
                        start = jnp.where(upper, 0, width) + shift_ref[row, angle]
                        fraction = weight_ref[row, angle]
                        total += (1.0 - fraction) * padded[row, channel, chunk, pl.ds(start, width)]
                        total += fraction * padded[row, channel, chunk, pl.ds(start + 1, width)]
                    out_ref[turn, channel, :, at] = total


def operator_kernel(*refs):
    packed_refs, (object_ref, high_ref, low_ref, object_out_ref) = refs[:-4], refs[-4:]
    object_out_ref[...] = object_ref[...]
    tiles = lax.axis_size("tile")
    columns = len(packed_refs)
    rows_out, reach = high_ref.shape[1:]
    width = reach // 3
    count = rows_out // (2 * width) - 1
    me, tile, scan = lax.axis_index("angle"), lax.axis_index("tile"), lax.axis_index("scan")

    def taps(shape, first, table, row, step):
        lanes = lax.broadcasted_iota(jnp.int32, shape, 1)
        sublanes = lax.broadcasted_iota(jnp.int32, shape, 0)
        offset = (lanes - sublanes).astype(jnp.float32) - first
        shift = step * table[2 * row : 2 * row + 1]
        fraction = table[2 * row + 1 : 2 * row + 2]
        return jnp.where(offset == shift, 1.0 - fraction, 0.0) + jnp.where(
            offset == shift + step, fraction, 0.0
        )

    def angle_of(turn, flip):
        return lax.rem(me + turn, columns) * tiles + (tile if flip == 0 else 1 - tile)

    def table_of(turn, flip, angle):
        at = 2 * width + SUBLANES * flip
        tile_of = packed_refs[turn][at : at + SUBLANES]
        lanes = lax.broadcasted_iota(jnp.int32, tile_of.shape, 1)
        return jnp.sum(jnp.where(lanes == angle, tile_of, 0.0), axis=1, keepdims=True)

    cells = lax.broadcasted_iota(jnp.int32, (width, 2 * width), 1)
    forward = []
    backward = [[] for _ in range(columns)]
    for turn in range(columns):
        upper = lax.rem(me + turn, columns) >= columns // 2
        base_at = jnp.where(upper, 0, width)
        first_cell = jnp.where(upper, 0, jnp.where(scan > 0, 0, width))
        end_cell = jnp.where(upper & (scan == lax.axis_size("scan") - 1), width, 2 * width)
        inside = (cells >= first_cell) & (cells < end_cell)
        for flip in range(tiles):
            for row in range(count):
                parts = []
                for own in range(tiles):
                    table = table_of(turn, flip, angle_of(0, own))
                    part = taps((width, 2 * width), base_at.astype(jnp.float32), table, row, 1.0)
                    parts.append(jnp.where(inside, part, 0.0))
                forward.append(jnp.concatenate(parts, axis=0))
                for source in range(columns):
                    table = table_of(turn, flip, angle_of(source, 0))
                    first = (width - base_at).astype(jnp.float32)
                    backward[source].append(taps((2 * width, reach), first, table, row, -1.0))
    left = split(jnp.concatenate(forward, axis=1))
    for source in range(columns):
        both = product(left, split(jnp.concatenate(backward[source], axis=0)))
        blocks = [both]
        for flip in range(tiles):
            for row in range(count):
                table = table_of(0, flip, angle_of(source, 0))
                blocks.append(taps((width, reach), float(width), table, row, -1.0))
        high_ref[source], low_ref[source] = split(jnp.concatenate(blocks, axis=0))


def apply_kernel(here_ref, side_a_ref, side_b_ref, high_ref, low_ref, keep_ref, own_ref, send_ref, wide):
    width = keep_ref.shape[1]
    columns = here_ref.shape[0]
    count = own_ref.shape[1]
    even = scan_is_even()
    at_a = pl.multiple_of(jnp.where(even, 2 * width, 0), width)
    at_b = pl.multiple_of(jnp.where(even, 0, 2 * width), width)
    for source in range(columns):
        for channel in range(2):
            at = slice(channel * width, (channel + 1) * width)
            wide[source, channel, width : 2 * width] = here_ref[source, at]
            wide[source, channel, pl.ds(at_a, width)] = side_a_ref[source, at]
            wide[source, channel, pl.ds(at_b, width)] = jnp.where(
                has_second(), side_b_ref[source, at], 0.0
            )
    for channel in range(2):
        total = 0.0
        for source in range(columns):
            total += product((high_ref[source], low_ref[source]), split(wide[source, channel]))
        keep_ref[channel] = total[:width]
        send_ref[channel * width : (channel + 1) * width] = total[width : 2 * width]
        for row in range(count):
            at = (2 + row) * width
            own_ref[channel, row] = total[at : at + width]
            target = (2 + channel * count + row) * width
            send_ref[target : target + width] = total[at + count * width : at + (count + 1) * width]


def finish_kernel(*refs):
    keep_ref, own_ref, received_ref, base_ref, object_ref, dual_ref = refs[:6]
    spreads, (dual_out_ref, volume_ref, projected_ref) = refs[6:-3], refs[-3:]
    count, width = own_ref.shape[1:3]
    for channel in range(2):
        received = received_ref[channel * width : (channel + 1) * width]
        projection = -step_size * (keep_ref[channel] + received)
        for spread_ref in spreads:
            projection = projection + spread_ref[channel]
        projected_ref[0, channel] = projection
        dual_out_ref[0, channel] = dual_ref[0, channel] + object_ref[0, channel] - projection
        for row in range(count):
            at = (2 + channel * count + row) * width
            descent = own_ref[channel, row] + received_ref[at : at + width]
            volume_ref[channel, row] = base_ref[channel, row] - step_size * descent


def call(
    kernel, shapes, operands, scratch, flops, scalars=0, staged=(), numbers=(), copies=0, kind=jnp.float32, kinds={}
):
    held = sum(operand.nbytes for operand in operands[scalars:] + staged)
    held += 4 * sum(math.prod(shape) for shape in shapes)
    own = 4 * sum(math.prod(shape) for shape in scratch)
    outputs = [
        jax.ShapeDtypeStruct(shape, kinds.get(number, kind)) for number, shape in enumerate(shapes)
    ]
    scratch_shapes = [pltpu.VMEM(shape, jnp.float32) for shape in scratch]
    if staged and not copies:
        outputs += [jax.ShapeDtypeStruct(array.shape, array.dtype) for array in staged]
        copies = len(staged) + len(numbers)
        scratch_shapes += [pltpu.SMEM(array.shape, array.dtype) for array in numbers]
    staged += numbers
    if copies:
        scratch_shapes.append(pltpu.SemaphoreType.DMA((copies,)))
    in_specs = [SMEM] * scalars + [VMEM] * (len(operands) - scalars) + [HBM] * len(staged)
    return pl.pallas_call(
        kernel,
        out_shape=outputs,
        in_specs=in_specs,
        out_specs=[VMEM] * len(outputs),
        scratch_shapes=scratch_shapes,
        compiler_params=pltpu.CompilerParams(vmem_limit_bytes=held + own + SPARE_BYTES),
        cost_estimate=pl.CostEstimate(flops=flops, bytes_accessed=held, transcendentals=0),
    )(*operands, *(pltpu.with_memory_space_constraint(array, pltpu.HBM) for array in staged))


def body(
    transmission,
    scaled_dual,
    projected,
    volume,
    intensities,
    probe_wave,
    slot_first_rows,
    slot_first_columns,
    patch_counts,
    shift_table,
    tap_weight,
):
    width, length = transmission.shape[2:]
    count = volume.shape[1]
    scans, columns, tiles = (lax.axis_size(axis) for axis in ("scan", "angle", "tile"))
    assert scans % 2 == 0 and columns % 2 == 0 and tiles == 2 and lax.axis_size("groups") % 2 == 0
    rounds = []
    for first in (0, 1):
        pairs = [(i, i + 1) for i in range(first, scans - 1, 2)]
        route = [(s * tiles + t, d * tiles + t) for s, d in pairs for t in range(tiles)]
        route += [(target, source) for source, target in route]
        ends = {i for i in range(scans)} - {i for pair in pairs for i in pair}
        for scan in sorted(ends):
            route += [(scan * tiles + t, scan * tiles + 1 - t) for t in range(tiles)]
        rounds.append(route)
    swap = [(0, 1), (1, 0)]

    def exchange(block, number):
        return lax.ppermute(block, ("scan", "tile"), rounds[number])

    def across(block):
        return lax.ppermute(block, "tile", swap)

    edges = 2 * 2 * count
    (plane,) = call(
        pack_kernel,
        [(2 * width + -(-edges // SUBLANES) * SUBLANES, length)],
        (),
        [(edges, SUBLANES, length)],
        10**5,
        staged=(transmission, volume),
        copies=2 + edges,
    )
    plane_a = exchange(plane, 0)
    plane_b = exchange(plane, 1)
    tables = [jnp.asarray(table) for table in dft_tables(probe_wave.shape[1])]
    slots = slot_first_rows.shape[1]
    side = probe_wave.shape[1]
    probes, density, slot_numbers, rays, _, *held = call(
        prepare_kernel,
        [
            (slots, 2, side, side),
            (1, 3 * width, length),
            (slots, SUBLANES, side),
            (SUBLANES, length),
        ],
        (patch_counts,),
        [],
        10**7,
        1,
        (probe_wave, intensities, volume, *tables),
        (slot_first_rows, slot_first_columns, shift_table.T, tap_weight.T),
        kinds={2: jnp.int32},
    )
    volume_here = held[1]
    turns = [[(i, (i - turn) % columns) for i in range(columns)] for turn in range(columns)]
    rays_too = across(rays)
    own, rim_a, rim_b, row_a, row_b = call(
        patch_kernel,
        [(3, width, length)]
        + [(3 * width, length)] * 2
        + [(2, width + SUBLANES, length)] * 2,
        (probes, density, slot_numbers, plane, *held, plane_a, plane_b),
        [(2, 3 * width, length), (3, 3 * width, length)],
        10**9,
    )
    rim_a = exchange(rim_a, 0)
    rim_b = exchange(rim_b, 1)
    per_group, groups = columns * tiles, lax.axis_size("groups")
    bridge = []
    for group in range(groups):
        at = group * per_group
        pairs = [(at + i * tiles + 1, at + (i + 1) * tiles) for i in range(columns - 1)]
        bridge += pairs + [(target, source) for source, target in pairs]
        beyond = (groups - 1 - group) * per_group
        for outer in (0, per_group - 1):
            bridge.append((at + outer, beyond + outer))
    row_b = lax.ppermute(row_b, ("groups", "angle", "tile"), bridge)
    row_a = across(row_a)
    updated, residual = call(
        fold_kernel,
        [transmission.shape, (2 * width + 2 * SUBLANES, length)],
        (own, rim_a, rim_b, projected, scaled_dual, rays, rays_too),
        [],
        10**6,
    )
    by_column = [residual]
    for turn in range(1, columns):
        by_column.append(lax.ppermute(residual, "angle", turns[turn]))
    (base,) = call(
        variation_kernel,
        [volume.shape],
        (volume_here, plane_a, plane_b, row_a, row_b),
        [(count + 2, width + 16, length), (width + 16, length)],
        10**7,
    )
    route = []
    for scan in range(scans):
        for column in range(columns):
            lower = column < columns // 2
            target = scan + 1 if lower else scan - 1
            turned = column
            if not 0 <= target < scans:
                target, turned = scan, (column + columns // 2) % columns
            route.append((scan * columns + column, target * columns + turned))
    beside = lax.ppermute(base, ("scan", "angle"), route)
    level = across(base[0, 0, :SUBLANES])
    here = jnp.stack(by_column)
    side_a = exchange(here, 0)
    side_b = exchange(here, 1)
    high, low, new_transmission = call(
        operator_kernel,
        [(columns, (2 + 2 * count) * width, 3 * width)] * 2 + [transmission.shape],
        (*by_column, updated),
        [],
        10**8,
        kind=jnp.bfloat16,
        kinds={2: jnp.float32},
    )
    block = (columns, 2, width, length)
    keep, send = call(
        spread_kernel,
        [block, block],
        (shift_table.T, tap_weight.T, base, beside, level),
        [(count, 2, length // LANES, 2 * width, LANES)],
        10**7,
        2,
    )
    received = across(send)
    spreads = [keep[0], received[0]]
    for turn in range(1, columns):
        route = [(i, (i + turn) % columns) for i in range(columns)]
        spreads.append(lax.ppermute(keep[turn] + received[turn], "angle", route))
    keep, own, send = call(
        apply_kernel,
        [(2, width, length), volume.shape, ((2 + 2 * count) * width, length)],
        (here, side_a, side_b, high, low),
        [(columns, 2, 3 * width, length)],
        10**9,
    )
    received = across(send)
    new_dual, new_volume, new_projected = call(
        finish_kernel,
        [transmission.shape, volume.shape, transmission.shape],
        (keep, own, received, base, updated, scaled_dual, *spreads),
        [],
        10**6,
    )
    return (new_transmission, new_dual, new_volume, new_projected)


def solution(mesh):
    plane = P(("groups", "angle", "tile"), None, "scan", None)
    cells = P("groups", ("angle", "tile"), "scan", None)
    slots = P(("groups", "angle", "tile"), "scan")
    return jax.shard_map(
        body,
        mesh=mesh,
        in_specs=(
            plane,
            plane,
            plane,
            cells,
            P(("groups", "angle", "tile"), "scan", None, None),
            P("groups", None, None),
            slots,
            slots,
            slots,
            P(None, ("angle", "tile")),
            P(None, ("angle", "tile")),
        ),
        out_specs=(plane, plane, cells, plane),
        check_vma=False,
    )
```

```python
import math

import jax
import jax.numpy as jnp
import numpy as np
from jax import lax
from jax.experimental import pallas as pl
from jax.experimental.pallas import tpu as pltpu
from jax.sharding import PartitionSpec as P


penalty = 4.0
amplitude_step = 0.25
tv_weight = 1.0
smoothing = 0.05
step_size = 0.008

VMEM = pl.BlockSpec(memory_space=pltpu.VMEM)
SMEM = pl.BlockSpec(memory_space=pltpu.SMEM)
HBM = pl.BlockSpec(memory_space=pltpu.MemorySpace.HBM)
LANES = 128
SUBLANES = 8
SPARE_BYTES = 8 << 20


def split(values):
    high = values.astype(jnp.bfloat16)
    return (high, (values - high.astype(jnp.float32)).astype(jnp.bfloat16))


def product(left, right):
    total = jnp.dot(left[0], right[0], preferred_element_type=jnp.float32)
    total += jnp.dot(left[0], right[1], preferred_element_type=jnp.float32)
    return total + jnp.dot(left[1], right[0], preferred_element_type=jnp.float32)


def dft_tables(length):
    grid_ids = np.arange(length)
    radians = (grid_ids[:, None] * grid_ids[None, :] % length) * (2.0 * math.pi / length)
    cosine = np.cos(radians) / math.sqrt(length)
    sine = np.sin(radians) / math.sqrt(length)
    forward = np.block([[cosine, sine], [-sine, cosine]])
    tables = []
    for table in (forward, forward.T):
        high = table.astype(jnp.bfloat16)
        tables += [high, (table - high.astype(np.float64)).astype(jnp.bfloat16)]
    return tables


def tile_is_first():
    return lax.axis_index("tile") == 0


def scan_is_even():
    return lax.rem(lax.axis_index("scan"), 2) == 0


def pack_kernel(plane_ref, volume_ref, packed_ref, slabs, done):
    width = plane_ref.shape[2]
    count = volume_ref.shape[1]
    copies = [
        (plane_ref.at[0, channel], packed_ref.at[channel * width : (channel + 1) * width])
        for channel in range(2)
    ]
    for channel in range(2):
        for row in range(count):
            for side, at in enumerate((0, width - SUBLANES)):
                source = volume_ref.at[channel, row, at : at + SUBLANES]
                copies.append((source, slabs.at[(channel * count + row) * 2 + side]))
    copies = [
        pltpu.make_async_copy(source, target, done.at[number])
        for number, (source, target) in enumerate(copies)
    ]
    for copy in copies:
        copy.start()
    for copy in copies[2:]:
        copy.wait()
    for edge in range(slabs.shape[0]):
        take = 0 if edge % 2 == 0 else SUBLANES - 1
        packed_ref[2 * width + edge : 2 * width + edge + 1] = slabs[edge, take : take + 1]
    for copy in copies[:2]:
        copy.wait()


def has_second():
    scan = lax.axis_index("scan")
    return (scan > 0) & (scan < lax.axis_size("scan") - 1)


def edges_of(plane_a_ref, plane_b_ref, number, width):
    even = scan_is_even()
    at = 2 * width + 2 * number
    first_a, last_a = plane_a_ref[at : at + 1], plane_a_ref[at + 1 : at + 2]
    first_b, last_b = (
        jnp.where(has_second(), plane_b_ref[edge : edge + 1], 0.0) for edge in (at, at + 1)
    )
    return (jnp.where(even, last_b, last_a), jnp.where(even, first_a, first_b))


def slot_masks(rows_ref, columns_ref, count_ref, slot, side):
    lanes = lax.broadcasted_iota(jnp.int32, (side, side), 1)
    sublanes = lax.broadcasted_iota(jnp.int32, (side, side), 0)
    near_lanes = lanes >= rows_ref[0, slot]
    near_columns = sublanes >= columns_ref[0, slot]
    return (near_lanes, near_columns, jnp.full((side, side), slot < count_ref[0, 0]))


def place(totals, part, term, masks, width):
    side = term.shape[0]
    near_lanes, near_columns, live = masks
    inner = live & near_columns
    outer = (live & jnp.logical_not(near_columns))[:width]
    for start, lane_mask in ((0, near_lanes), (side, jnp.logical_not(near_lanes))):
        at = slice(start, start + side)
        totals[part, :side, at] += jnp.where(inner & lane_mask, term, 0.0)
        totals[part, side:, at] += jnp.where(outer & lane_mask[:width], term[:width], 0.0)


def prepare_kernel(count_ref, *refs):
    held = (len(refs) - 13) // 2
    sources = refs[: held + 4]
    probes_ref, density_ref, slots_ref, rays_ref = refs[held + 4 : held + 8]
    targets, done = refs[held + 8 : -1], refs[-1]
    rows_ref, columns_ref, shift_ref, weight_ref = targets[held:]
    copies = [
        pltpu.make_async_copy(source, target, done.at[number])
        for number, (source, target) in enumerate(zip(sources, targets))
    ]
    for copy in copies:
        copy.start()
    probe_ref = targets[0]
    side = probe_ref.shape[1]
    slots = probes_ref.shape[0]
    width = density_ref.shape[1] - side
    density_ref[...] = jnp.zeros_like(density_ref)
    for copy in copies[:1] + copies[held:]:
        copy.wait()
    places = lax.broadcasted_iota(jnp.int32, slots_ref.shape[1:], 0)
    for slot in range(slots):
        live = jnp.where(slot < count_ref[0, 0], 1, 0)
        numbers = jnp.where(places == 0, rows_ref[0, slot], columns_ref[0, slot])
        slots_ref[slot] = jnp.where(places == 2, live, numbers)
        turn = lax.rem(rows_ref[0, slot], side)
        probe = [
            pltpu.roll(pltpu.roll(probe_ref[part], columns_ref[0, slot], 0), turn, 1)
            for part in range(2)
        ]
        for part in range(2):
            probes_ref[slot, part] = probe[part]
        masks = slot_masks(rows_ref, columns_ref, count_ref, slot, side)
        place(density_ref, 0, probe[0] * probe[0] + probe[1] * probe[1], masks, width)
    places = lax.broadcasted_iota(jnp.int32, rays_ref.shape, 0)
    lanes = lax.broadcasted_iota(jnp.int32, rays_ref.shape, 1)
    rays = jnp.zeros(rays_ref.shape, jnp.float32)
    for row in range(shift_ref.shape[0]):
        for angle in range(shift_ref.shape[1]):
            shift = shift_ref[row, angle].astype(jnp.float32)
            here = lanes == angle
            rays = jnp.where(here & (places == 2 * row), shift, rays)
            rays = jnp.where(here & (places == 2 * row + 1), weight_ref[row, angle], rays)
    rays_ref[...] = rays
    for copy in copies[1:held]:
        copy.wait()


def patch_kernel(
    probes_ref,
    density_ref,
    slots_ref,
    plane_ref,
    intensity_ref,
    volume_ref,
    forward_high_ref,
    forward_low_ref,
    inverse_high_ref,
    inverse_low_ref,
    plane_a_ref,
    plane_b_ref,
    own_ref,
    rim_a_ref,
    rim_b_ref,
    row_a_ref,
    row_b_ref,
    wide,
    totals,
):
    width = volume_ref.shape[2]
    slots, _, side, _ = probes_ref.shape
    even = scan_is_even()
    at_a = pl.multiple_of(jnp.where(even, 2 * width, 0), width)
    at_b = pl.multiple_of(jnp.where(even, 0, 2 * width), width)
    for part in range(2):
        at = slice(part * width, (part + 1) * width)
        wide[part, width : 2 * width] = plane_ref[at]
        wide[part, pl.ds(at_a, width)] = plane_a_ref[at]
        wide[part, pl.ds(at_b, width)] = jnp.where(has_second(), plane_b_ref[at], 0.0)
    forward = (forward_high_ref[...], forward_low_ref[...])
    inverse = (inverse_high_ref[...], inverse_low_ref[...])
    waves, masks = [], []
    lanes = lax.broadcasted_iota(jnp.int32, (side, side), 1)
    sublanes = lax.broadcasted_iota(jnp.int32, (side, side), 0)
    for slot in range(slots):
        probe = probes_ref[slot]
        row, column, live = (
            jnp.broadcast_to(slots_ref[slot, number : number + 1], (side, side))
            for number in range(3)
        )
        near_lanes, near_columns = lanes >= row, sublanes >= column
        masks.append((near_lanes, near_columns, live > 0))
        window = []
        for part in range(2):
            near = jnp.where(near_lanes, wide[part, :side, :side], wide[part, :side, side:])
            wrapped = jnp.where(
                near_lanes[:width], wide[part, side:, :side], wide[part, side:, side:]
            )
            wrapped = jnp.concatenate([wrapped, near[width:]], axis=0)
            window.append(jnp.where(near_columns, near, wrapped))
        wave_real = probe[0] * window[0] - probe[1] * window[1]
        wave_imaginary = probe[0] * window[1] + probe[1] * window[0]
        waves.append(jnp.concatenate([wave_real, wave_imaginary], axis=1))
    half = product(split(jnp.concatenate(waves, axis=0)), inverse)
    half = jnp.concatenate(
        [
            jnp.concatenate(
                [half[slot * side : (slot + 1) * side, part * side : (part + 1) * side] for slot in range(slots)],
                axis=1,
            )
            for part in range(2)
        ],
        axis=0,
    )
    far = product(forward, split(half))
    far_real, far_imaginary = far[:side], far[side:]
    intensity = jnp.concatenate(
        [intensity_ref[0, slot].astype(jnp.float32) for slot in range(slots)], axis=1
    )
    factor = 1.0 - amplitude_step * (
        far_real * far_real + far_imaginary * far_imaginary - intensity
    )
    corrected = jnp.concatenate([far_real * factor, far_imaginary * factor], axis=0)
    half = product(inverse, split(corrected))
    half = jnp.concatenate(
        [
            jnp.concatenate(
                [half[part * side : (part + 1) * side, slot * side : (slot + 1) * side] for part in range(2)],
                axis=1,
            )
            for slot in range(slots)
        ],
        axis=0,
    )
    near = product(split(half), forward)
    totals[:2] = jnp.zeros_like(totals[:2])
    totals[2:] = density_ref[...]
    for slot in range(slots):
        probe = probes_ref[slot]
        near_real = near[slot * side : (slot + 1) * side, :side]
        near_imaginary = near[slot * side : (slot + 1) * side, side:]
        place(totals, 0, probe[0] * near_real + probe[1] * near_imaginary, masks[slot], width)
        place(totals, 1, probe[0] * near_imaginary - probe[1] * near_real, masks[slot], width)
    own_ref[...] = totals[:, width : 2 * width]
    for rim_ref, at in ((rim_a_ref, at_a), (rim_b_ref, at_b)):
        for part in range(totals.shape[0]):
            rim_ref[part * width : (part + 1) * width] = totals[part, pl.ds(at, width)]
    first_tile = tile_is_first()
    count = volume_ref.shape[1]
    for channel in range(2):
        rows = []
        for row in (0, count - 1):
            before, after = edges_of(plane_a_ref, plane_b_ref, channel * count + row, width)
            rows.append((volume_ref[channel, row], jnp.concatenate([before, after], axis=0)))
        for low, row_ref in ((jnp.logical_not(first_tile), row_a_ref), (first_tile, row_b_ref)):
            row_ref[channel, :width] = jnp.where(low, rows[0][0], rows[1][0])
            row_ref[channel, width : width + 2] = jnp.where(low, rows[0][1], rows[1][1])


def fold_kernel(
    own_ref, rim_a_ref, rim_b_ref, projected_ref, dual_ref, rays_ref, too_ref, object_ref, residual_ref, packed_ref
):
    width = own_ref.shape[1]
    second = has_second()
    sums = [
        own_ref[part]
        + rim_a_ref[part * width : (part + 1) * width]
        + jnp.where(second, rim_b_ref[part * width : (part + 1) * width], 0.0)
        for part in range(3)
    ]
    for part in range(2):
        target = projected_ref[0, part]
        dual = dual_ref[0, part]
        updated = (sums[part] + penalty * (target - dual)) / (sums[2] + penalty)
        object_ref[0, part] = updated
        residual = target - updated - dual
        residual_ref[part * width : (part + 1) * width] = residual
        packed_ref[part * width : (part + 1) * width] = residual
    packed_ref[2 * width : 2 * width + SUBLANES] = rays_ref[...]
    packed_ref[2 * width + SUBLANES :] = too_ref[...]


def variation_kernel(
    volume_ref, plane_a_ref, plane_b_ref, row_a_ref, row_b_ref, base_ref, padded, norms
):
    width = volume_ref.shape[2]
    length = volume_ref.shape[3]
    count = volume_ref.shape[1]
    margin = 8
    first_tile = tile_is_first()
    place = lax.axis_index("angle") * 2 + lax.axis_index("tile")
    bridged = (place > 0) & (place < 2 * lax.axis_size("angle") - 1)
    lanes = lax.broadcasted_iota(jnp.int32, (width, length), 1)
    first_lane = lanes == 0
    last_lane = lanes == length - 1
    for channel in range(2):
        for row in range(count):
            before, after = edges_of(plane_a_ref, plane_b_ref, channel * count + row, width)
            padded[row + 1, margin : margin + width] = volume_ref[channel, row]
            padded[row + 1, margin - 1 : margin] = before
            padded[row + 1, margin + width : margin + width + 1] = after
        row_a, row_b = row_a_ref[channel], jnp.where(bridged, row_b_ref[channel], 0.0)
        for row, beside in (
            (0, jnp.where(first_tile, row_b, row_a)),
            (count + 1, jnp.where(first_tile, row_a, row_b)),
        ):
            padded[row, margin : margin + width] = beside[:width]
            padded[row, margin - 1 : margin] = beside[width : width + 1]
            padded[row, margin + width : margin + width + 1] = beside[width + 1 : width + 2]
        previous_y = None
        for row in range(count + 1):
            here = padded[row, margin : margin + width]
            along_y = padded[row + 1, margin : margin + width] - here
            along_x = padded[row, margin + 1 : margin + width + 1] - here
            along_z = jnp.where(last_lane, 0.0, pltpu.roll(here, length - 1, 1)) - here
            inverse = lax.rsqrt(
                along_y * along_y + along_x * along_x + along_z * along_z + smoothing * smoothing
            )
            norm_y = along_y * inverse
            if row > 0:
                norm_x = along_x * inverse
                norm_z = along_z * inverse
                corner = padded[row, margin - 1 : margin]
                corner_y = padded[row + 1, margin - 1 : margin] - corner
                corner_x = here[:1] - corner
                corner_z = (
                    jnp.where(last_lane[:1], 0.0, pltpu.roll(corner, length - 1, 1)) - corner
                )
                corner_norm = corner_x * lax.rsqrt(
                    corner_y * corner_y
                    + corner_x * corner_x
                    + corner_z * corner_z
                    + smoothing * smoothing
                )
                norms[margin : margin + width] = norm_x
                norms[margin - 1 : margin] = corner_norm
                behind_x = norms[margin - 1 : margin + width - 1]
                ahead = here * lax.rsqrt(here * here + smoothing * smoothing)
                behind_z = jnp.where(first_lane, ahead, pltpu.roll(norm_z, 1, 1))
                divergence = (
                    norm_y - previous_y + (norm_x - behind_x) + (norm_z - behind_z)
                )
                base_ref[channel, row - 1] = here + (step_size * tv_weight) * divergence
            previous_y = norm_y


def spread_kernel(
    shift_ref, weight_ref, base_ref, beside_ref, keep_ref, send_ref, padded
):
    width = base_ref.shape[2]
    count = base_ref.shape[1]
    columns, tiles = keep_ref.shape[0], lax.axis_size("tile")
    me, tile, scan = lax.axis_index("angle"), lax.axis_index("tile"), lax.axis_index("scan")
    upper = me >= columns // 2
    chunks = [slice(at, at + LANES) for at in range(0, base_ref.shape[3], LANES)]
    exists = jnp.where(upper, scan < lax.axis_size("scan") - 1, scan > 0).astype(jnp.float32)
    own_at = pl.multiple_of(jnp.where(upper, 0, width), width)
    beside_at = pl.multiple_of(jnp.where(upper, width, 0), width)
    for row in range(count):
        for channel in range(2):
            for chunk, at in enumerate(chunks):
                padded[row, channel, chunk, pl.ds(own_at, width)] = base_ref[channel, row, :, at]
                padded[row, channel, chunk, pl.ds(beside_at, width)] = (
                    beside_ref[channel, row, :, at] * exists
                )
    for turn in range(columns):
        for flip, out_ref in ((0, keep_ref), (1, send_ref)):
            angle = lax.rem(me + turn, columns) * tiles + (tile if flip == 0 else 1 - tile)
            for channel in range(2):
                for chunk, at in enumerate(chunks):
                    total = jnp.zeros((width, LANES), jnp.float32)
                    for row in range(count):
                        start = jnp.where(upper, 0, width) + shift_ref[row, angle]
                        fraction = weight_ref[row, angle]
                        total += (1.0 - fraction) * padded[row, channel, chunk, pl.ds(start, width)]
                        total += fraction * padded[row, channel, chunk, pl.ds(start + 1, width)]
                    out_ref[turn, channel, :, at] = total


def operator_kernel(*refs):
    packed_refs, (object_ref, high_ref, low_ref, object_out_ref) = refs[:-4], refs[-4:]
    object_out_ref[...] = object_ref[...]
    tiles = lax.axis_size("tile")
    columns = len(packed_refs)
    rows_out, reach = high_ref.shape[1:]
    width = reach // 3
    count = rows_out // (2 * width) - 1
    me, tile, scan = lax.axis_index("angle"), lax.axis_index("tile"), lax.axis_index("scan")

    def taps(shape, first, table, row, step):
        lanes = lax.broadcasted_iota(jnp.int32, shape, 1)
        sublanes = lax.broadcasted_iota(jnp.int32, shape, 0)
        offset = (lanes - sublanes).astype(jnp.float32) - first
        shift = step * table[2 * row : 2 * row + 1]
        fraction = table[2 * row + 1 : 2 * row + 2]
        return jnp.where(offset == shift, 1.0 - fraction, 0.0) + jnp.where(
            offset == shift + step, fraction, 0.0
        )

    def angle_of(turn, flip):
        return lax.rem(me + turn, columns) * tiles + (tile if flip == 0 else 1 - tile)

    def table_of(turn, flip, angle):
        at = 2 * width + SUBLANES * flip
        tile_of = packed_refs[turn][at : at + SUBLANES]
        lanes = lax.broadcasted_iota(jnp.int32, tile_of.shape, 1)
        return jnp.sum(jnp.where(lanes == angle, tile_of, 0.0), axis=1, keepdims=True)

    cells = lax.broadcasted_iota(jnp.int32, (width, 2 * width), 1)
    forward = []
    backward = [[] for _ in range(columns)]
    for turn in range(columns):
        upper = lax.rem(me + turn, columns) >= columns // 2
        base_at = jnp.where(upper, 0, width)
        first_cell = jnp.where(upper, 0, jnp.where(scan > 0, 0, width))
        end_cell = jnp.where(upper & (scan == lax.axis_size("scan") - 1), width, 2 * width)
        inside = (cells >= first_cell) & (cells < end_cell)
        for flip in range(tiles):
            for row in range(count):
                parts = []
                for own in range(tiles):
                    table = table_of(turn, flip, angle_of(0, own))
                    part = taps((width, 2 * width), base_at.astype(jnp.float32), table, row, 1.0)
                    parts.append(jnp.where(inside, part, 0.0))
                forward.append(jnp.concatenate(parts, axis=0))
                for source in range(columns):
                    table = table_of(turn, flip, angle_of(source, 0))
                    first = (width - base_at).astype(jnp.float32)
                    backward[source].append(taps((2 * width, reach), first, table, row, -1.0))
    left = split(jnp.concatenate(forward, axis=1))
    for source in range(columns):
        both = product(left, split(jnp.concatenate(backward[source], axis=0)))
        blocks = [both]
        for flip in range(tiles):
            for row in range(count):
                table = table_of(0, flip, angle_of(source, 0))
                blocks.append(taps((width, reach), float(width), table, row, -1.0))
        high_ref[source], low_ref[source] = split(jnp.concatenate(blocks, axis=0))


def apply_kernel(here_ref, side_a_ref, side_b_ref, high_ref, low_ref, keep_ref, own_ref, send_ref, wide):
    width = keep_ref.shape[1]
    columns = here_ref.shape[0]
    count = own_ref.shape[1]
    even = scan_is_even()
    at_a = pl.multiple_of(jnp.where(even, 2 * width, 0), width)
    at_b = pl.multiple_of(jnp.where(even, 0, 2 * width), width)
    for source in range(columns):
        for channel in range(2):
            at = slice(channel * width, (channel + 1) * width)
            wide[source, channel, width : 2 * width] = here_ref[source, at]
            wide[source, channel, pl.ds(at_a, width)] = side_a_ref[source, at]
            wide[source, channel, pl.ds(at_b, width)] = jnp.where(
                has_second(), side_b_ref[source, at], 0.0
            )
    for channel in range(2):
        total = 0.0
        for source in range(columns):
            total += product((high_ref[source], low_ref[source]), split(wide[source, channel]))
        keep_ref[channel] = total[:width]
        send_ref[channel * width : (channel + 1) * width] = total[width : 2 * width]
        for row in range(count):
            at = (2 + row) * width
            own_ref[channel, row] = total[at : at + width]
            target = (2 + channel * count + row) * width
            send_ref[target : target + width] = total[at + count * width : at + (count + 1) * width]


def finish_kernel(*refs):
    keep_ref, own_ref, received_ref, base_ref, object_ref, dual_ref = refs[:6]
    spreads, (dual_out_ref, volume_ref, projected_ref) = refs[6:-3], refs[-3:]
    count, width = own_ref.shape[1:3]
    for channel in range(2):
        received = received_ref[channel * width : (channel + 1) * width]
        projection = -step_size * (keep_ref[channel] + received)
        for spread_ref in spreads:
            projection = projection + spread_ref[channel]
        projected_ref[0, channel] = projection
        dual_out_ref[0, channel] = dual_ref[0, channel] + object_ref[0, channel] - projection
        for row in range(count):
            at = (2 + channel * count + row) * width
            descent = own_ref[channel, row] + received_ref[at : at + width]
            volume_ref[channel, row] = base_ref[channel, row] - step_size * descent


def call(
    kernel, shapes, operands, scratch, flops, scalars=0, staged=(), numbers=(), copies=0, kind=jnp.float32, kinds={}
):
    held = sum(operand.nbytes for operand in operands[scalars:] + staged)
    held += 4 * sum(math.prod(shape) for shape in shapes)
    own = 4 * sum(math.prod(shape) for shape in scratch)
    outputs = [
        jax.ShapeDtypeStruct(shape, kinds.get(number, kind)) for number, shape in enumerate(shapes)
    ]
    scratch_shapes = [pltpu.VMEM(shape, jnp.float32) for shape in scratch]
    if staged and not copies:
        outputs += [jax.ShapeDtypeStruct(array.shape, array.dtype) for array in staged]
        copies = len(staged) + len(numbers)
        scratch_shapes += [pltpu.SMEM(array.shape, array.dtype) for array in numbers]
    staged += numbers
    if copies:
        scratch_shapes.append(pltpu.SemaphoreType.DMA((copies,)))
    in_specs = [SMEM] * scalars + [VMEM] * (len(operands) - scalars) + [HBM] * len(staged)
    return pl.pallas_call(
        kernel,
        out_shape=outputs,
        in_specs=in_specs,
        out_specs=[VMEM] * len(outputs),
        scratch_shapes=scratch_shapes,
        compiler_params=pltpu.CompilerParams(vmem_limit_bytes=held + own + SPARE_BYTES),
        cost_estimate=pl.CostEstimate(flops=flops, bytes_accessed=held, transcendentals=0),
    )(*operands, *(pltpu.with_memory_space_constraint(array, pltpu.HBM) for array in staged))


def body(
    transmission,
    scaled_dual,
    projected,
    volume,
    intensities,
    probe_wave,
    slot_first_rows,
    slot_first_columns,
    patch_counts,
    shift_table,
    tap_weight,
):
    width, length = transmission.shape[2:]
    count = volume.shape[1]
    scans, columns, tiles = (lax.axis_size(axis) for axis in ("scan", "angle", "tile"))
    assert scans % 2 == 0 and columns % 2 == 0 and tiles == 2 and lax.axis_size("groups") % 2 == 0
    rounds = []
    for first in (0, 1):
        pairs = [(i, i + 1) for i in range(first, scans - 1, 2)]
        route = [(s * tiles + t, d * tiles + t) for s, d in pairs for t in range(tiles)]
        route += [(target, source) for source, target in route]
        ends = {i for i in range(scans)} - {i for pair in pairs for i in pair}
        for scan in sorted(ends):
            route += [(scan * tiles + t, scan * tiles + 1 - t) for t in range(tiles)]
        rounds.append(route)
    swap = [(0, 1), (1, 0)]

    def exchange(block, number):
        return lax.ppermute(block, ("scan", "tile"), rounds[number])

    def across(block):
        return lax.ppermute(block, "tile", swap)

    edges = 2 * 2 * count
    (plane,) = call(
        pack_kernel,
        [(2 * width + -(-edges // SUBLANES) * SUBLANES, length)],
        (),
        [(edges, SUBLANES, length)],
        10**5,
        staged=(transmission, volume),
        copies=2 + edges,
    )
    plane_a = exchange(plane, 0)
    plane_b = exchange(plane, 1)
    tables = [jnp.asarray(table) for table in dft_tables(probe_wave.shape[1])]
    slots = slot_first_rows.shape[1]
    side = probe_wave.shape[1]
    probes, density, slot_numbers, rays, _, *held = call(
        prepare_kernel,
        [
            (slots, 2, side, side),
            (1, 3 * width, length),
            (slots, SUBLANES, side),
            (SUBLANES, length),
        ],
        (patch_counts,),
        [],
        10**7,
        1,
        (probe_wave, intensities, volume, *tables),
        (slot_first_rows, slot_first_columns, shift_table.T, tap_weight.T),
        kinds={2: jnp.int32},
    )
    volume_here = held[1]
    turns = [[(i, (i - turn) % columns) for i in range(columns)] for turn in range(columns)]
    rays_too = across(rays)
    own, rim_a, rim_b, row_a, row_b = call(
        patch_kernel,
        [(3, width, length)]
        + [(3 * width, length)] * 2
        + [(2, width + SUBLANES, length)] * 2,
        (probes, density, slot_numbers, plane, *held, plane_a, plane_b),
        [(2, 3 * width, length), (3, 3 * width, length)],
        10**9,
    )
    rim_a = exchange(rim_a, 0)
    rim_b = exchange(rim_b, 1)
    per_group, groups = columns * tiles, lax.axis_size("groups")
    bridge = []
    for group in range(groups):
        at = group * per_group
        pairs = [(at + i * tiles + 1, at + (i + 1) * tiles) for i in range(columns - 1)]
        bridge += pairs + [(target, source) for source, target in pairs]
        beyond = (groups - 1 - group) * per_group
        for outer in (0, per_group - 1):
            bridge.append((at + outer, beyond + outer))
    row_b = lax.ppermute(row_b, ("groups", "angle", "tile"), bridge)
    row_a = across(row_a)
    updated, residual, packed = call(
        fold_kernel,
        [
            transmission.shape,
            (2 * width, length),
            (2 * width + 2 * SUBLANES, length),
        ],
        (own, rim_a, rim_b, projected, scaled_dual, rays, rays_too),
        [],
        10**6,
    )
    by_column = [packed]
    for turn in range(1, columns):
        by_column.append(lax.ppermute(packed, "angle", turns[turn]))
    (base,) = call(
        variation_kernel,
        [volume.shape],
        (volume_here, plane_a, plane_b, row_a, row_b),
        [(count + 2, width + 16, length), (width + 16, length)],
        10**7,
    )
    route = []
    for scan in range(scans):
        for column in range(columns):
            lower = column < columns // 2
            target = scan + 1 if lower else scan - 1
            turned = column
            if not 0 <= target < scans:
                target, turned = scan, (column + columns // 2) % columns
            route.append((scan * columns + column, target * columns + turned))
    beside = lax.ppermute(base, ("scan", "angle"), route)
    here = jnp.stack([residual] + [block[: 2 * width] for block in by_column[1:]])
    side_a = exchange(here, 0)
    side_b = exchange(here, 1)
    high, low, new_transmission = call(
        operator_kernel,
        [(columns, (2 + 2 * count) * width, 3 * width)] * 2 + [transmission.shape],
        (*by_column, updated),
        [],
        10**8,
        kind=jnp.bfloat16,
        kinds={2: jnp.float32},
    )
    block = (columns, 2, width, length)
    keep, send = call(
        spread_kernel,
        [block, block],
        (shift_table.T, tap_weight.T, base, beside),
        [(count, 2, length // LANES, 2 * width, LANES)],
        10**7,
        2,
    )
    received = across(send)
    spreads = [keep[0], received[0]]
    for turn in range(1, columns):
        route = [(i, (i + turn) % columns) for i in range(columns)]
        spreads.append(lax.ppermute(keep[turn] + received[turn], "angle", route))
    keep, own, send = call(
        apply_kernel,
        [(2, width, length), volume.shape, ((2 + 2 * count) * width, length)],
        (here, side_a, side_b, high, low),
        [(columns, 2, 3 * width, length)],
        10**9,
    )
    received = across(send)
    new_dual, new_volume, new_projected = call(
        finish_kernel,
        [transmission.shape, volume.shape, transmission.shape],
        (keep, own, received, base, updated, scaled_dual, *spreads),
        [],
        10**6,
    )
    return (new_transmission, new_dual, new_volume, new_projected)


def solution(mesh):
    plane = P(("groups", "angle", "tile"), None, "scan", None)
    cells = P("groups", ("angle", "tile"), "scan", None)
    slots = P(("groups", "angle", "tile"), "scan")
    return jax.shard_map(
        body,
        mesh=mesh,
        in_specs=(
            plane,
            plane,
            plane,
            cells,
            P(("groups", "angle", "tile"), "scan", None, None),
            P("groups", None, None),
            slots,
            slots,
            slots,
            P(None, ("angle", "tile")),
            P(None, ("angle", "tile")),
        ),
        out_specs=(plane, plane, cells, plane),
        check_vma=False,
    )
```

```python
import math

import jax
import jax.numpy as jnp
import numpy as np
from jax import lax
from jax.experimental import pallas as pl
from jax.experimental.pallas import tpu as pltpu
from jax.sharding import PartitionSpec as P


penalty = 4.0
amplitude_step = 0.25
tv_weight = 1.0
smoothing = 0.05
step_size = 0.008

VMEM = pl.BlockSpec(memory_space=pltpu.VMEM)
SMEM = pl.BlockSpec(memory_space=pltpu.SMEM)
HBM = pl.BlockSpec(memory_space=pltpu.MemorySpace.HBM)
LANES = 128
SUBLANES = 8
SPARE_BYTES = 8 << 20


def split(values):
    high = values.astype(jnp.bfloat16)
    return (high, (values - high.astype(jnp.float32)).astype(jnp.bfloat16))


def product(left, right):
    total = jnp.dot(left[0], right[0], preferred_element_type=jnp.float32)
    total += jnp.dot(left[0], right[1], preferred_element_type=jnp.float32)
    return total + jnp.dot(left[1], right[0], preferred_element_type=jnp.float32)


def dft_tables(length):
    grid_ids = np.arange(length)
    radians = (grid_ids[:, None] * grid_ids[None, :] % length) * (2.0 * math.pi / length)
    cosine = np.cos(radians) / math.sqrt(length)
    sine = np.sin(radians) / math.sqrt(length)
    forward = np.block([[cosine, sine], [-sine, cosine]])
    tables = []
    for table in (forward, forward.T):
        high = table.astype(jnp.bfloat16)
        tables += [high, (table - high.astype(np.float64)).astype(jnp.bfloat16)]
    return tables


def tile_is_first():
    return lax.axis_index("tile") == 0


def scan_is_even():
    return lax.rem(lax.axis_index("scan"), 2) == 0


def pack_kernel(plane_ref, volume_ref, packed_ref, slabs, done):
    width = plane_ref.shape[2]
    count = volume_ref.shape[1]
    copies = [
        (plane_ref.at[0, channel], packed_ref.at[channel * width : (channel + 1) * width])
        for channel in range(2)
    ]
    for channel in range(2):
        for row in range(count):
            for side, at in enumerate((0, width - SUBLANES)):
                source = volume_ref.at[channel, row, at : at + SUBLANES]
                copies.append((source, slabs.at[(channel * count + row) * 2 + side]))
    copies = [
        pltpu.make_async_copy(source, target, done.at[number])
        for number, (source, target) in enumerate(copies)
    ]
    for copy in copies:
        copy.start()
    for copy in copies[2:]:
        copy.wait()
    for edge in range(slabs.shape[0]):
        take = 0 if edge % 2 == 0 else SUBLANES - 1
        packed_ref[2 * width + edge : 2 * width + edge + 1] = slabs[edge, take : take + 1]
    for copy in copies[:2]:
        copy.wait()


def has_second():
    scan = lax.axis_index("scan")
    return (scan > 0) & (scan < lax.axis_size("scan") - 1)


def edges_of(plane_a_ref, plane_b_ref, number, width):
    even = scan_is_even()
    at = 2 * width + 2 * number
    first_a, last_a = plane_a_ref[at : at + 1], plane_a_ref[at + 1 : at + 2]
    first_b, last_b = (
        jnp.where(has_second(), plane_b_ref[edge : edge + 1], 0.0) for edge in (at, at + 1)
    )
    return (jnp.where(even, last_b, last_a), jnp.where(even, first_a, first_b))


def slot_masks(rows_ref, columns_ref, count_ref, slot, side):
    lanes = lax.broadcasted_iota(jnp.int32, (side, side), 1)
    sublanes = lax.broadcasted_iota(jnp.int32, (side, side), 0)
    near_lanes = lanes >= rows_ref[0, slot]
    near_columns = sublanes >= columns_ref[0, slot]
    return (near_lanes, near_columns, jnp.full((side, side), slot < count_ref[0, 0]))


def place(totals, part, term, masks, width):
    side = term.shape[0]
    near_lanes, near_columns, live = masks
    inner = live & near_columns
    outer = (live & jnp.logical_not(near_columns))[:width]
    for start, lane_mask in ((0, near_lanes), (side, jnp.logical_not(near_lanes))):
        at = slice(start, start + side)
        totals[part, :side, at] += jnp.where(inner & lane_mask, term, 0.0)
        totals[part, side:, at] += jnp.where(outer & lane_mask[:width], term[:width], 0.0)


def prepare_kernel(count_ref, *refs):
    held = (len(refs) - 13) // 2
    sources = refs[: held + 4]
    probes_ref, density_ref, slots_ref, rays_ref = refs[held + 4 : held + 8]
    targets, done = refs[held + 8 : -1], refs[-1]
    rows_ref, columns_ref, shift_ref, weight_ref = targets[held:]
    copies = [
        pltpu.make_async_copy(source, target, done.at[number])
        for number, (source, target) in enumerate(zip(sources, targets))
    ]
    for copy in copies:
        copy.start()
    probe_ref = targets[0]
    side = probe_ref.shape[1]
    slots = probes_ref.shape[0]
    width = density_ref.shape[1] - side
    density_ref[...] = jnp.zeros_like(density_ref)
    for copy in copies[:1] + copies[held:]:
        copy.wait()
    places = lax.broadcasted_iota(jnp.int32, slots_ref.shape[1:], 0)
    for slot in range(slots):
        live = jnp.where(slot < count_ref[0, 0], 1, 0)
        numbers = jnp.where(places == 0, rows_ref[0, slot], columns_ref[0, slot])
        slots_ref[slot] = jnp.where(places == 2, live, numbers)
        turn = lax.rem(rows_ref[0, slot], side)
        probe = [
            pltpu.roll(pltpu.roll(probe_ref[part], columns_ref[0, slot], 0), turn, 1)
            for part in range(2)
        ]
        for part in range(2):
            probes_ref[slot, part] = probe[part]
        masks = slot_masks(rows_ref, columns_ref, count_ref, slot, side)
        place(density_ref, 0, probe[0] * probe[0] + probe[1] * probe[1], masks, width)
    places = lax.broadcasted_iota(jnp.int32, rays_ref.shape, 0)
    lanes = lax.broadcasted_iota(jnp.int32, rays_ref.shape, 1)
    rays = jnp.zeros(rays_ref.shape, jnp.float32)
    for row in range(shift_ref.shape[0]):
        for angle in range(shift_ref.shape[1]):
            shift = shift_ref[row, angle].astype(jnp.float32)
            here = lanes == angle
            rays = jnp.where(here & (places == 2 * row), shift, rays)
            rays = jnp.where(here & (places == 2 * row + 1), weight_ref[row, angle], rays)
    rays_ref[...] = rays
    for copy in copies[1:held]:
        copy.wait()


def patch_kernel(
    probes_ref,
    density_ref,
    slots_ref,
    plane_ref,
    intensity_ref,
    volume_ref,
    forward_high_ref,
    forward_low_ref,
    inverse_high_ref,
    inverse_low_ref,
    plane_a_ref,
    plane_b_ref,
    own_ref,
    rim_a_ref,
    rim_b_ref,
    row_a_ref,
    row_b_ref,
    wide,
    totals,
):
    width = volume_ref.shape[2]
    slots, _, side, _ = probes_ref.shape
    even = scan_is_even()
    at_a = pl.multiple_of(jnp.where(even, 2 * width, 0), width)
    at_b = pl.multiple_of(jnp.where(even, 0, 2 * width), width)
    for part in range(2):
        at = slice(part * width, (part + 1) * width)
        wide[part, width : 2 * width] = plane_ref[at]
        wide[part, pl.ds(at_a, width)] = plane_a_ref[at]
        wide[part, pl.ds(at_b, width)] = jnp.where(has_second(), plane_b_ref[at], 0.0)
    forward = (forward_high_ref[...], forward_low_ref[...])
    inverse = (inverse_high_ref[...], inverse_low_ref[...])
    waves, masks = [], []
    lanes = lax.broadcasted_iota(jnp.int32, (side, side), 1)
    sublanes = lax.broadcasted_iota(jnp.int32, (side, side), 0)
    for slot in range(slots):
        probe = probes_ref[slot]
        row, column, live = (
            jnp.broadcast_to(slots_ref[slot, number : number + 1], (side, side))
            for number in range(3)
        )
        near_lanes, near_columns = lanes >= row, sublanes >= column
        masks.append((near_lanes, near_columns, live > 0))
        window = []
        for part in range(2):
            near = jnp.where(near_lanes, wide[part, :side, :side], wide[part, :side, side:])
            wrapped = jnp.where(
                near_lanes[:width], wide[part, side:, :side], wide[part, side:, side:]
            )
            wrapped = jnp.concatenate([wrapped, near[width:]], axis=0)
            window.append(jnp.where(near_columns, near, wrapped))
        wave_real = probe[0] * window[0] - probe[1] * window[1]
        wave_imaginary = probe[0] * window[1] + probe[1] * window[0]
        waves.append(jnp.concatenate([wave_real, wave_imaginary], axis=1))
    half = product(split(jnp.concatenate(waves, axis=0)), inverse)
    half = jnp.concatenate(
        [
            jnp.concatenate(
                [half[slot * side : (slot + 1) * side, part * side : (part + 1) * side] for slot in range(slots)],
                axis=1,
            )
            for part in range(2)
        ],
        axis=0,
    )
    far = product(forward, split(half))
    far_real, far_imaginary = far[:side], far[side:]
    intensity = jnp.concatenate(
        [intensity_ref[0, slot].astype(jnp.float32) for slot in range(slots)], axis=1
    )
    factor = 1.0 - amplitude_step * (
        far_real * far_real + far_imaginary * far_imaginary - intensity
    )
    corrected = jnp.concatenate([far_real * factor, far_imaginary * factor], axis=0)
    half = product(inverse, split(corrected))
    half = jnp.concatenate(
        [
            jnp.concatenate(
                [half[part * side : (part + 1) * side, slot * side : (slot + 1) * side] for part in range(2)],
                axis=1,
            )
            for slot in range(slots)
        ],
        axis=0,
    )
    near = product(split(half), forward)
    totals[:2] = jnp.zeros_like(totals[:2])
    totals[2:] = density_ref[...]
    for slot in range(slots):
        probe = probes_ref[slot]
        near_real = near[slot * side : (slot + 1) * side, :side]
        near_imaginary = near[slot * side : (slot + 1) * side, side:]
        place(totals, 0, probe[0] * near_real + probe[1] * near_imaginary, masks[slot], width)
        place(totals, 1, probe[0] * near_imaginary - probe[1] * near_real, masks[slot], width)
    own_ref[...] = totals[:, width : 2 * width]
    for rim_ref, at in ((rim_a_ref, at_a), (rim_b_ref, at_b)):
        for part in range(totals.shape[0]):
            rim_ref[part * width : (part + 1) * width] = totals[part, pl.ds(at, width)]
    first_tile = tile_is_first()
    count = volume_ref.shape[1]
    for channel in range(2):
        rows = []
        for row in (0, count - 1):
            before, after = edges_of(plane_a_ref, plane_b_ref, channel * count + row, width)
            rows.append((volume_ref[channel, row], jnp.concatenate([before, after], axis=0)))
        for low, row_ref in ((jnp.logical_not(first_tile), row_a_ref), (first_tile, row_b_ref)):
            row_ref[channel, :width] = jnp.where(low, rows[0][0], rows[1][0])
            row_ref[channel, width : width + 2] = jnp.where(low, rows[0][1], rows[1][1])


def fold_kernel(
    own_ref, rim_a_ref, rim_b_ref, projected_ref, dual_ref, rays_ref, too_ref, object_ref, residual_ref, packed_ref
):
    width = own_ref.shape[1]
    second = has_second()
    sums = [
        own_ref[part]
        + rim_a_ref[part * width : (part + 1) * width]
        + jnp.where(second, rim_b_ref[part * width : (part + 1) * width], 0.0)
        for part in range(3)
    ]
    for part in range(2):
        target = projected_ref[0, part]
        dual = dual_ref[0, part]
        updated = (sums[part] + penalty * (target - dual)) / (sums[2] + penalty)
        object_ref[0, part] = updated
        residual = target - updated - dual
        residual_ref[part * width : (part + 1) * width] = residual
        packed_ref[part * width : (part + 1) * width] = residual
    packed_ref[2 * width : 2 * width + SUBLANES] = rays_ref[...]
    packed_ref[2 * width + SUBLANES :] = too_ref[...]


def variation_kernel(
    volume_ref, plane_a_ref, plane_b_ref, row_a_ref, row_b_ref, base_ref, padded, norms
):
    width = volume_ref.shape[2]
    length = volume_ref.shape[3]
    count = volume_ref.shape[1]
    margin = 8
    first_tile = tile_is_first()
    place = lax.axis_index("angle") * 2 + lax.axis_index("tile")
    bridged = (place > 0) & (place < 2 * lax.axis_size("angle") - 1)
    lanes = lax.broadcasted_iota(jnp.int32, (width, length), 1)
    first_lane = lanes == 0
    last_lane = lanes == length - 1
    for channel in range(2):
        for row in range(count):
            before, after = edges_of(plane_a_ref, plane_b_ref, channel * count + row, width)
            padded[row + 1, margin : margin + width] = volume_ref[channel, row]
            padded[row + 1, margin - 1 : margin] = before
            padded[row + 1, margin + width : margin + width + 1] = after
        row_a, row_b = row_a_ref[channel], jnp.where(bridged, row_b_ref[channel], 0.0)
        for row, beside in (
            (0, jnp.where(first_tile, row_b, row_a)),
            (count + 1, jnp.where(first_tile, row_a, row_b)),
        ):
            padded[row, margin : margin + width] = beside[:width]
            padded[row, margin - 1 : margin] = beside[width : width + 1]
            padded[row, margin + width : margin + width + 1] = beside[width + 1 : width + 2]
        previous_y = None
        for row in range(count + 1):
            here = padded[row, margin : margin + width]
            along_y = padded[row + 1, margin : margin + width] - here
            along_x = padded[row, margin + 1 : margin + width + 1] - here
            along_z = jnp.where(last_lane, 0.0, pltpu.roll(here, length - 1, 1)) - here
            inverse = lax.rsqrt(
                along_y * along_y + along_x * along_x + along_z * along_z + smoothing * smoothing
            )
            norm_y = along_y * inverse
            if row > 0:
                norm_x = along_x * inverse
                norm_z = along_z * inverse
                corner = padded[row, margin - 1 : margin]
                corner_y = padded[row + 1, margin - 1 : margin] - corner
                corner_x = here[:1] - corner
                corner_z = (
                    jnp.where(last_lane[:1], 0.0, pltpu.roll(corner, length - 1, 1)) - corner
                )
                corner_norm = corner_x * lax.rsqrt(
                    corner_y * corner_y
                    + corner_x * corner_x
                    + corner_z * corner_z
                    + smoothing * smoothing
                )
                norms[margin : margin + width] = norm_x
                norms[margin - 1 : margin] = corner_norm
                behind_x = norms[margin - 1 : margin + width - 1]
                ahead = here * lax.rsqrt(here * here + smoothing * smoothing)
                behind_z = jnp.where(first_lane, ahead, pltpu.roll(norm_z, 1, 1))
                divergence = (
                    norm_y - previous_y + (norm_x - behind_x) + (norm_z - behind_z)
                )
                base_ref[channel, row - 1] = here + (step_size * tv_weight) * divergence
            previous_y = norm_y


def spread_kernel(
    shift_ref, weight_ref, base_ref, beside_ref, *refs
):
    width = base_ref.shape[2]
    count = base_ref.shape[1]
    padded, tiles = refs[-1], lax.axis_size("tile")
    columns = (len(refs) - 1) // tiles
    me, tile, scan = lax.axis_index("angle"), lax.axis_index("tile"), lax.axis_index("scan")
    upper = me >= columns // 2
    chunks = [slice(at, at + LANES) for at in range(0, base_ref.shape[3], LANES)]
    exists = jnp.where(upper, scan < lax.axis_size("scan") - 1, scan > 0).astype(jnp.float32)
    own_at = pl.multiple_of(jnp.where(upper, 0, width), width)
    beside_at = pl.multiple_of(jnp.where(upper, width, 0), width)
    for row in range(count):
        for channel in range(2):
            for chunk, at in enumerate(chunks):
                padded[row, channel, chunk, pl.ds(own_at, width)] = base_ref[channel, row, :, at]
                padded[row, channel, chunk, pl.ds(beside_at, width)] = (
                    beside_ref[channel, row, :, at] * exists
                )
    for turn in range(columns):
        for flip, out_ref in ((0, refs[turn]), (1, refs[columns + turn])):
            angle = lax.rem(me + turn, columns) * tiles + (tile if flip == 0 else 1 - tile)
            for channel in range(2):
                for chunk, at in enumerate(chunks):
                    total = jnp.zeros((width, LANES), jnp.float32)
                    for row in range(count):
                        start = jnp.where(upper, 0, width) + shift_ref[row, angle]
                        fraction = weight_ref[row, angle]
                        total += (1.0 - fraction) * padded[row, channel, chunk, pl.ds(start, width)]
                        total += fraction * padded[row, channel, chunk, pl.ds(start + 1, width)]
                    out_ref[channel, :, at] = total


def operator_kernel(*refs):
    packed_refs, (object_ref, high_ref, low_ref, object_out_ref) = refs[:-4], refs[-4:]
    object_out_ref[...] = object_ref[...]
    tiles = lax.axis_size("tile")
    columns = len(packed_refs)
    rows_out, reach = high_ref.shape[1:]
    width = reach // 3
    count = rows_out // (2 * width) - 1
    me, tile, scan = lax.axis_index("angle"), lax.axis_index("tile"), lax.axis_index("scan")

    def taps(shape, first, table, row, step):
        lanes = lax.broadcasted_iota(jnp.int32, shape, 1)
        sublanes = lax.broadcasted_iota(jnp.int32, shape, 0)
        offset = (lanes - sublanes).astype(jnp.float32) - first
        shift = step * table[2 * row : 2 * row + 1]
        fraction = table[2 * row + 1 : 2 * row + 2]
        return jnp.where(offset == shift, 1.0 - fraction, 0.0) + jnp.where(
            offset == shift + step, fraction, 0.0
        )

    def angle_of(turn, flip):
        return lax.rem(me + turn, columns) * tiles + (tile if flip == 0 else 1 - tile)

    def table_of(turn, flip, angle):
        at = 2 * width + SUBLANES * flip
        tile_of = packed_refs[turn][at : at + SUBLANES]
        lanes = lax.broadcasted_iota(jnp.int32, tile_of.shape, 1)
        return jnp.sum(jnp.where(lanes == angle, tile_of, 0.0), axis=1, keepdims=True)

    cells = lax.broadcasted_iota(jnp.int32, (width, 2 * width), 1)
    forward = []
    backward = [[] for _ in range(columns)]
    for turn in range(columns):
        upper = lax.rem(me + turn, columns) >= columns // 2
        base_at = jnp.where(upper, 0, width)
        first_cell = jnp.where(upper, 0, jnp.where(scan > 0, 0, width))
        end_cell = jnp.where(upper & (scan == lax.axis_size("scan") - 1), width, 2 * width)
        inside = (cells >= first_cell) & (cells < end_cell)
        for flip in range(tiles):
            for row in range(count):
                parts = []
                for own in range(tiles):
                    table = table_of(turn, flip, angle_of(0, own))
                    part = taps((width, 2 * width), base_at.astype(jnp.float32), table, row, 1.0)
                    parts.append(jnp.where(inside, part, 0.0))
                forward.append(jnp.concatenate(parts, axis=0))
                for source in range(columns):
                    table = table_of(turn, flip, angle_of(source, 0))
                    first = (width - base_at).astype(jnp.float32)
                    backward[source].append(taps((2 * width, reach), first, table, row, -1.0))
    left = split(jnp.concatenate(forward, axis=1))
    for source in range(columns):
        both = product(left, split(jnp.concatenate(backward[source], axis=0)))
        blocks = [both]
        for flip in range(tiles):
            for row in range(count):
                table = table_of(0, flip, angle_of(source, 0))
                blocks.append(taps((width, reach), float(width), table, row, -1.0))
        high_ref[source], low_ref[source] = split(jnp.concatenate(blocks, axis=0))


def apply_kernel(here_ref, side_a_ref, side_b_ref, high_ref, low_ref, keep_ref, own_ref, send_ref, wide):
    width = keep_ref.shape[1]
    columns = here_ref.shape[0]
    count = own_ref.shape[1]
    even = scan_is_even()
    at_a = pl.multiple_of(jnp.where(even, 2 * width, 0), width)
    at_b = pl.multiple_of(jnp.where(even, 0, 2 * width), width)
    for source in range(columns):
        for channel in range(2):
            at = slice(channel * width, (channel + 1) * width)
            wide[source, channel, width : 2 * width] = here_ref[source, at]
            wide[source, channel, pl.ds(at_a, width)] = side_a_ref[source, at]
            wide[source, channel, pl.ds(at_b, width)] = jnp.where(
                has_second(), side_b_ref[source, at], 0.0
            )
    for channel in range(2):
        total = 0.0
        for source in range(columns):
            total += product((high_ref[source], low_ref[source]), split(wide[source, channel]))
        keep_ref[channel] = total[:width]
        send_ref[channel * width : (channel + 1) * width] = total[width : 2 * width]
        for row in range(count):
            at = (2 + row) * width
            own_ref[channel, row] = total[at : at + width]
            target = (2 + channel * count + row) * width
            send_ref[target : target + width] = total[at + count * width : at + (count + 1) * width]


def finish_kernel(*refs):
    keep_ref, own_ref, received_ref, base_ref, object_ref, dual_ref = refs[:6]
    spreads, (dual_out_ref, volume_ref, projected_ref) = refs[6:-3], refs[-3:]
    count, width = own_ref.shape[1:3]
    for channel in range(2):
        received = received_ref[channel * width : (channel + 1) * width]
        projection = -step_size * (keep_ref[channel] + received)
        for spread_ref in spreads:
            projection = projection + spread_ref[channel]
        projected_ref[0, channel] = projection
        dual_out_ref[0, channel] = dual_ref[0, channel] + object_ref[0, channel] - projection
        for row in range(count):
            at = (2 + channel * count + row) * width
            descent = own_ref[channel, row] + received_ref[at : at + width]
            volume_ref[channel, row] = base_ref[channel, row] - step_size * descent


def call(
    kernel, shapes, operands, scratch, flops, scalars=0, staged=(), numbers=(), copies=0, kind=jnp.float32, kinds={}
):
    held = sum(operand.nbytes for operand in operands[scalars:] + staged)
    held += 4 * sum(math.prod(shape) for shape in shapes)
    own = 4 * sum(math.prod(shape) for shape in scratch)
    outputs = [
        jax.ShapeDtypeStruct(shape, kinds.get(number, kind)) for number, shape in enumerate(shapes)
    ]
    scratch_shapes = [pltpu.VMEM(shape, jnp.float32) for shape in scratch]
    if staged and not copies:
        outputs += [jax.ShapeDtypeStruct(array.shape, array.dtype) for array in staged]
        copies = len(staged) + len(numbers)
        scratch_shapes += [pltpu.SMEM(array.shape, array.dtype) for array in numbers]
    staged += numbers
    if copies:
        scratch_shapes.append(pltpu.SemaphoreType.DMA((copies,)))
    in_specs = [SMEM] * scalars + [VMEM] * (len(operands) - scalars) + [HBM] * len(staged)
    return pl.pallas_call(
        kernel,
        out_shape=outputs,
        in_specs=in_specs,
        out_specs=[VMEM] * len(outputs),
        scratch_shapes=scratch_shapes,
        compiler_params=pltpu.CompilerParams(vmem_limit_bytes=held + own + SPARE_BYTES),
        cost_estimate=pl.CostEstimate(flops=flops, bytes_accessed=held, transcendentals=0),
    )(*operands, *(pltpu.with_memory_space_constraint(array, pltpu.HBM) for array in staged))


def body(
    transmission,
    scaled_dual,
    projected,
    volume,
    intensities,
    probe_wave,
    slot_first_rows,
    slot_first_columns,
    patch_counts,
    shift_table,
    tap_weight,
):
    width, length = transmission.shape[2:]
    count = volume.shape[1]
    scans, columns, tiles = (lax.axis_size(axis) for axis in ("scan", "angle", "tile"))
    assert scans % 2 == 0 and columns % 2 == 0 and tiles == 2 and lax.axis_size("groups") % 2 == 0
    rounds = []
    for first in (0, 1):
        pairs = [(i, i + 1) for i in range(first, scans - 1, 2)]
        route = [(s * tiles + t, d * tiles + t) for s, d in pairs for t in range(tiles)]
        route += [(target, source) for source, target in route]
        ends = {i for i in range(scans)} - {i for pair in pairs for i in pair}
        for scan in sorted(ends):
            route += [(scan * tiles + t, scan * tiles + 1 - t) for t in range(tiles)]
        rounds.append(route)
    swap = [(0, 1), (1, 0)]

    def exchange(block, number):
        return lax.ppermute(block, ("scan", "tile"), rounds[number])

    def across(block):
        return lax.ppermute(block, "tile", swap)

    edges = 2 * 2 * count
    (plane,) = call(
        pack_kernel,
        [(2 * width + -(-edges // SUBLANES) * SUBLANES, length)],
        (),
        [(edges, SUBLANES, length)],
        10**5,
        staged=(transmission, volume),
        copies=2 + edges,
    )
    plane_a = exchange(plane, 0)
    plane_b = exchange(plane, 1)
    tables = [jnp.asarray(table) for table in dft_tables(probe_wave.shape[1])]
    slots = slot_first_rows.shape[1]
    side = probe_wave.shape[1]
    probes, density, slot_numbers, rays, _, *held = call(
        prepare_kernel,
        [
            (slots, 2, side, side),
            (1, 3 * width, length),
            (slots, SUBLANES, side),
            (SUBLANES, length),
        ],
        (patch_counts,),
        [],
        10**7,
        1,
        (probe_wave, intensities, volume, *tables),
        (slot_first_rows, slot_first_columns, shift_table.T, tap_weight.T),
        kinds={2: jnp.int32},
    )
    volume_here = held[1]
    turns = [[(i, (i - turn) % columns) for i in range(columns)] for turn in range(columns)]
    rays_too = across(rays)
    own, rim_a, rim_b, row_a, row_b = call(
        patch_kernel,
        [(3, width, length)]
        + [(3 * width, length)] * 2
        + [(2, width + SUBLANES, length)] * 2,
        (probes, density, slot_numbers, plane, *held, plane_a, plane_b),
        [(2, 3 * width, length), (3, 3 * width, length)],
        10**9,
    )
    rim_a = exchange(rim_a, 0)
    rim_b = exchange(rim_b, 1)
    per_group, groups = columns * tiles, lax.axis_size("groups")
    bridge = []
    for group in range(groups):
        at = group * per_group
        pairs = [(at + i * tiles + 1, at + (i + 1) * tiles) for i in range(columns - 1)]
        bridge += pairs + [(target, source) for source, target in pairs]
        beyond = (groups - 1 - group) * per_group
        for outer in (0, per_group - 1):
            bridge.append((at + outer, beyond + outer))
    row_b = lax.ppermute(row_b, ("groups", "angle", "tile"), bridge)
    row_a = across(row_a)
    updated, residual, packed = call(
        fold_kernel,
        [
            transmission.shape,
            (2 * width, length),
            (2 * width + 2 * SUBLANES, length),
        ],
        (own, rim_a, rim_b, projected, scaled_dual, rays, rays_too),
        [],
        10**6,
    )
    by_column = [packed]
    for turn in range(1, columns):
        by_column.append(lax.ppermute(packed, "angle", turns[turn]))
    (base,) = call(
        variation_kernel,
        [volume.shape],
        (volume_here, plane_a, plane_b, row_a, row_b),
        [(count + 2, width + 16, length), (width + 16, length)],
        10**7,
    )
    route = []
    for scan in range(scans):
        for column in range(columns):
            lower = column < columns // 2
            target = scan + 1 if lower else scan - 1
            turned = column
            if not 0 <= target < scans:
                target, turned = scan, (column + columns // 2) % columns
            route.append((scan * columns + column, target * columns + turned))
    beside = lax.ppermute(base, ("scan", "angle"), route)
    here = jnp.stack([residual] + [block[: 2 * width] for block in by_column[1:]])
    side_a = exchange(here, 0)
    side_b = exchange(here, 1)
    high, low, new_transmission = call(
        operator_kernel,
        [(columns, (2 + 2 * count) * width, 3 * width)] * 2 + [transmission.shape],
        (*by_column, updated),
        [],
        10**8,
        kind=jnp.bfloat16,
        kinds={2: jnp.float32},
    )
    parts = call(
        spread_kernel,
        [(2, width, length)] * (columns * tiles),
        (shift_table.T, tap_weight.T, base, beside),
        [(count, 2, length // LANES, 2 * width, LANES)],
        10**7,
        2,
    )
    spreads = [parts[0]]
    for turn in range(columns):
        for flip in range(tiles):
            route = [
                (x * tiles + t, (x + turn) % columns * tiles + (t ^ flip))
                for x in range(columns)
                for t in range(tiles)
            ]
            if turn or flip:
                spreads.append(lax.ppermute(parts[flip * columns + turn], ("angle", "tile"), route))
    keep, own, send = call(
        apply_kernel,
        [(2, width, length), volume.shape, ((2 + 2 * count) * width, length)],
        (here, side_a, side_b, high, low),
        [(columns, 2, 3 * width, length)],
        10**9,
    )
    received = across(send)
    new_dual, new_volume, new_projected = call(
        finish_kernel,
        [transmission.shape, volume.shape, transmission.shape],
        (keep, own, received, base, updated, scaled_dual, *spreads),
        [],
        10**6,
    )
    return (new_transmission, new_dual, new_volume, new_projected)


def solution(mesh):
    plane = P(("groups", "angle", "tile"), None, "scan", None)
    cells = P("groups", ("angle", "tile"), "scan", None)
    slots = P(("groups", "angle", "tile"), "scan")
    return jax.shard_map(
        body,
        mesh=mesh,
        in_specs=(
            plane,
            plane,
            plane,
            cells,
            P(("groups", "angle", "tile"), "scan", None, None),
            P("groups", None, None),
            slots,
            slots,
            slots,
            P(None, ("angle", "tile")),
            P(None, ("angle", "tile")),
        ),
        out_specs=(plane, plane, cells, plane),
        check_vma=False,
    )
```

```python
import math

import jax
import jax.numpy as jnp
import numpy as np
from jax import lax
from jax.experimental import pallas as pl
from jax.experimental.pallas import tpu as pltpu
from jax.sharding import PartitionSpec as P


penalty = 4.0
amplitude_step = 0.25
tv_weight = 1.0
smoothing = 0.05
step_size = 0.008

VMEM = pl.BlockSpec(memory_space=pltpu.VMEM)
SMEM = pl.BlockSpec(memory_space=pltpu.SMEM)
HBM = pl.BlockSpec(memory_space=pltpu.MemorySpace.HBM)
LANES = 128
SUBLANES = 8
SPARE_BYTES = 8 << 20


def split(values):
    high = values.astype(jnp.bfloat16)
    return (high, (values - high.astype(jnp.float32)).astype(jnp.bfloat16))


def product(left, right):
    total = jnp.dot(left[0], right[0], preferred_element_type=jnp.float32)
    total += jnp.dot(left[0], right[1], preferred_element_type=jnp.float32)
    return total + jnp.dot(left[1], right[0], preferred_element_type=jnp.float32)


def dft_tables(length):
    grid_ids = np.arange(length)
    radians = (grid_ids[:, None] * grid_ids[None, :] % length) * (2.0 * math.pi / length)
    cosine = np.cos(radians) / math.sqrt(length)
    sine = np.sin(radians) / math.sqrt(length)
    forward = np.block([[cosine, sine], [-sine, cosine]])
    tables = []
    for table in (forward, forward.T):
        high = table.astype(jnp.bfloat16)
        tables += [high, (table - high.astype(np.float64)).astype(jnp.bfloat16)]
    return tables


def tile_is_first():
    return lax.axis_index("tile") == 0


def scan_is_even():
    return lax.rem(lax.axis_index("scan"), 2) == 0


def pack_kernel(plane_ref, volume_ref, packed_ref, slabs, done):
    width = plane_ref.shape[2]
    count = volume_ref.shape[1]
    copies = [
        (plane_ref.at[0, channel], packed_ref.at[channel * width : (channel + 1) * width])
        for channel in range(2)
    ]
    for channel in range(2):
        for row in range(count):
            for side, at in enumerate((0, width - SUBLANES)):
                source = volume_ref.at[channel, row, at : at + SUBLANES]
                copies.append((source, slabs.at[(channel * count + row) * 2 + side]))
    copies = [
        pltpu.make_async_copy(source, target, done.at[number])
        for number, (source, target) in enumerate(copies)
    ]
    for copy in copies:
        copy.start()
    for copy in copies[2:]:
        copy.wait()
    for edge in range(slabs.shape[0]):
        take = 0 if edge % 2 == 0 else SUBLANES - 1
        packed_ref[2 * width + edge : 2 * width + edge + 1] = slabs[edge, take : take + 1]
    for copy in copies[:2]:
        copy.wait()


def has_second():
    scan = lax.axis_index("scan")
    return (scan > 0) & (scan < lax.axis_size("scan") - 1)


def edges_of(plane_a_ref, plane_b_ref, number, width):
    even = scan_is_even()
    at = 2 * width + 2 * number
    first_a, last_a = plane_a_ref[at : at + 1], plane_a_ref[at + 1 : at + 2]
    first_b, last_b = (
        jnp.where(has_second(), plane_b_ref[edge : edge + 1], 0.0) for edge in (at, at + 1)
    )
    return (jnp.where(even, last_b, last_a), jnp.where(even, first_a, first_b))


def slot_masks(rows_ref, columns_ref, count_ref, slot, side):
    lanes = lax.broadcasted_iota(jnp.int32, (side, side), 1)
    sublanes = lax.broadcasted_iota(jnp.int32, (side, side), 0)
    near_lanes = lanes >= rows_ref[0, slot]
    near_columns = sublanes >= columns_ref[0, slot]
    return (near_lanes, near_columns, jnp.full((side, side), slot < count_ref[0, 0]))


def place(totals, part, term, masks, width):
    side = term.shape[0]
    near_lanes, near_columns, live = masks
    inner = live & near_columns
    outer = (live & jnp.logical_not(near_columns))[:width]
    for start, lane_mask in ((0, near_lanes), (side, jnp.logical_not(near_lanes))):
        at = slice(start, start + side)
        totals[part, :side, at] += jnp.where(inner & lane_mask, term, 0.0)
        totals[part, side:, at] += jnp.where(outer & lane_mask[:width], term[:width], 0.0)


def prepare_kernel(count_ref, *refs):
    held = (len(refs) - 13) // 2
    sources = refs[: held + 4]
    probes_ref, density_ref, slots_ref, rays_ref = refs[held + 4 : held + 8]
    targets, done = refs[held + 8 : -1], refs[-1]
    rows_ref, columns_ref, shift_ref, weight_ref = targets[held:]
    copies = [
        pltpu.make_async_copy(source, target, done.at[number])
        for number, (source, target) in enumerate(zip(sources, targets))
    ]
    for copy in copies:
        copy.start()
    probe_ref = targets[0]
    side = probe_ref.shape[1]
    slots = probes_ref.shape[0]
    width = density_ref.shape[1] - side
    density_ref[...] = jnp.zeros_like(density_ref)
    for copy in copies[:1] + copies[held:]:
        copy.wait()
    places = lax.broadcasted_iota(jnp.int32, slots_ref.shape[1:], 0)
    for slot in range(slots):
        live = jnp.where(slot < count_ref[0, 0], 1, 0)
        numbers = jnp.where(places == 0, rows_ref[0, slot], columns_ref[0, slot])
        slots_ref[slot] = jnp.where(places == 2, live, numbers)
        turn = lax.rem(rows_ref[0, slot], side)
        probe = [
            pltpu.roll(pltpu.roll(probe_ref[part], columns_ref[0, slot], 0), turn, 1)
            for part in range(2)
        ]
        for part in range(2):
            probes_ref[slot, part] = probe[part]
        masks = slot_masks(rows_ref, columns_ref, count_ref, slot, side)
        place(density_ref, 0, probe[0] * probe[0] + probe[1] * probe[1], masks, width)
    places = lax.broadcasted_iota(jnp.int32, rays_ref.shape, 0)
    lanes = lax.broadcasted_iota(jnp.int32, rays_ref.shape, 1)
    rays = jnp.zeros(rays_ref.shape, jnp.float32)
    for row in range(shift_ref.shape[0]):
        for angle in range(shift_ref.shape[1]):
            shift = shift_ref[row, angle].astype(jnp.float32)
            here = lanes == angle
            rays = jnp.where(here & (places == 2 * row), shift, rays)
            rays = jnp.where(here & (places == 2 * row + 1), weight_ref[row, angle], rays)
    rays_ref[...] = rays
    for copy in copies[1:held]:
        copy.wait()


def patch_kernel(
    probes_ref,
    density_ref,
    slots_ref,
    plane_ref,
    intensity_ref,
    volume_ref,
    forward_high_ref,
    forward_low_ref,
    inverse_high_ref,
    inverse_low_ref,
    plane_a_ref,
    plane_b_ref,
    own_ref,
    rim_a_ref,
    rim_b_ref,
    row_a_ref,
    row_b_ref,
    wide,
    totals,
):
    width = volume_ref.shape[2]
    slots, _, side, _ = probes_ref.shape
    even = scan_is_even()
    at_a = pl.multiple_of(jnp.where(even, 2 * width, 0), width)
    at_b = pl.multiple_of(jnp.where(even, 0, 2 * width), width)
    for part in range(2):
        at = slice(part * width, (part + 1) * width)
        wide[part, width : 2 * width] = plane_ref[at]
        wide[part, pl.ds(at_a, width)] = plane_a_ref[at]
        wide[part, pl.ds(at_b, width)] = jnp.where(has_second(), plane_b_ref[at], 0.0)
    forward = (forward_high_ref[...], forward_low_ref[...])
    inverse = (inverse_high_ref[...], inverse_low_ref[...])
    waves, masks = [], []
    lanes = lax.broadcasted_iota(jnp.int32, (side, side), 1)
    sublanes = lax.broadcasted_iota(jnp.int32, (side, side), 0)
    for slot in range(slots):
        probe = probes_ref[slot]
        row, column, live = (
            jnp.broadcast_to(slots_ref[slot, number : number + 1], (side, side))
            for number in range(3)
        )
        near_lanes, near_columns = lanes >= row, sublanes >= column
        masks.append((near_lanes, near_columns, live > 0))
        window = []
        for part in range(2):
            near = jnp.where(near_lanes, wide[part, :side, :side], wide[part, :side, side:])
            wrapped = jnp.where(
                near_lanes[:width], wide[part, side:, :side], wide[part, side:, side:]
            )
            wrapped = jnp.concatenate([wrapped, near[width:]], axis=0)
            window.append(jnp.where(near_columns, near, wrapped))
        wave_real = probe[0] * window[0] - probe[1] * window[1]
        wave_imaginary = probe[0] * window[1] + probe[1] * window[0]
        waves.append(jnp.concatenate([wave_real, wave_imaginary], axis=1))
    half = product(split(jnp.concatenate(waves, axis=0)), inverse)
    half = jnp.concatenate(
        [
            jnp.concatenate(
                [half[slot * side : (slot + 1) * side, part * side : (part + 1) * side] for slot in range(slots)],
                axis=1,
            )
            for part in range(2)
        ],
        axis=0,
    )
    far = product(forward, split(half))
    far_real, far_imaginary = far[:side], far[side:]
    intensity = jnp.concatenate(
        [intensity_ref[0, slot].astype(jnp.float32) for slot in range(slots)], axis=1
    )
    factor = 1.0 - amplitude_step * (
        far_real * far_real + far_imaginary * far_imaginary - intensity
    )
    corrected = jnp.concatenate([far_real * factor, far_imaginary * factor], axis=0)
    half = product(inverse, split(corrected))
    half = jnp.concatenate(
        [
            jnp.concatenate(
                [half[part * side : (part + 1) * side, slot * side : (slot + 1) * side] for part in range(2)],
                axis=1,
            )
            for slot in range(slots)
        ],
        axis=0,
    )
    near = product(split(half), forward)
    totals[:2] = jnp.zeros_like(totals[:2])
    totals[2:] = density_ref[...]
    for slot in range(slots):
        probe = probes_ref[slot]
        near_real = near[slot * side : (slot + 1) * side, :side]
        near_imaginary = near[slot * side : (slot + 1) * side, side:]
        place(totals, 0, probe[0] * near_real + probe[1] * near_imaginary, masks[slot], width)
        place(totals, 1, probe[0] * near_imaginary - probe[1] * near_real, masks[slot], width)
    own_ref[...] = totals[:, width : 2 * width]
    for rim_ref, at in ((rim_a_ref, at_a), (rim_b_ref, at_b)):
        for part in range(totals.shape[0]):
            rim_ref[part * width : (part + 1) * width] = totals[part, pl.ds(at, width)]
    first_tile = tile_is_first()
    count = volume_ref.shape[1]
    for channel in range(2):
        rows = []
        for row in (0, count - 1):
            before, after = edges_of(plane_a_ref, plane_b_ref, channel * count + row, width)
            rows.append((volume_ref[channel, row], jnp.concatenate([before, after], axis=0)))
        for low, row_ref in ((jnp.logical_not(first_tile), row_a_ref), (first_tile, row_b_ref)):
            row_ref[channel, :width] = jnp.where(low, rows[0][0], rows[1][0])
            row_ref[channel, width : width + 2] = jnp.where(low, rows[0][1], rows[1][1])


def fold_kernel(
    own_ref, rim_a_ref, rim_b_ref, projected_ref, dual_ref, rays_ref, too_ref, object_ref, residual_ref, packed_ref
):
    width = own_ref.shape[1]
    second = has_second()
    sums = [
        own_ref[part]
        + rim_a_ref[part * width : (part + 1) * width]
        + jnp.where(second, rim_b_ref[part * width : (part + 1) * width], 0.0)
        for part in range(3)
    ]
    for part in range(2):
        target = projected_ref[0, part]
        dual = dual_ref[0, part]
        updated = (sums[part] + penalty * (target - dual)) / (sums[2] + penalty)
        object_ref[0, part] = updated
        residual = target - updated - dual
        residual_ref[part * width : (part + 1) * width] = residual
        packed_ref[part * width : (part + 1) * width] = residual
    packed_ref[2 * width : 2 * width + SUBLANES] = rays_ref[...]
    packed_ref[2 * width + SUBLANES :] = too_ref[...]


def variation_kernel(
    volume_ref, plane_a_ref, plane_b_ref, row_a_ref, row_b_ref, base_ref, padded, norms
):
    width = volume_ref.shape[2]
    length = volume_ref.shape[3]
    count = volume_ref.shape[1]
    margin = 8
    first_tile = tile_is_first()
    place = lax.axis_index("angle") * 2 + lax.axis_index("tile")
    bridged = (place > 0) & (place < 2 * lax.axis_size("angle") - 1)
    lanes = lax.broadcasted_iota(jnp.int32, (width, length), 1)
    first_lane = lanes == 0
    last_lane = lanes == length - 1
    for channel in range(2):
        for row in range(count):
            before, after = edges_of(plane_a_ref, plane_b_ref, channel * count + row, width)
            padded[row + 1, margin : margin + width] = volume_ref[channel, row]
            padded[row + 1, margin - 1 : margin] = before
            padded[row + 1, margin + width : margin + width + 1] = after
        row_a, row_b = row_a_ref[channel], jnp.where(bridged, row_b_ref[channel], 0.0)
        for row, beside in (
            (0, jnp.where(first_tile, row_b, row_a)),
            (count + 1, jnp.where(first_tile, row_a, row_b)),
        ):
            padded[row, margin : margin + width] = beside[:width]
            padded[row, margin - 1 : margin] = beside[width : width + 1]
            padded[row, margin + width : margin + width + 1] = beside[width + 1 : width + 2]
        previous_y = None
        for row in range(count + 1):
            here = padded[row, margin : margin + width]
            along_y = padded[row + 1, margin : margin + width] - here
            along_x = padded[row, margin + 1 : margin + width + 1] - here
            along_z = jnp.where(last_lane, 0.0, pltpu.roll(here, length - 1, 1)) - here
            inverse = lax.rsqrt(
                along_y * along_y + along_x * along_x + along_z * along_z + smoothing * smoothing
            )
            norm_y = along_y * inverse
            if row > 0:
                norm_x = along_x * inverse
                norm_z = along_z * inverse
                corner = padded[row, margin - 1 : margin]
                corner_y = padded[row + 1, margin - 1 : margin] - corner
                corner_x = here[:1] - corner
                corner_z = (
                    jnp.where(last_lane[:1], 0.0, pltpu.roll(corner, length - 1, 1)) - corner
                )
                corner_norm = corner_x * lax.rsqrt(
                    corner_y * corner_y
                    + corner_x * corner_x
                    + corner_z * corner_z
                    + smoothing * smoothing
                )
                norms[margin : margin + width] = norm_x
                norms[margin - 1 : margin] = corner_norm
                behind_x = norms[margin - 1 : margin + width - 1]
                ahead = here * lax.rsqrt(here * here + smoothing * smoothing)
                behind_z = jnp.where(first_lane, ahead, pltpu.roll(norm_z, 1, 1))
                divergence = (
                    norm_y - previous_y + (norm_x - behind_x) + (norm_z - behind_z)
                )
                base_ref[channel, row - 1] = here + (step_size * tv_weight) * divergence
            previous_y = norm_y


def spread_kernel(
    shift_ref, weight_ref, base_ref, beside_ref, keep_ref, send_ref, padded
):
    width = base_ref.shape[2]
    count = base_ref.shape[1]
    columns, tiles = keep_ref.shape[0], lax.axis_size("tile")
    me, tile, scan = lax.axis_index("angle"), lax.axis_index("tile"), lax.axis_index("scan")
    upper = me >= columns // 2
    chunks = [slice(at, at + LANES) for at in range(0, base_ref.shape[3], LANES)]
    exists = jnp.where(upper, scan < lax.axis_size("scan") - 1, scan > 0).astype(jnp.float32)
    own_at = pl.multiple_of(jnp.where(upper, 0, width), width)
    beside_at = pl.multiple_of(jnp.where(upper, width, 0), width)
    for row in range(count):
        for channel in range(2):
            for chunk, at in enumerate(chunks):
                padded[row, channel, chunk, pl.ds(own_at, width)] = base_ref[channel, row, :, at]
                padded[row, channel, chunk, pl.ds(beside_at, width)] = (
                    beside_ref[channel, row, :, at] * exists
                )
    for turn in range(columns):
        for flip, out_ref in ((0, keep_ref), (1, send_ref)):
            angle = lax.rem(me + turn, columns) * tiles + (tile if flip == 0 else 1 - tile)
            for channel in range(2):
                for chunk, at in enumerate(chunks):
                    total = jnp.zeros((width, LANES), jnp.float32)
                    for row in range(count):
                        start = jnp.where(upper, 0, width) + shift_ref[row, angle]
                        fraction = weight_ref[row, angle]
                        total += (1.0 - fraction) * padded[row, channel, chunk, pl.ds(start, width)]
                        total += fraction * padded[row, channel, chunk, pl.ds(start + 1, width)]
                    out_ref[turn, channel, :, at] = total


def operator_kernel(*refs):
    packed_refs, (object_ref, high_ref, low_ref, object_out_ref) = refs[:-4], refs[-4:]
    object_out_ref[...] = object_ref[...]
    tiles = lax.axis_size("tile")
    columns = len(packed_refs)
    rows_out, reach = high_ref.shape[1:]
    width = reach // 3
    count = rows_out // (2 * width) - 1
    me, tile, scan = lax.axis_index("angle"), lax.axis_index("tile"), lax.axis_index("scan")

    def taps(shape, first, table, row, step):
        lanes = lax.broadcasted_iota(jnp.int32, shape, 1)
        sublanes = lax.broadcasted_iota(jnp.int32, shape, 0)
        offset = (lanes - sublanes).astype(jnp.float32) - first
        shift = step * table[2 * row : 2 * row + 1]
        fraction = table[2 * row + 1 : 2 * row + 2]
        return jnp.where(offset == shift, 1.0 - fraction, 0.0) + jnp.where(
            offset == shift + step, fraction, 0.0
        )

    def angle_of(turn, flip):
        return lax.rem(me + turn, columns) * tiles + (tile if flip == 0 else 1 - tile)

    def table_of(turn, flip, angle):
        at = 2 * width + SUBLANES * flip
        tile_of = packed_refs[turn][at : at + SUBLANES]
        lanes = lax.broadcasted_iota(jnp.int32, tile_of.shape, 1)
        return jnp.sum(jnp.where(lanes == angle, tile_of, 0.0), axis=1, keepdims=True)

    cells = lax.broadcasted_iota(jnp.int32, (width, 2 * width), 1)
    forward = []
    backward = [[] for _ in range(columns)]
    for turn in range(columns):
        upper = lax.rem(me + turn, columns) >= columns // 2
        base_at = jnp.where(upper, 0, width)
        first_cell = jnp.where(upper, 0, jnp.where(scan > 0, 0, width))
        end_cell = jnp.where(upper & (scan == lax.axis_size("scan") - 1), width, 2 * width)
        inside = (cells >= first_cell) & (cells < end_cell)
        for flip in range(tiles):
            for row in range(count):
                parts = []
                for own in range(tiles):
                    table = table_of(turn, flip, angle_of(0, own))
                    part = taps((width, 2 * width), base_at.astype(jnp.float32), table, row, 1.0)
                    parts.append(jnp.where(inside, part, 0.0))
                forward.append(jnp.concatenate(parts, axis=0))
                for source in range(columns):
                    table = table_of(turn, flip, angle_of(source, 0))
                    first = (width - base_at).astype(jnp.float32)
                    backward[source].append(taps((2 * width, reach), first, table, row, -1.0))
    left = split(jnp.concatenate(forward, axis=1))
    for source in range(columns):
        both = product(left, split(jnp.concatenate(backward[source], axis=0)))
        blocks = [both]
        for flip in range(tiles):
            for row in range(count):
                table = table_of(0, flip, angle_of(source, 0))
                blocks.append(taps((width, reach), float(width), table, row, -1.0))
        high_ref[source], low_ref[source] = split(jnp.concatenate(blocks, axis=0))


def apply_kernel(here_ref, side_a_ref, side_b_ref, high_ref, low_ref, keep_ref, own_ref, send_ref, wide):
    width = keep_ref.shape[1]
    columns = here_ref.shape[0]
    count = own_ref.shape[1]
    even = scan_is_even()
    at_a = pl.multiple_of(jnp.where(even, 2 * width, 0), width)
    at_b = pl.multiple_of(jnp.where(even, 0, 2 * width), width)
    for source in range(columns):
        for channel in range(2):
            at = slice(channel * width, (channel + 1) * width)
            wide[source, channel, width : 2 * width] = here_ref[source, at]
            wide[source, channel, pl.ds(at_a, width)] = side_a_ref[source, at]
            wide[source, channel, pl.ds(at_b, width)] = jnp.where(
                has_second(), side_b_ref[source, at], 0.0
            )
    for channel in range(2):
        total = 0.0
        for source in range(columns):
            total += product((high_ref[source], low_ref[source]), split(wide[source, channel]))
        keep_ref[channel] = total[:width]
        send_ref[channel * width : (channel + 1) * width] = total[width : 2 * width]
        for row in range(count):
            at = (2 + row) * width
            own_ref[channel, row] = total[at : at + width]
            target = (2 + channel * count + row) * width
            send_ref[target : target + width] = total[at + count * width : at + (count + 1) * width]


def volume_kernel(own_ref, received_ref, base_ref, volume_ref):
    count, width = own_ref.shape[1:3]
    for channel in range(2):
        for row in range(count):
            at = (2 + channel * count + row) * width
            descent = own_ref[channel, row] + received_ref[at : at + width]
            volume_ref[channel, row] = base_ref[channel, row] - step_size * descent


def finish_kernel(*refs):
    keep_ref, received_ref, object_ref, dual_ref = refs[:4]
    spreads, (dual_out_ref, projected_ref) = refs[4:-2], refs[-2:]
    width = keep_ref.shape[1]
    for channel in range(2):
        received = received_ref[channel * width : (channel + 1) * width]
        projection = -step_size * (keep_ref[channel] + received)
        for spread_ref in spreads:
            projection = projection + spread_ref[channel]
        projected_ref[0, channel] = projection
        dual_out_ref[0, channel] = dual_ref[0, channel] + object_ref[0, channel] - projection


def call(
    kernel, shapes, operands, scratch, flops, scalars=0, staged=(), numbers=(), copies=0, kind=jnp.float32, kinds={}
):
    held = sum(operand.nbytes for operand in operands[scalars:] + staged)
    held += 4 * sum(math.prod(shape) for shape in shapes)
    own = 4 * sum(math.prod(shape) for shape in scratch)
    outputs = [
        jax.ShapeDtypeStruct(shape, kinds.get(number, kind)) for number, shape in enumerate(shapes)
    ]
    scratch_shapes = [pltpu.VMEM(shape, jnp.float32) for shape in scratch]
    if staged and not copies:
        outputs += [jax.ShapeDtypeStruct(array.shape, array.dtype) for array in staged]
        copies = len(staged) + len(numbers)
        scratch_shapes += [pltpu.SMEM(array.shape, array.dtype) for array in numbers]
    staged += numbers
    if copies:
        scratch_shapes.append(pltpu.SemaphoreType.DMA((copies,)))
    in_specs = [SMEM] * scalars + [VMEM] * (len(operands) - scalars) + [HBM] * len(staged)
    return pl.pallas_call(
        kernel,
        out_shape=outputs,
        in_specs=in_specs,
        out_specs=[VMEM] * len(outputs),
        scratch_shapes=scratch_shapes,
        compiler_params=pltpu.CompilerParams(vmem_limit_bytes=held + own + SPARE_BYTES),
        cost_estimate=pl.CostEstimate(flops=flops, bytes_accessed=held, transcendentals=0),
    )(*operands, *(pltpu.with_memory_space_constraint(array, pltpu.HBM) for array in staged))


def body(
    transmission,
    scaled_dual,
    projected,
    volume,
    intensities,
    probe_wave,
    slot_first_rows,
    slot_first_columns,
    patch_counts,
    shift_table,
    tap_weight,
):
    width, length = transmission.shape[2:]
    count = volume.shape[1]
    scans, columns, tiles = (lax.axis_size(axis) for axis in ("scan", "angle", "tile"))
    assert scans % 2 == 0 and columns % 2 == 0 and tiles == 2 and lax.axis_size("groups") % 2 == 0
    rounds = []
    for first in (0, 1):
        pairs = [(i, i + 1) for i in range(first, scans - 1, 2)]
        route = [(s * tiles + t, d * tiles + t) for s, d in pairs for t in range(tiles)]
        route += [(target, source) for source, target in route]
        ends = {i for i in range(scans)} - {i for pair in pairs for i in pair}
        for scan in sorted(ends):
            route += [(scan * tiles + t, scan * tiles + 1 - t) for t in range(tiles)]
        rounds.append(route)
    swap = [(0, 1), (1, 0)]

    def exchange(block, number):
        return lax.ppermute(block, ("scan", "tile"), rounds[number])

    def across(block):
        return lax.ppermute(block, "tile", swap)

    edges = 2 * 2 * count
    (plane,) = call(
        pack_kernel,
        [(2 * width + -(-edges // SUBLANES) * SUBLANES, length)],
        (),
        [(edges, SUBLANES, length)],
        10**5,
        staged=(transmission, volume),
        copies=2 + edges,
    )
    plane_a = exchange(plane, 0)
    plane_b = exchange(plane, 1)
    tables = [jnp.asarray(table) for table in dft_tables(probe_wave.shape[1])]
    slots = slot_first_rows.shape[1]
    side = probe_wave.shape[1]
    probes, density, slot_numbers, rays, _, *held = call(
        prepare_kernel,
        [
            (slots, 2, side, side),
            (1, 3 * width, length),
            (slots, SUBLANES, side),
            (SUBLANES, length),
        ],
        (patch_counts,),
        [],
        10**7,
        1,
        (probe_wave, intensities, volume, *tables),
        (slot_first_rows, slot_first_columns, shift_table.T, tap_weight.T),
        kinds={2: jnp.int32},
    )
    volume_here = held[1]
    turns = [[(i, (i - turn) % columns) for i in range(columns)] for turn in range(columns)]
    rays_too = across(rays)
    own, rim_a, rim_b, row_a, row_b = call(
        patch_kernel,
        [(3, width, length)]
        + [(3 * width, length)] * 2
        + [(2, width + SUBLANES, length)] * 2,
        (probes, density, slot_numbers, plane, *held, plane_a, plane_b),
        [(2, 3 * width, length), (3, 3 * width, length)],
        10**9,
    )
    rim_a = exchange(rim_a, 0)
    rim_b = exchange(rim_b, 1)
    per_group, groups = columns * tiles, lax.axis_size("groups")
    bridge = []
    for group in range(groups):
        at = group * per_group
        pairs = [(at + i * tiles + 1, at + (i + 1) * tiles) for i in range(columns - 1)]
        bridge += pairs + [(target, source) for source, target in pairs]
        beyond = (groups - 1 - group) * per_group
        for outer in (0, per_group - 1):
            bridge.append((at + outer, beyond + outer))
    row_b = lax.ppermute(row_b, ("groups", "angle", "tile"), bridge)
    row_a = across(row_a)
    updated, residual, packed = call(
        fold_kernel,
        [
            transmission.shape,
            (2 * width, length),
            (2 * width + 2 * SUBLANES, length),
        ],
        (own, rim_a, rim_b, projected, scaled_dual, rays, rays_too),
        [],
        10**6,
    )
    by_column = [packed]
    for turn in range(1, columns):
        by_column.append(lax.ppermute(packed, "angle", turns[turn]))
    (base,) = call(
        variation_kernel,
        [volume.shape],
        (volume_here, plane_a, plane_b, row_a, row_b),
        [(count + 2, width + 16, length), (width + 16, length)],
        10**7,
    )
    route = []
    for scan in range(scans):
        for column in range(columns):
            lower = column < columns // 2
            target = scan + 1 if lower else scan - 1
            turned = column
            if not 0 <= target < scans:
                target, turned = scan, (column + columns // 2) % columns
            route.append((scan * columns + column, target * columns + turned))
    beside = lax.ppermute(base, ("scan", "angle"), route)
    here = jnp.stack([residual] + [block[: 2 * width] for block in by_column[1:]])
    side_a = exchange(here, 0)
    side_b = exchange(here, 1)
    high, low, new_transmission = call(
        operator_kernel,
        [(columns, (2 + 2 * count) * width, 3 * width)] * 2 + [transmission.shape],
        (*by_column, updated),
        [],
        10**8,
        kind=jnp.bfloat16,
        kinds={2: jnp.float32},
    )
    block = (columns, 2, width, length)
    keep, send = call(
        spread_kernel,
        [block, block],
        (shift_table.T, tap_weight.T, base, beside),
        [(count, 2, length // LANES, 2 * width, LANES)],
        10**7,
        2,
    )
    received = across(send)
    spreads = [keep[0], received[0]]
    for turn in range(1, columns):
        route = [(i, (i + turn) % columns) for i in range(columns)]
        spreads.append(lax.ppermute(keep[turn] + received[turn], "angle", route))
    keep, own, send = call(
        apply_kernel,
        [(2, width, length), volume.shape, ((2 + 2 * count) * width, length)],
        (here, side_a, side_b, high, low),
        [(columns, 2, 3 * width, length)],
        10**9,
    )
    received = across(send)
    (new_volume,) = call(volume_kernel, [volume.shape], (own, received, base), [], 10**6)
    new_dual, new_projected = call(
        finish_kernel,
        [transmission.shape] * 2,
        (keep, received, updated, scaled_dual, *spreads),
        [],
        10**6,
    )
    return (new_transmission, new_dual, new_volume, new_projected)


def solution(mesh):
    plane = P(("groups", "angle", "tile"), None, "scan", None)
    cells = P("groups", ("angle", "tile"), "scan", None)
    slots = P(("groups", "angle", "tile"), "scan")
    return jax.shard_map(
        body,
        mesh=mesh,
        in_specs=(
            plane,
            plane,
            plane,
            cells,
            P(("groups", "angle", "tile"), "scan", None, None),
            P("groups", None, None),
            slots,
            slots,
            slots,
            P(None, ("angle", "tile")),
            P(None, ("angle", "tile")),
        ),
        out_specs=(plane, plane, cells, plane),
        check_vma=False,
    )
```
